256 devices in a mesh: seq: 64 (over y, z, core), head: 4 (over x).
Axes of the slice: x: 4, y: 4, z: 8, core: 2. Of those that a mesh axis runs over, the one named last changes fastest.
Arguments:
- query_rows: bfloat16 [8192, 2048], P('seq', 'head'), may hold values from -6 to 6
- key_rows: bfloat16 [8192, 2048], P('seq', 'head'), may hold values from -0.52734375 to 0.52734375
- value_rows: bfloat16 [8192, 2048], P('seq', 'head'), may hold values from -6 to 6
- ridge_reg: float32 [16], P('head'), may hold values from 0.5 to 4
- out_weight: bfloat16 [2048, 2048], P('head'), may hold values from -0.125 to 0.125
- out_grad: bfloat16 [8192, 2048], P('seq', 'head'), may hold values from -8 to 8
- doc_ids: int32 [8192], P('seq'), may hold values from 0 to 7, never falling along the last dimension, each value on 1 to 4096 neighbouring positions
Outputs:
- layer_out: bfloat16 [8192, 2048], P('seq', 'head')
- grad_queries: bfloat16 [8192, 2048], P('seq', 'head')
- grad_keys: bfloat16 [8192, 2048], P('seq', 'head')
- grad_values: bfloat16 [8192, 2048], P('seq', 'head')
- grad_weight: float32 [2048, 2048], P('seq', 'head')
The draws below stay inside these ranges and needn't reach their ends.
Inputs may be any that keep to these rules, and one draw needn't show every extreme that they name: `doc_ids`: document numbers never fall along the tokens; every number occurs, each document has 1 to 4096 tokens and one has exactly 4096.
All inputs are finite; a program needn't handle non-finite values.
Results may differ from the reference program's by a relative error of at most 0.018.
Values may be sent and summed in bfloat16 or wider, within the bound.
A program may use at most 128 MiB of HBM per device.

```python
import math
import jax
import jax.numpy as jnp
import numpy as np
from jax import lax

D = 2048
HEADS = 16
DH = 128
PIECE = 128
CG_STEPS = 4
TOKENS = 8192
DOCS = 8
DOC_MOST = 4096


def strengthened(values, own_key, source, target, shards_of, factor):
    owner, partner = [(jnp.arange(values.shape[position]) // (values.shape[position] // shards_of)).reshape([-1 if axis == position else 1 for axis in range(values.ndim)]) for position in (source, target)]
    chosen = jax.random.permutation(own_key, shards_of)[partner]
    strong = (owner == chosen) | (owner == (partner + shards_of // 2) % shards_of)
    return jnp.where(strong, factor * values, values)


def block_levels(rng, dims, cuts, least, top_value):
    level, own = 1.0, jax.random.fold_in(rng, 6)
    for dim, parts in cuts:
        draws = jnp.exp(jax.random.uniform(jax.random.fold_in(own, dim), (parts,), jnp.float32, least / len(cuts), top_value / len(cuts)))
        level = level * jnp.repeat(draws, dims[dim] // parts).reshape([-1 if axis == dim else 1 for axis in range(len(dims))])
    return level


def profile(count, total, bound, skew):
    loads = [(1 << 20) // math.isqrt(standing ** skew) + 1 for standing in range(2, count + 1)]
    rest, holding = total - bound - (count - 1), [1] * (count - 1)
    while rest > 0:
        candidates = [i for i in range(count - 1) if holding[i] < bound]
        pool, remaining = sum([loads[i] for i in candidates]), rest
        for i in candidates:
            addition = min(bound - holding[i], max(1, remaining * loads[i] // pool), rest)
            holding[i] = holding[i] + addition
            rest = rest - addition
    return np.array([bound] + holding)


def uneven_parts(key, number_of, total, limit, slope):
    if number_of == 2:
        one = jax.random.randint(key, (), max(1, total - limit), min(limit, total - 1) + 1)
        return jnp.stack([one, total - one])
    lengths = jnp.asarray(profile(number_of, total, limit, slope), jnp.int32)
    couples = (number_of - 1) // 2
    giver, receiver = lengths[1:1 + 2 * couples:2], lengths[2:2 + 2 * couples:2]
    slack = jnp.minimum(giver - 1, limit - receiver)
    moved = jax.random.randint(jax.random.fold_in(key, 1), (couples,), 0, 1 << 20) % (slack + 1)
    lengths = lengths.at[1:1 + 2 * couples:2].set(giver - moved).at[2:2 + 2 * couples:2].set(receiver + moved)
    return lengths[jax.random.permutation(jax.random.fold_in(key, 2), number_of)]


def normal_values(own_key, dims, scale, bound, cuts=(), dtype=jnp.bfloat16):
    values = scale * jax.random.normal(own_key, dims, jnp.float32)
    if cuts:
        values = values * block_levels(own_key, dims, cuts, -0.22, 0.18)
    return jnp.clip(values, -bound, bound).astype(dtype)


def bell_draw_with(key, dims, deviation, reach, split, heavy, held_as=jnp.bfloat16):
    values = deviation * jax.random.normal(key, dims, jnp.float32)
    if split:
        values = values * block_levels(key, dims, split, -0.22, 0.18)
    return jnp.clip(strengthened(values, jax.random.fold_in(key, 3), *heavy), -reach, reach).astype(held_as)


def setup_inputs(seed: int = 0) -> dict:
    splits = jax.random.split(jax.random.key(seed), 8)
    query_rows = normal_values(splits[0], (TOKENS, HEADS * DH), 1.0, 6.0, ((0, 64), (1, 4)))
    key_rows = normal_values(splits[1], (TOKENS, HEADS * DH), (DH ** -0.5), 0.52734375, ((0, 64), (1, 4)))
    value_rows = normal_values(splits[2], (TOKENS, HEADS * DH), 1.0, 6.0, ((0, 64), (1, 4)))
    ridge_reg = jnp.clip(jnp.exp(math.log(4.0) - 2.0794415 * jax.random.uniform(splits[3], (HEADS,), jnp.float32) ** block_levels(splits[3], (HEADS,), ((0, 4),), -0.2, 0.2)), 0.5, 4.0)
    out_weight = normal_values(splits[4], (HEADS * DH, D), (HEADS * DH) ** -0.5, 0.125, ((0, 4),))
    out_grad = bell_draw_with(splits[5], (TOKENS, D), 1.0, 8.0, ((0, 64), (1, 4)), (0, 1, 64, 4.0))
    doc_ids = jnp.searchsorted(jnp.cumsum(uneven_parts(splits[6], DOCS, TOKENS, DOC_MOST, 2)), jnp.arange(TOKENS), side="right").astype(jnp.int32)
    return dict(query_rows=query_rows, key_rows=key_rows, value_rows=value_rows, ridge_reg=ridge_reg, out_weight=out_weight, out_grad=out_grad, doc_ids=doc_ids)


epsilon = 1e-6


def matmul_high(left_side, right_side):
    return jnp.dot(left_side, right_side, precision=lax.Precision.HIGHEST, preferred_element_type=jnp.float32)


def causal_mask(labels):
    length = labels.shape[0]
    row_idx = lax.broadcasted_iota(jnp.int32, (length, length), 0)
    col_idx = lax.broadcasted_iota(jnp.int32, (length, length), 1)
    return ((labels[:, None] == labels[None, :]) & (col_idx <= row_idx)).astype(jnp.float32)


def conj_solve(target, key_rows, same_doc, carried, gram_in, ridge_reg):
    def apply_matrix(direction):
        scores = matmul_high(direction, key_rows.T) * same_doc
        return carried[:, None] * matmul_high(direction, gram_in) + matmul_high(scores, key_rows) + ridge_reg * direction

    solution = jnp.zeros_like(target)
    residual = target
    direction = target
    res_sq = jnp.sum(residual * residual, axis=1, keepdims=True)
    for number in range(CG_STEPS):
        applied = apply_matrix(direction)
        step_size = res_sq / (jnp.sum(direction * applied, axis=1, keepdims=True) + epsilon)
        solution = solution + step_size * direction
        residual = residual - step_size * applied
        new_sq = jnp.sum(residual * residual, axis=1, keepdims=True)
        direction = residual + (new_sq / (res_sq + epsilon)) * direction
        res_sq = new_sq
    return solution


def head_forward(query_rows, key_rows, value_rows, same_doc, carried, gram_in, value_in, ridge_reg):
    solution = conj_solve(query_rows, key_rows, same_doc, carried, gram_in, ridge_reg)
    score_one = matmul_high(solution, key_rows.T) * same_doc
    output = carried[:, None] * matmul_high(solution, value_in.T) + matmul_high(score_one, value_rows)
    return solution, output


def head_dual(key_rows, value_rows, same_doc, carried, head_rows, gram_in, value_in, ridge_reg, solution, out_cot):
    score_two = matmul_high(out_cot, value_rows.T) * same_doc
    target = carried[:, None] * matmul_high(out_cot, value_in) + matmul_high(score_two, key_rows)
    dual_sol = conj_solve(target, key_rows, same_doc, carried, gram_in, ridge_reg)
    state_part = matmul_high(out_cot.T, head_rows[:, None] * solution)
    cross_sum = matmul_high(dual_sol.T, head_rows[:, None] * solution)
    return dual_sol, state_part, cross_sum + cross_sum.T, score_two


def head_grads(key_rows, value_rows, same_doc, later_rows, solution, out_cot, dual_sol, score_two, grad_state, gram_grad):
    score_one = matmul_high(solution, key_rows.T) * same_doc
    score_three = matmul_high(dual_sol, key_rows.T) * same_doc
    grad_v = later_rows[:, None] * matmul_high(key_rows, grad_state.T) + matmul_high(score_one.T, out_cot)
    grad_k = later_rows[:, None] * (matmul_high(value_rows, grad_state) - matmul_high(key_rows, gram_grad))
    grad_k = grad_k + matmul_high(score_two.T, solution) - matmul_high(score_one.T, dual_sol) - matmul_high(score_three.T, solution)
    return grad_k, grad_v


def split_heads(array):
    return array.astype(jnp.float32).reshape(-1, PIECE, HEADS, DH).transpose(0, 2, 1, 3)


def join_heads(array):
    return array.transpose(0, 2, 1, 3).reshape(-1, HEADS * DH)


def reference(query_rows, key_rows, value_rows, ridge_reg, out_weight, out_grad, doc_ids):
    query_h = split_heads(query_rows)
    key_h = split_heads(key_rows)
    value_h = split_heads(value_rows)
    label_rows = doc_ids.reshape(-1, PIECE)
    zero_state = jnp.zeros((HEADS, DH, DH), jnp.float32)
    start_state = (jnp.array(-1, jnp.int32), zero_state, zero_state)

    def forward_piece(carry, inputs):
        label_in, gram_in, value_in = carry
        query_p, key_p, value_p, labels = inputs
        same_doc = causal_mask(labels)
        carried = (labels == label_in).astype(jnp.float32)
        solution, output = jax.vmap(head_forward, in_axes=(0, 0, 0, None, None, 0, 0, 0))(
            query_p, key_p, value_p, same_doc, carried, gram_in, value_in, ridge_reg)
        tail_rows = (labels == labels[-1]).astype(jnp.float32)[None, :, None]
        gram_tail = jnp.einsum("hpk,hpl->hkl", key_p * tail_rows, key_p, precision=lax.Precision.HIGHEST, preferred_element_type=jnp.float32)
        value_tail = jnp.einsum("hpv,hpk->hvk", value_p * tail_rows, key_p, precision=lax.Precision.HIGHEST, preferred_element_type=jnp.float32)
        joined = ((labels[0] == labels[-1]) & (labels[-1] == label_in)).astype(jnp.float32)
        new_carry = (labels[-1], gram_tail + joined * gram_in, value_tail + joined * value_in)
        return new_carry, (solution, output, gram_in, value_in, label_in)

    final_state, saved = lax.scan(forward_piece, start_state, (query_h, key_h, value_h, label_rows))
    solution_all, output_all, gram_all, value_all, label_all = saved
    mixed = join_heads(output_all).astype(jnp.bfloat16)
    layer_out = jnp.dot(mixed, out_weight, preferred_element_type=jnp.float32).astype(jnp.bfloat16)
    grad_weight = jnp.dot(out_grad.T, mixed, preferred_element_type=jnp.float32)
    out_cot_all = split_heads(jnp.dot(out_grad, out_weight.T, preferred_element_type=jnp.float32))

    def backward_piece(carry, inputs):
        label_after, grad_state, gram_grad = carry
        key_p, value_p, labels, solution, out_cot, gram_in, value_in, label_in = inputs
        same_doc = causal_mask(labels)
        carried = (labels == label_in).astype(jnp.float32)
        head_rows = (labels == labels[0]).astype(jnp.float32)
        later_rows = (labels == label_after).astype(jnp.float32)
        dual_sol, state_part, gram_part, score_two = jax.vmap(head_dual, in_axes=(0, 0, None, None, None, 0, 0, 0, 0, 0))(
            key_p, value_p, same_doc, carried, head_rows, gram_in, value_in, ridge_reg, solution, out_cot)
        grad_k, grad_v = jax.vmap(head_grads, in_axes=(0, 0, None, None, 0, 0, 0, 0, 0, 0))(
            key_p, value_p, same_doc, later_rows, solution, out_cot, dual_sol, score_two, grad_state, gram_grad)
        joined = ((labels[0] == labels[-1]) & (labels[0] == label_after)).astype(jnp.float32)
        new_carry = (labels[0], state_part + joined * grad_state, gram_part + joined * gram_grad)
        return new_carry, (dual_sol, grad_k, grad_v)

    end_state, grads = lax.scan(backward_piece, start_state,
                                (key_h, value_h, label_rows, solution_all, out_cot_all, gram_all, value_all, label_all),
                                reverse=True)
    dual_all, grad_k_all, grad_v_all = grads
    grad_queries = join_heads(dual_all).astype(jnp.bfloat16)
    grad_keys = join_heads(grad_k_all).astype(jnp.bfloat16)
    grad_values = join_heads(grad_v_all).astype(jnp.bfloat16)
    return (layer_out, grad_queries, grad_keys, grad_values, grad_weight)
```

```python
import functools

import jax
import jax.numpy as jnp
from jax import lax
from jax.experimental import pallas as pl
from jax.experimental.pallas import tpu as pltpu
from jax.sharding import PartitionSpec as P

CG_STEPS = 4
EPS = 1e-6
DH = 128
F32 = jnp.float32
BF = jnp.bfloat16
MESH = pl.DeviceIdType.MESH

SEQ_DIMS = (4, 8, 2)


def nn(a, b):
    return lax.dot_general(a, b, (((1,), (0,)), ((), ())), preferred_element_type=F32)


def nt(a, b):
    return lax.dot_general(a, b, (((1,), (1,)), ((), ())), preferred_element_type=F32)


def tn(a, b):
    return lax.dot_general(a, b, (((0,), (0,)), ((), ())), preferred_element_type=F32)


def halves(a):
    high = a.astype(BF)
    return high, (a - high.astype(F32)).astype(BF)


def kernel(
    dims, nx,
    ridge, q_in, k_in, v_in, w_in, og_in, doc_in,
    lay_out, gq_out, gk_out, gv_out, gw_out,
    q, k, v, w, doc, lab_own, lab,
    t_send, t_recv, p_send, p_recv, b_send, b_recv, r_send, r_recv,
    cot, cot_y, cot_t, mix, l_send, l_recv, l_own,
    gw_own, gw_send, gw_recv, z_send, z_recv,
    lay, gq, gk, gv, gw,
    load_sem, out_sem,
    lab_s, lab_r, t_s, t_r, p_s, p_r, b_s, b_r, r_s, r_r,
    cot_s, cot_r, coty_s, coty_r, mix_s, mix_r, l_s, l_r, gw_s, gw_r, z_s, z_r,
):
    ny, nz, nc = dims
    n = ny * nz * nc
    heads = ridge.shape[0]
    width = heads * DH
    me, mh = lax.axis_index("seq"), lax.axis_index("head")
    c = lax.rem(me, nc)
    z = lax.rem(me // nc, nz)
    y = me // (nc * nz)
    rows = t_send.shape[1]
    per_head = 2 * DH // rows

    def remote(src, dst, ssem, rsem, seq, head):
        return pltpu.make_async_remote_copy(
            src_ref=src, dst_ref=dst, send_sem=ssem, recv_sem=rsem,
            device_id=(seq, head), device_id_type=MESH,
        )

    def settle(ref, sem):
        pltpu.make_async_copy(ref, ref, sem).wait()

    loads = [
        pltpu.make_async_copy(src, dst, load_sem.at[i])
        for i, (src, dst) in enumerate(
            ((doc_in, doc), (k_in, k), (v_in, v), (og_in, cot.at[mh]), (w_in, w), (q_in, q))
        )
    ]
    for load in loads:
        load.start()

    barrier = pltpu.get_barrier_semaphore()

    @pl.loop(1, n)
    def _(i):
        pl.semaphore_signal(barrier, inc=1, device_id=(lax.rem(me + i, n), mh), device_id_type=MESH)

    for i in range(1, nx):
        pl.semaphore_signal(barrier, inc=1, device_id=(me, lax.rem(mh + i, nx)), device_id_type=MESH)

    loads[0].wait()
    doc_row = jnp.broadcast_to(doc[...].astype(F32), (DH, DH))
    doc_col = doc_row.T
    last, first = doc_col[DH - 1 : DH, :], doc_col[0:1, :]
    lab_own[0:1, :] = last
    lab_own[1:2, :] = first
    lab[me] = lab_own[...]
    below = lax.broadcasted_iota(jnp.int32, (DH, DH), 1) <= lax.broadcasted_iota(jnp.int32, (DH, DH), 0)
    same_doc = jnp.where((doc_row == doc_col) & below, 1.0, 0.0).astype(F32)
    tail = jnp.where(doc_col == last, 1.0, 0.0).astype(BF)
    head_rows = jnp.where(doc_col == first, 1.0, 0.0).astype(F32)

    loads[1].wait()
    loads[2].wait()
    for h in range(heads):
        cols = slice(h * DH, (h + 1) * DH)
        kh, vh = k[:, cols], v[:, cols]
        state = tn(jnp.concatenate([kh * tail, vh * tail], axis=1), kh).astype(BF)
        t_send[h * per_head : (h + 1) * per_head] = state.reshape(per_head, rows, DH)
    t_recv[me] = t_send[me]

    loads[3].wait()
    pl.semaphore_wait(barrier, n - 1 + nx - 1)

    def exchange(src, dst, ssem, rsem):
        @pl.loop(1, n)
        def _(i):
            to = lax.rem(me + i, n)
            remote(src.at[to], dst.at[me], ssem, rsem, to, mh).start()

    @pl.loop(1, n)
    def _(i):
        to = lax.rem(me + i, n)
        remote(lab_own, lab.at[me], lab_s, lab_r, to, mh).start()

    exchange(t_send, t_recv, t_s, t_r)
    for i in range(1, nx):
        remote(cot.at[mh], cot.at[mh], cot_s, cot_r, me, lax.rem(mh + i, nx)).start()

    loads[4].wait()
    settle(cot.at[pl.ds(0, nx - 1)], cot_r)
    for i in range(1, ny):
        to = lax.rem(y + i, ny)
        remote(cot.at[to], cot_y.at[y], coty_s, coty_r, (to * nz + z) * nc + c, mh).start()
    cot_y[y] = cot[y]
    do = nt(cot[0], w[:, 0:width])
    for b in range(1, nx):
        do = do + nt(cot[b], w[:, b * width : (b + 1) * width])

    do_high, do_low, score_two, target_own = [], [], [], []
    for h in range(heads):
        cols = slice(h * DH, (h + 1) * DH)
        kh, vh = k[:, cols], v[:, cols]
        high, low = halves(do[:, cols])
        two = (nt(high, vh) + nt(low, vh)) * same_doc
        two_high, two_low = halves(two)
        do_high.append(high)
        do_low.append(low)
        score_two.append(two)
        target_own.append(nn(two_high, kh) + nn(two_low, kh))

    def scan(src, dst, row, reverse):
        def step(i, carry):
            total, before = carry
            at = n - 1 - i if reverse else i
            dst[at] = total.astype(BF)
            label = lab[at, pl.ds(row, 1)]
            total = jnp.where(label == before, total, 0.0) + src[at].astype(F32)
            return total, label

        lax.fori_loop(
            0, n, step,
            (jnp.zeros((rows, DH), F32), jnp.full((1, DH), -1.0, F32)),
            unroll=4,
        )

    settle(lab.at[pl.ds(0, n - 1)], lab_r)
    settle(t_recv.at[pl.ds(0, n - 1)], t_r)
    scan(t_recv, p_send, 0, False)
    exchange(p_send, p_recv, p_s, p_r)
    p_recv[me] = p_send[me]

    label_in = jnp.where(me > 0, lab[jnp.maximum(me - 1, 0), pl.ds(0, 1)], -1.0)
    label_next = jnp.where(me < n - 1, lab[jnp.minimum(me + 1, n - 1), pl.ds(1, 1)], -1.0)
    carried = jnp.where(doc_col == label_in, 1.0, 0.0).astype(F32)
    later = jnp.where(doc_col == label_next, 1.0, 0.0).astype(F32)
    carried_two = jnp.concatenate([carried, carried], axis=0).astype(BF)
    same_two = jnp.concatenate([same_doc, same_doc], axis=0)

    settle(cot_y.at[pl.ds(0, ny - 1)], coty_r)
    strip = gw.shape[0]
    for b in range(ny):
        turned = cot_y[b].T
        for zz in range(nz):
            for cc in range(nc):
                at = (zz * nc + cc) * strip
                cot_t[cc, zz * strip : (zz + 1) * strip, b * DH : (b + 1) * DH] = turned[at : at + strip, :]

    loads[5].wait()
    settle(p_recv.at[pl.ds(0, n - 1)], p_r)

    keys, gram, x, r, p, rr = [], [], [], [], [], []
    for h in range(heads):
        cols = slice(h * DH, (h + 1) * DH)
        kh = k[:, cols]
        state = p_recv[h * per_head : (h + 1) * per_head].reshape(2 * DH, DH)
        value_in = state[DH:]
        target = carried * (nn(do_high[h], value_in) + nn(do_low[h], value_in)) + target_own[h]
        b = jnp.concatenate([q[:, cols].astype(F32), target], axis=0)
        keys.append(jnp.concatenate([kh, state[:DH]], axis=0))
        x.append(jnp.zeros_like(b))
        r.append(b)
        p.append(b)
        rr.append(jnp.sum(b * b, axis=1, keepdims=True))
    for number in range(CG_STEPS):
        for h in range(heads):
            cols = slice(h * DH, (h + 1) * DH)
            kh = k[:, cols]
            p_high, p_low = halves(p[h])
            scores = (nt(p_high, kh) + nt(p_low, kh)) * same_two
            s_high, s_low = halves(scores)
            applied = (
                nn(jnp.concatenate([s_high, p_high * carried_two], axis=1), keys[h])
                + nn(jnp.concatenate([s_low, p_low * carried_two], axis=1), keys[h])
                + ridge[h] * p[h]
            )
            step = rr[h] / (jnp.sum(p[h] * applied, axis=1, keepdims=True) + EPS)
            x[h] = x[h] + step * p[h]
            if number < CG_STEPS - 1:
                r[h] = r[h] - step * applied
                fresh = jnp.sum(r[h] * r[h], axis=1, keepdims=True)
                p[h] = r[h] + fresh / (rr[h] + EPS) * p[h]
                rr[h] = fresh

    x_high, x_low, score_x = [], [], []
    for h in range(heads):
        high, low = halves(x[h])
        x_high.append(high)
        x_low.append(low)
        rows_x = (head_rows * x[h][:DH]).astype(BF)
        both = tn(jnp.concatenate([do_high[h], high[DH:]], axis=1), rows_x)
        cross = both[DH:]
        state = jnp.concatenate([both[:DH], cross + cross.T], axis=0).astype(BF)
        b_send[h * per_head : (h + 1) * per_head] = state.reshape(per_head, rows, DH)
    exchange(b_send, b_recv, b_s, b_r)
    b_recv[me] = b_send[me]
    for h in range(heads):
        cols = slice(h * DH, (h + 1) * DH)
        kh, vh = k[:, cols], v[:, cols]
        value_in = p_recv[h * per_head : (h + 1) * per_head].reshape(2 * DH, DH)[DH:]
        scores = (nt(x_high[h], kh) + nt(x_low[h], kh)) * same_two
        score_x.append(scores)
        s_high, s_low = halves(scores[:DH])
        out = nn(s_high, vh) + nn(s_low, vh) + carried * (nt(x_high[h][:DH], value_in) + nt(x_low[h][:DH], value_in))
        mix[y, :, cols] = out.astype(BF)
        gq[:, cols] = x[h][DH:].astype(BF)
    pltpu.make_async_copy(gq, gq_out, out_sem.at[0]).start()
    for i in range(1, ny):
        to = lax.rem(y + i, ny)
        remote(mix.at[y], mix.at[y], mix_s, mix_r, (to * nz + z) * nc + c, mh).start()

    mixed = mix[y]
    for i in range(1, nx):
        to = lax.rem(mh + i, nx)
        part = nn(mixed, w[:, pl.ds(pl.multiple_of(to * width, width), width)])
        l_send[i] = part.astype(BF)
        remote(l_send.at[i], l_recv.at[mh], l_s, l_r, me, to).start()
    l_own[...] = nn(mixed, w[:, pl.ds(pl.multiple_of(mh * width, width), width)])
    l_recv[mh] = jnp.zeros((DH, width), BF)

    for h in range(heads):
        cols = slice(h * DH, (h + 1) * DH)
        one = score_x[h][:DH].astype(BF)
        rest = (score_two[h] - score_x[h][DH:]).astype(BF)
        gv[:, cols] = tn(one, do_high[h])
        gk[:, cols] = tn(rest, x_high[h][:DH]) - tn(one, x_high[h][DH:])

    settle(b_recv.at[pl.ds(0, n - 1)], b_r)
    scan(b_recv, r_send, 1, True)
    exchange(r_send, r_recv, r_s, r_r)
    r_recv[me] = r_send[me]

    settle(mix.at[pl.ds(0, ny - 1)], mix_r)
    gathered = mix[...].reshape(ny * DH, width)
    other = nc - 1 - c
    gw_send[...] = nn(cot_t[other], gathered).astype(BF).reshape(nz, strip, width)
    remote(gw_send, gw_recv, gw_s, gw_r, (y * nz + z) * nc + other, mh).start()
    gw_own[...] = nn(cot_t[c], gathered).reshape(nz, strip, width)
    settle(gw_recv, gw_r)
    z_send[...] = (gw_own[...] + gw_recv[...].astype(F32)).astype(BF)
    for i in range(1, nz):
        to = lax.rem(z + i, nz)
        remote(z_send.at[to], z_recv.at[z], z_s, z_r, (y * nz + to) * nc + c, mh).start()
    z_recv[z] = z_send[z]

    settle(l_recv.at[pl.ds(0, nx - 1)], l_r)
    total = l_own[...]
    for b in range(nx):
        total = total + l_recv[b].astype(F32)
    lay[...] = total.astype(BF)
    pltpu.make_async_copy(lay, lay_out, out_sem.at[1]).start()

    settle(r_recv.at[pl.ds(0, n - 1)], r_r)
    outs = [pltpu.make_async_copy(gq, gq_out, out_sem.at[0]), pltpu.make_async_copy(lay, lay_out, out_sem.at[1])]
    for h in range(heads):
        cols = slice(h * DH, (h + 1) * DH)
        kh, vh = k[:, cols], v[:, cols]
        state = r_recv[h * per_head : (h + 1) * per_head].reshape(2 * DH, DH)
        grad_state, gram_grad = state[:DH], state[DH:]
        q[:, cols] = (gv[:, cols] + later * nt(kh, grad_state)).astype(BF)
        k[:, cols] = (gk[:, cols] + later * (nn(vh, grad_state) - nn(kh, gram_grad))).astype(BF)
    outs += [pltpu.make_async_copy(q, gv_out, out_sem.at[2]), pltpu.make_async_copy(k, gk_out, out_sem.at[3])]
    outs[2].start()
    outs[3].start()

    settle(z_recv.at[pl.ds(0, nz - 1)], z_r)
    total = z_recv[0].astype(F32)
    for b in range(1, nz):
        total = total + z_recv[b].astype(F32)
    gw[...] = total
    outs.append(pltpu.make_async_copy(gw, gw_out, out_sem.at[4]))
    outs[4].start()

    settle(lab.at[pl.ds(0, n - 1)], lab_s)
    for src, sem in ((t_send, t_s), (p_send, p_s), (b_send, b_s), (r_send, r_s)):
        settle(src.at[pl.ds(0, n - 1)], sem)
    settle(cot.at[pl.ds(0, nx - 1)], cot_s)
    settle(cot_y.at[pl.ds(0, ny - 1)], coty_s)
    settle(mix.at[pl.ds(0, ny - 1)], mix_s)
    settle(l_send.at[pl.ds(1, nx - 1)], l_s)
    settle(gw_send, gw_s)
    settle(z_send.at[pl.ds(0, nz - 1)], z_s)
    for out in outs:
        out.wait()


def per_device(dims, nx, query_rows, key_rows, value_rows, ridge_reg, out_weight, out_grad, doc_ids):
    ny, nz, nc = dims
    n = ny * nz * nc
    heads = ridge_reg.shape[0]
    width = heads * DH
    rows = heads * 2 * DH // n
    strip = width // (nz * nc)
    states = [pltpu.VMEM((n, rows, DH), BF)] * 8
    dma = pltpu.SemaphoreType.DMA
    any_space = pl.BlockSpec(memory_space=pl.ANY)
    piece = jax.ShapeDtypeStruct((DH, width), BF)
    return pl.pallas_call(
        functools.partial(kernel, dims, nx),
        out_shape=(piece, piece, piece, piece, jax.ShapeDtypeStruct((strip, width), F32)),
        in_specs=[pl.BlockSpec(memory_space=pltpu.SMEM)] + [any_space] * 6,
        out_specs=(any_space,) * 5,
        scratch_shapes=[
            pltpu.VMEM((DH, width), BF),
            pltpu.VMEM((DH, width), BF),
            pltpu.VMEM((DH, width), BF),
            pltpu.VMEM((width, nx * width), BF),
            pltpu.VMEM((1, DH), jnp.int32),
            pltpu.VMEM((2, DH), F32),
            pltpu.VMEM((n, 2, DH), F32),
            *states,
            pltpu.VMEM((nx, DH, width), BF),
            pltpu.VMEM((ny, DH, width), BF),
            pltpu.VMEM((nc, nz * strip, ny * DH), BF),
            pltpu.VMEM((ny, DH, width), BF),
            pltpu.VMEM((nx, DH, width), BF),
            pltpu.VMEM((nx, DH, width), BF),
            pltpu.VMEM((DH, width), F32),
            pltpu.VMEM((nz, strip, width), F32),
            pltpu.VMEM((nz, strip, width), BF),
            pltpu.VMEM((nz, strip, width), BF),
            pltpu.VMEM((nz, strip, width), BF),
            pltpu.VMEM((nz, strip, width), BF),
            pltpu.VMEM((DH, width), BF),
            pltpu.VMEM((DH, width), BF),
            pltpu.VMEM((DH, width), F32),
            pltpu.VMEM((DH, width), F32),
            pltpu.VMEM((strip, width), F32),
            dma((6,)),
            dma((5,)),
        ]
        + [dma] * 22,
        compiler_params=pltpu.CompilerParams(collective_id=0, has_side_effects=True),
    )(ridge_reg, query_rows, key_rows, value_rows, out_weight, out_grad, doc_ids.reshape(1, -1))


def build(mesh, dims):
    nx = mesh.shape["head"]
    spec = P("seq", "head")
    return jax.shard_map(
        functools.partial(per_device, dims, nx),
        mesh=mesh,
        in_specs=(spec, spec, spec, P("head"), P("head", None), spec, P("seq")),
        out_specs=(spec,) * 5,
        check_vma=False,
    )


def solution(mesh):
    return build(mesh, SEQ_DIMS)
```

```python
import functools

import jax
import jax.numpy as jnp
from jax import lax
from jax.experimental import pallas as pl
from jax.experimental.pallas import tpu as pltpu
from jax.sharding import PartitionSpec as P

CG_STEPS = 4
EPS = 1e-6
DH = 128
F32 = jnp.float32
BF = jnp.bfloat16
MESH = pl.DeviceIdType.MESH

SEQ_DIMS = (4, 8, 2)


def nn(a, b):
    return lax.dot_general(a, b, (((1,), (0,)), ((), ())), preferred_element_type=F32)


def nt(a, b):
    return lax.dot_general(a, b, (((1,), (1,)), ((), ())), preferred_element_type=F32)


def tn(a, b):
    return lax.dot_general(a, b, (((0,), (0,)), ((), ())), preferred_element_type=F32)


def halves(a):
    high = a.astype(BF)
    return high, (a - high.astype(F32)).astype(BF)


def kernel(
    dims, nx,
    ridge, q_in, k_in, v_in, w_in, og_in, doc_in,
    lay_out, gq_out, gk_out, gv_out, gw_out,
    q, k, v, w, doc, lab_own, lab_mate, lab_chip, lab, edge_own, edge,
    t_own, t_mate, t_send, t_recv, t_line, t_lines, p_send, p_recv, p_mate, p_all,
    b_own, b_mate, b_send, b_recv, b_line, b_lines, r_send, r_recv, r_mate, r_all,
    cot, cot_y, cot_t, mix, l_send, l_recv, l_own,
    gw_own, gw_send, gw_recv, z_send, z_recv,
    lay, gq, gk, gv, gw,
    load_sem, out_sem, send_sem, recv_sem,
):
    ny, nz, nc = dims
    heads = ridge.shape[0]
    width = heads * DH
    me, mh = lax.axis_index("seq"), lax.axis_index("head")
    c = lax.rem(me, nc)
    z = lax.rem(me // nc, nz)
    y = me // (nc * nz)
    other = nc - 1 - c
    rows = t_line.shape[0]
    strip = gw.shape[0]

    def at(yy, zz, cc):
        return (yy * nz + zz) * nc + cc

    mate = at(y, z, other)
    y_peers = [lax.rem(y + i, ny) for i in range(1, ny)]
    z_peers = [lax.rem(z + i, nz) for i in sorted(range(1, nz), key=lambda i: -min(i, nz - i))]
    x_peers = [lax.rem(mh + i, nx) for i in range(1, nx)]

    names = ("lab_mate", "lab", "edge", "t_mate", "t", "t_line", "p", "p_mate", "b_mate", "b", "b_line",
             "r", "r_mate", "cot", "cot_y", "mix", "l", "gw", "z")
    sems = {name: i for i, name in enumerate(names)}
    sent = []

    def send(name, src, dst, seq, head=None):
        copy = pltpu.make_async_remote_copy(
            src_ref=src, dst_ref=dst,
            send_sem=send_sem.at[sems[name]], recv_sem=recv_sem.at[sems[name]],
            device_id=(seq, mh if head is None else head), device_id_type=MESH,
        )
        copy.start()

    def settle(name, ref):
        sent.append((name, ref))
        pltpu.make_async_copy(ref, ref, recv_sem.at[sems[name]]).wait()

    loads = [
        pltpu.make_async_copy(src, dst, load_sem.at[i])
        for i, (src, dst) in enumerate(
            ((doc_in, doc), (k_in, k), (v_in, v), (og_in, cot.at[mh]), (w_in, w), (q_in, q))
        )
    ]
    for load in loads:
        load.start()

    barrier = pltpu.get_barrier_semaphore()
    peers = [(at(y, zz, c), mh) for zz in z_peers] + [(at(yy, z, c), mh) for yy in y_peers]
    peers += [(me, hh) for hh in x_peers] + [(mate, mh)]
    for peer in peers:
        pl.semaphore_signal(barrier, inc=1, device_id=peer, device_id_type=MESH)

    loads[0].wait()
    doc_row = jnp.broadcast_to(doc[...].astype(F32), (DH, DH))
    doc_col = doc_row.T
    last, first = doc_col[DH - 1 : DH, :], doc_col[0:1, :]
    lab_own[0:1, :] = last
    lab_own[1:2, :] = first
    below = lax.broadcasted_iota(jnp.int32, (DH, DH), 1) <= lax.broadcasted_iota(jnp.int32, (DH, DH), 0)
    same_doc = jnp.where((doc_row == doc_col) & below, 1.0, 0.0).astype(F32)
    tail = jnp.where(doc_col == last, 1.0, 0.0).astype(BF)
    head_rows = jnp.where(doc_col == first, 1.0, 0.0).astype(F32)

    in_half = heads // nc
    per_head = 2 * DH // rows

    def put_state(ref, h, state):
        first_slice = (h % in_half) * per_head
        ref[h // in_half, first_slice : first_slice + per_head] = state.astype(BF).reshape(per_head, rows, DH)

    def get_state(ref, h):
        first_slice = (h % in_half) * per_head
        return ref[h // in_half, first_slice : first_slice + per_head].reshape(2 * DH, DH)

    loads[1].wait()
    loads[2].wait()
    for h in range(heads):
        cols = slice(h * DH, (h + 1) * DH)
        kh, vh = k[:, cols], v[:, cols]
        put_state(t_own, h, tn(jnp.concatenate([kh * tail, vh * tail], axis=1), kh))

    loads[3].wait()
    pl.semaphore_wait(barrier, len(peers))

    def combine(own, from_mate, chip, row, leads):
        joined = jnp.where(lab_own[row : row + 1, :] == lab_mate[row : row + 1, :], 1.0, 0.0)
        own_part = jnp.where(leads, joined, 1.0)
        mate_part = jnp.where(leads, 1.0, joined)
        for i in range(nz):
            chip[i] = (own[c, i].astype(F32) * own_part + from_mate[i].astype(F32) * mate_part).astype(BF)

    def line_total(parts, line, row, reverse):
        total, before = jnp.zeros((rows, DH), F32), None
        for i in reversed(range(nz)) if reverse else range(nz):
            label = lab[i, row : row + 1, :]
            if before is not None:
                total = jnp.where(label == before, total, 0.0)
            total = total + parts[i].astype(F32)
            before = label
        line[...] = total.astype(BF)

    def incoming(lines, row, reverse):
        total, before = jnp.zeros((rows, DH), F32), jnp.full((1, DH), -1.0, F32)
        for i in reversed(range(ny)) if reverse else range(ny):
            label = edge[i, row : row + 1, :]
            grown = jnp.where(label == before, total, 0.0) + lines[i].astype(F32)
            reached = i > y if reverse else i < y
            total = jnp.where(reached, grown, total)
            before = jnp.where(reached, label, before)
        return total, before

    def scan(parts, total, before, out, row, reverse):
        chip_before = before
        for i in reversed(range(nz)) if reverse else range(nz):
            label = lab[i, row : row + 1, :]
            out[i] = total.astype(BF)
            chip_before = jnp.where(i == z, before, chip_before)
            total = jnp.where(label == before, total, 0.0) + parts[i].astype(F32)
            before = label
        return chip_before

    def spread(own, from_mate, chip, to_mate, whole, row, chip_before, leads):
        lead_label = jnp.where(leads, lab_own[row : row + 1, :], lab_mate[row : row + 1, :])
        joined = jnp.where(lead_label == chip_before, 1.0, 0.0)
        for i in range(nz):
            ahead = chip[i].astype(F32)
            lead_state = jnp.where(leads, own[c, i].astype(F32), from_mate[i].astype(F32))
            trail = lead_state + joined * ahead
            whole[c, i] = jnp.where(leads, ahead, trail).astype(BF)
            to_mate[i] = jnp.where(leads, trail, ahead).astype(BF)
        return jnp.where(leads, chip_before, lead_label)

    leads, leads_back = c == 0, c == nc - 1

    send("lab_mate", lab_own, lab_mate, mate)
    send("t_mate", t_own.at[other], t_mate, mate)
    for hh in x_peers:
        send("cot", cot.at[mh], cot.at[mh], me, hh)

    settle("lab_mate", lab_mate)
    lab_chip[0:1, :] = jnp.where(leads, lab_mate[0:1, :], lab_own[0:1, :])
    lab_chip[1:2, :] = jnp.where(leads, lab_own[1:2, :], lab_mate[1:2, :])
    lab[z] = lab_chip[...]
    for zz in z_peers:
        send("lab", lab_chip, lab.at[z], at(y, zz, c))
    settle("t_mate", t_mate)
    combine(t_own, t_mate, t_send, 0, leads)
    for zz in z_peers:
        send("t", t_send.at[zz], t_recv.at[z], at(y, zz, c))
    t_recv[z] = t_send[z]

    settle("lab", lab.at[pl.ds(0, nz - 1)])
    edge_own[0:1, :] = lab[nz - 1, 0:1, :]
    edge_own[1:2, :] = lab[0, 1:2, :]
    edge[y] = edge_own[...]
    for yy in y_peers:
        send("edge", edge_own, edge.at[y], at(yy, z, c))
    settle("t", t_recv.at[pl.ds(0, nz - 1)])
    line_total(t_recv, t_line, 0, False)
    for yy in y_peers:
        send("t_line", t_line, t_lines.at[y], at(yy, z, c))
    t_lines[y] = t_line[...]
    settle("edge", edge.at[pl.ds(0, ny - 1)])
    settle("t_line", t_lines.at[pl.ds(0, ny - 1)])
    total, before = incoming(t_lines, 0, False)
    chip_before = scan(t_recv, total, before, p_send, 0, False)
    for zz in z_peers:
        send("p", p_send.at[zz], p_recv.at[z], at(y, zz, c))
    p_recv[z] = p_send[z]

    loads[4].wait()
    settle("cot", cot.at[pl.ds(0, nx - 1)])
    for yy in y_peers:
        send("cot_y", cot.at[yy], cot_y.at[y], at(yy, z, c))
    cot_y[y] = cot[y]
    do = nt(cot[0], w[:, 0:width])
    for b in range(1, nx):
        do = do + nt(cot[b], w[:, b * width : (b + 1) * width])

    do_high, do_low, score_two, target_own = [], [], [], []
    for h in range(heads):
        cols = slice(h * DH, (h + 1) * DH)
        kh, vh = k[:, cols], v[:, cols]
        high, low = halves(do[:, cols])
        two = (nt(high, vh) + nt(low, vh)) * same_doc
        two_high, two_low = halves(two)
        do_high.append(high)
        do_low.append(low)
        score_two.append(two)
        target_own.append(nn(two_high, kh) + nn(two_low, kh))
    loads[5].wait()

    settle("p", p_recv.at[pl.ds(0, nz - 1)])
    label_in = spread(t_own, t_mate, p_recv, p_mate, p_all, 0, chip_before, leads)
    send("p_mate", p_mate, p_all.at[c], mate)
    carried = jnp.where(doc_col == label_in, 1.0, 0.0).astype(F32)
    carried_two = jnp.concatenate([carried, carried], axis=0).astype(BF)
    same_two = jnp.concatenate([same_doc, same_doc], axis=0)
    settle("p_mate", p_mate)

    keys, x, r, p, rr = [], [], [], [], []
    for h in range(heads):
        cols = slice(h * DH, (h + 1) * DH)
        kh = k[:, cols]
        state = get_state(p_all, h)
        value_in = state[DH:]
        target = carried * (nn(do_high[h], value_in) + nn(do_low[h], value_in)) + target_own[h]
        b = jnp.concatenate([q[:, cols].astype(F32), target], axis=0)
        keys.append(jnp.concatenate([kh, state[:DH]], axis=0))
        x.append(jnp.zeros_like(b))
        r.append(b)
        p.append(b)
        rr.append(jnp.sum(b * b, axis=1, keepdims=True))
    for number in range(CG_STEPS):
        for h in range(heads):
            cols = slice(h * DH, (h + 1) * DH)
            kh = k[:, cols]
            p_high, p_low = halves(p[h])
            scores = (nt(p_high, kh) + nt(p_low, kh)) * same_two
            s_high, s_low = halves(scores)
            applied = (
                nn(jnp.concatenate([s_high, p_high * carried_two], axis=1), keys[h])
                + nn(jnp.concatenate([s_low, p_low * carried_two], axis=1), keys[h])
                + ridge[h] * p[h]
            )
            step = rr[h] / (jnp.sum(p[h] * applied, axis=1, keepdims=True) + EPS)
            x[h] = x[h] + step * p[h]
            if number < CG_STEPS - 1:
                r[h] = r[h] - step * applied
                fresh = jnp.sum(r[h] * r[h], axis=1, keepdims=True)
                p[h] = r[h] + fresh / (rr[h] + EPS) * p[h]
                rr[h] = fresh

    x_high, x_low, score_x = [], [], []
    for h in range(heads):
        high, low = halves(x[h])
        x_high.append(high)
        x_low.append(low)
        rows_x = (head_rows * x[h][:DH]).astype(BF)
        both = tn(jnp.concatenate([do_high[h], high[DH:]], axis=1), rows_x)
        cross = both[DH:]
        put_state(b_own, h, jnp.concatenate([both[:DH], cross + cross.T], axis=0))
    send("b_mate", b_own.at[other], b_mate, mate)

    for h in range(heads):
        cols = slice(h * DH, (h + 1) * DH)
        kh, vh = k[:, cols], v[:, cols]
        value_in = get_state(p_all, h)[DH:]
        scores = (nt(x_high[h], kh) + nt(x_low[h], kh)) * same_two
        score_x.append(scores)
        s_high, s_low = halves(scores[:DH])
        out = nn(s_high, vh) + nn(s_low, vh) + carried * (nt(x_high[h][:DH], value_in) + nt(x_low[h][:DH], value_in))
        mix[y, :, cols] = out.astype(BF)
    for yy in y_peers:
        send("mix", mix.at[y], mix.at[y], at(yy, z, c))

    settle("b_mate", b_mate)
    combine(b_own, b_mate, b_send, 1, leads_back)
    for zz in z_peers:
        send("b", b_send.at[zz], b_recv.at[z], at(y, zz, c))
    b_recv[z] = b_send[z]

    for h in range(heads):
        gq[:, h * DH : (h + 1) * DH] = x[h][DH:].astype(BF)
    outs = [pltpu.make_async_copy(gq, gq_out, out_sem.at[0])]
    outs[0].start()
    mixed = mix[y]
    for i, hh in enumerate(x_peers):
        part = nn(mixed, w[:, pl.ds(pl.multiple_of(hh * width, width), width)])
        l_send[i] = part.astype(BF)
        send("l", l_send.at[i], l_recv.at[mh], me, hh)
    l_own[...] = nn(mixed, w[:, pl.ds(pl.multiple_of(mh * width, width), width)])
    l_recv[mh] = jnp.zeros((DH, width), BF)

    for h in range(heads):
        cols = slice(h * DH, (h + 1) * DH)
        one = score_x[h][:DH].astype(BF)
        rest = (score_two[h] - score_x[h][DH:]).astype(BF)
        gv[:, cols] = tn(one, do_high[h])
        gk[:, cols] = tn(rest, x_high[h][:DH]) - tn(one, x_high[h][DH:])

    settle("b", b_recv.at[pl.ds(0, nz - 1)])
    line_total(b_recv, b_line, 1, True)
    for yy in y_peers:
        send("b_line", b_line, b_lines.at[y], at(yy, z, c))
    b_lines[y] = b_line[...]

    settle("cot_y", cot_y.at[pl.ds(0, ny - 1)])
    for b in range(ny):
        turned = cot_y[b].T
        for zz in range(nz):
            for cc in range(nc):
                cut = (zz * nc + cc) * strip
                cot_t[cc, zz * strip : (zz + 1) * strip, b * DH : (b + 1) * DH] = turned[cut : cut + strip, :]

    settle("b_line", b_lines.at[pl.ds(0, ny - 1)])
    total, before = incoming(b_lines, 1, True)
    chip_before = scan(b_recv, total, before, r_send, 1, True)
    for zz in z_peers:
        send("r", r_send.at[zz], r_recv.at[z], at(y, zz, c))
    r_recv[z] = r_send[z]

    settle("mix", mix.at[pl.ds(0, ny - 1)])
    gathered = mix[...].reshape(ny * DH, width)
    gw_send[...] = nn(cot_t[other], gathered).astype(BF).reshape(nz, strip, width)
    send("gw", gw_send, gw_recv, mate)
    gw_own[...] = nn(cot_t[c], gathered).reshape(nz, strip, width)
    settle("gw", gw_recv)
    z_send[...] = (gw_own[...] + gw_recv[...].astype(F32)).astype(BF)
    for zz in z_peers:
        send("z", z_send.at[zz], z_recv.at[z], at(y, zz, c))
    z_recv[z] = z_send[z]

    settle("l", l_recv.at[pl.ds(0, nx - 1)])
    total = l_own[...]
    for b in range(nx):
        total = total + l_recv[b].astype(F32)
    lay[...] = total.astype(BF)
    outs.append(pltpu.make_async_copy(lay, lay_out, out_sem.at[1]))
    outs[1].start()

    settle("r", r_recv.at[pl.ds(0, nz - 1)])
    label_next = spread(b_own, b_mate, r_recv, r_mate, r_all, 1, chip_before, leads_back)
    send("r_mate", r_mate, r_all.at[c], mate)
    later = jnp.where(doc_col == label_next, 1.0, 0.0).astype(F32)
    settle("r_mate", r_mate)
    for h in range(heads):
        cols = slice(h * DH, (h + 1) * DH)
        kh, vh = k[:, cols], v[:, cols]
        state = get_state(r_all, h)
        grad_state, gram_grad = state[:DH], state[DH:]
        q[:, cols] = (gv[:, cols] + later * nt(kh, grad_state)).astype(BF)
        k[:, cols] = (gk[:, cols] + later * (nn(vh, grad_state) - nn(kh, gram_grad))).astype(BF)
    outs += [pltpu.make_async_copy(q, gv_out, out_sem.at[2]), pltpu.make_async_copy(k, gk_out, out_sem.at[3])]
    outs[2].start()
    outs[3].start()

    settle("z", z_recv.at[pl.ds(0, nz - 1)])
    total = z_recv[0].astype(F32)
    for b in range(1, nz):
        total = total + z_recv[b].astype(F32)
    gw[...] = total
    outs.append(pltpu.make_async_copy(gw, gw_out, out_sem.at[4]))
    outs[4].start()

    for name, ref in sent:
        pltpu.make_async_copy(ref, ref, send_sem.at[sems[name]]).wait()
    for out in outs:
        out.wait()


def move(*refs):
    count = (len(refs) - 1) // 3
    ins, outs, held, sem = refs[:count], refs[count : 2 * count], refs[2 * count : 3 * count], refs[-1]
    reads = [pltpu.make_async_copy(a, b, sem.at[0, i]) for i, (a, b) in enumerate(zip(ins, held))]
    writes = [pltpu.make_async_copy(a, b, sem.at[1, i]) for i, (a, b) in enumerate(zip(held, outs))]
    for read in reads:
        read.start()
    for read, write in zip(reads, writes):
        read.wait()
        write.start()
    for write in writes:
        write.wait()


def per_device(dims, nx, query_rows, key_rows, value_rows, ridge_reg, out_weight, out_grad, doc_ids):
    ny, nz, nc = dims
    heads = ridge_reg.shape[0]
    width = heads * DH
    rows = heads * 2 * DH // (nc * nz)
    strip = width // (nz * nc)
    any_space = pl.BlockSpec(memory_space=pl.ANY)
    piece = jax.ShapeDtypeStruct((DH, width), BF)
    half = pltpu.VMEM((nz, rows, DH), BF)
    both = pltpu.VMEM((nc, nz, rows, DH), BF)
    line = pltpu.VMEM((rows, DH), BF)
    lines = pltpu.VMEM((ny, rows, DH), BF)
    label = pltpu.VMEM((2, DH), F32)
    wide = pltpu.VMEM((DH, width), BF)
    results = (piece, piece, piece, piece, jax.ShapeDtypeStruct((strip, width), F32))
    states = [both, half, half, half, line, lines, half, half, half, both]
    made = pl.pallas_call(
        functools.partial(kernel, dims, nx),
        out_shape=results,
        in_specs=[pl.BlockSpec(memory_space=pltpu.SMEM)] + [any_space] * 6,
        out_specs=(any_space,) * 5,
        scratch_shapes=[
            wide,
            wide,
            wide,
            pltpu.VMEM((width, nx * width), BF),
            pltpu.VMEM((1, DH), jnp.int32),
            label,
            label,
            label,
            pltpu.VMEM((nz, 2, DH), F32),
            label,
            pltpu.VMEM((ny, 2, DH), F32),
            *states,
            *states,
            pltpu.VMEM((nx, DH, width), BF),
            pltpu.VMEM((ny, DH, width), BF),
            pltpu.VMEM((nc, nz * strip, ny * DH), BF),
            pltpu.VMEM((ny, DH, width), BF),
            pltpu.VMEM((nx, DH, width), BF),
            pltpu.VMEM((nx, DH, width), BF),
            pltpu.VMEM((DH, width), F32),
            pltpu.VMEM((nz, strip, width), F32),
            pltpu.VMEM((nz, strip, width), BF),
            pltpu.VMEM((nz, strip, width), BF),
            pltpu.VMEM((nz, strip, width), BF),
            pltpu.VMEM((nz, strip, width), BF),
            wide,
            wide,
            pltpu.VMEM((DH, width), F32),
            pltpu.VMEM((DH, width), F32),
            pltpu.VMEM((strip, width), F32),
            pltpu.SemaphoreType.DMA((6,)),
            pltpu.SemaphoreType.DMA((5,)),
            pltpu.SemaphoreType.DMA((19,)),
            pltpu.SemaphoreType.DMA((19,)),
        ],
        compiler_params=pltpu.CompilerParams(collective_id=0, has_side_effects=True),
    )(ridge_reg, query_rows, key_rows, value_rows, out_weight, out_grad, doc_ids.reshape(1, -1))
    return pl.pallas_call(
        move,
        out_shape=results,
        in_specs=[any_space] * 5,
        out_specs=(any_space,) * 5,
        scratch_shapes=[wide] * 4 + [pltpu.VMEM((strip, width), F32), pltpu.SemaphoreType.DMA((2, 5))],
    )(*made)


def build(mesh, dims):
    nx = mesh.shape["head"]
    spec = P("seq", "head")
    return jax.shard_map(
        functools.partial(per_device, dims, nx),
        mesh=mesh,
        in_specs=(spec, spec, spec, P("head"), P("head", None), spec, P("seq")),
        out_specs=(spec,) * 5,
        check_vma=False,
    )


def solution(mesh):
    return build(mesh, SEQ_DIMS)
```

```python
import functools

import jax
import jax.numpy as jnp
from jax import lax
from jax.experimental import pallas as pl
from jax.experimental.pallas import tpu as pltpu
from jax.sharding import PartitionSpec as P

CG_STEPS = 4
EPS = 1e-6
DH = 128
F32 = jnp.float32
BF = jnp.bfloat16
MESH = pl.DeviceIdType.MESH

SEQ_DIMS = (4, 8, 2)


def nn(a, b):
    return lax.dot_general(a, b, (((1,), (0,)), ((), ())), preferred_element_type=F32)


def nt(a, b):
    return lax.dot_general(a, b, (((1,), (1,)), ((), ())), preferred_element_type=F32)


def tn(a, b):
    return lax.dot_general(a, b, (((0,), (0,)), ((), ())), preferred_element_type=F32)


def halves(a):
    high = a.astype(BF)
    return high, (a - high.astype(F32)).astype(BF)


def kernel(
    dims, nx,
    ridge_in, q_in, k_in, v_in, w_in, og_in, doc_in,
    lay, gq, gk_out, gv_out, gw,
    ridge,
    q, k, v, w, doc, lab_own, lab_mate, lab_chip, lab, edge_own, edge,
    t_own, t_mate, t_send, t_recv, t_line, t_lines, p_send, p_recv, p_mate, p_all,
    b_own, b_mate, b_send, b_recv, b_line, b_lines, r_send, r_recv, r_mate, r_all,
    cot, cot_y, cot_t, mix, l_send, l_recv, l_own,
    gw_own, gw_send, gw_recv, z_send, z_recv,
    gk, gv,
    load_sem, send_sem, recv_sem,
):
    ny, nz, nc = dims
    heads = ridge.shape[1]
    width = heads * DH
    me, mh = lax.axis_index("seq"), lax.axis_index("head")
    c = lax.rem(me, nc)
    z = lax.rem(me // nc, nz)
    y = me // (nc * nz)
    other = nc - 1 - c
    rows = t_line.shape[0]
    strip = gw.shape[0]

    def at(yy, zz, cc):
        return (yy * nz + zz) * nc + cc

    mate = at(y, z, other)
    y_peers = [lax.rem(y + i, ny) for i in range(1, ny)]
    z_peers = [lax.rem(z + i, nz) for i in sorted(range(1, nz), key=lambda i: -min(i, nz - i))]
    x_peers = [lax.rem(mh + i, nx) for i in range(1, nx)]

    names = ("lab_mate", "lab", "edge", "t_mate", "t", "t_line", "p", "p_mate", "b_mate", "b", "b_line",
             "r", "r_mate", "cot", "cot_y", "mix", "l", "gw", "z")
    sems = {name: i for i, name in enumerate(names)}
    sent = []

    def send(name, src, dst, seq, head=None):
        copy = pltpu.make_async_remote_copy(
            src_ref=src, dst_ref=dst,
            send_sem=send_sem.at[sems[name]], recv_sem=recv_sem.at[sems[name]],
            device_id=(seq, mh if head is None else head), device_id_type=MESH,
        )
        copy.start()

    def settle(name, ref):
        sent.append((name, ref))
        pltpu.make_async_copy(ref, ref, recv_sem.at[sems[name]]).wait()

    loads = [
        pltpu.make_async_copy(src, dst, load_sem.at[i])
        for i, (src, dst) in enumerate(
            ((doc_in, doc), (k_in, k), (v_in, v), (og_in, cot.at[mh]), (w_in, w), (q_in, q), (ridge_in, ridge))
        )
    ]
    for load in loads:
        load.start()

    barrier = pltpu.get_barrier_semaphore()
    peers = [(at(y, zz, c), mh) for zz in z_peers] + [(at(yy, z, c), mh) for yy in y_peers]
    peers += [(me, hh) for hh in x_peers] + [(mate, mh)]
    for peer in peers:
        pl.semaphore_signal(barrier, inc=1, device_id=peer, device_id_type=MESH)

    loads[0].wait()
    doc_row = jnp.broadcast_to(doc[...].astype(F32), (DH, DH))
    doc_col = doc_row.T
    last, first = doc_col[DH - 1 : DH, :], doc_col[0:1, :]
    lab_own[0:1, :] = last
    lab_own[1:2, :] = first
    below = lax.broadcasted_iota(jnp.int32, (DH, DH), 1) <= lax.broadcasted_iota(jnp.int32, (DH, DH), 0)
    same_doc = jnp.where((doc_row == doc_col) & below, 1.0, 0.0).astype(F32)
    tail = jnp.where(doc_col == last, 1.0, 0.0).astype(BF)
    head_rows = jnp.where(doc_col == first, 1.0, 0.0).astype(F32)

    in_half = heads // nc
    per_head = 2 * DH // rows

    def put_state(ref, h, state):
        first_slice = (h % in_half) * per_head
        ref[h // in_half, first_slice : first_slice + per_head] = state.astype(BF).reshape(per_head, rows, DH)

    def get_state(ref, h):
        first_slice = (h % in_half) * per_head
        return ref[h // in_half, first_slice : first_slice + per_head].reshape(2 * DH, DH)

    loads[1].wait()
    loads[2].wait()
    for h in range(heads):
        cols = slice(h * DH, (h + 1) * DH)
        kh, vh = k[:, cols], v[:, cols]
        put_state(t_own, h, tn(jnp.concatenate([kh * tail, vh * tail], axis=1), kh))

    loads[3].wait()
    pl.semaphore_wait(barrier, len(peers))

    def combine(own, from_mate, chip, row, leads):
        joined = jnp.where(lab_own[row : row + 1, :] == lab_mate[row : row + 1, :], 1.0, 0.0)
        own_part = jnp.where(leads, joined, 1.0)
        mate_part = jnp.where(leads, 1.0, joined)
        for i in range(nz):
            chip[i] = (own[c, i].astype(F32) * own_part + from_mate[i].astype(F32) * mate_part).astype(BF)

    def line_total(parts, line, row, reverse):
        total, before = jnp.zeros((rows, DH), F32), None
        for i in reversed(range(nz)) if reverse else range(nz):
            label = lab[i, row : row + 1, :]
            if before is not None:
                total = jnp.where(label == before, total, 0.0)
            total = total + parts[i].astype(F32)
            before = label
        line[...] = total.astype(BF)

    def incoming(lines, row, reverse):
        total, before = jnp.zeros((rows, DH), F32), jnp.full((1, DH), -1.0, F32)
        for i in reversed(range(ny)) if reverse else range(ny):
            label = edge[i, row : row + 1, :]
            grown = jnp.where(label == before, total, 0.0) + lines[i].astype(F32)
            reached = i > y if reverse else i < y
            total = jnp.where(reached, grown, total)
            before = jnp.where(reached, label, before)
        return total, before

    def scan(parts, total, before, out, row, reverse):
        chip_before = before
        for i in reversed(range(nz)) if reverse else range(nz):
            label = lab[i, row : row + 1, :]
            out[i] = total.astype(BF)
            chip_before = jnp.where(i == z, before, chip_before)
            total = jnp.where(label == before, total, 0.0) + parts[i].astype(F32)
            before = label
        return chip_before

    def spread(own, from_mate, chip, to_mate, whole, row, chip_before, leads):
        lead_label = jnp.where(leads, lab_own[row : row + 1, :], lab_mate[row : row + 1, :])
        joined = jnp.where(lead_label == chip_before, 1.0, 0.0)
        for i in range(nz):
            ahead = chip[i].astype(F32)
            lead_state = jnp.where(leads, own[c, i].astype(F32), from_mate[i].astype(F32))
            trail = lead_state + joined * ahead
            whole[c, i] = jnp.where(leads, ahead, trail).astype(BF)
            to_mate[i] = jnp.where(leads, trail, ahead).astype(BF)
        return jnp.where(leads, chip_before, lead_label)

    leads, leads_back = c == 0, c == nc - 1

    send("lab_mate", lab_own, lab_mate, mate)
    send("t_mate", t_own.at[other], t_mate, mate)
    for hh in x_peers:
        send("cot", cot.at[mh], cot.at[mh], me, hh)

    settle("lab_mate", lab_mate)
    lab_chip[0:1, :] = jnp.where(leads, lab_mate[0:1, :], lab_own[0:1, :])
    lab_chip[1:2, :] = jnp.where(leads, lab_own[1:2, :], lab_mate[1:2, :])
    lab[z] = lab_chip[...]
    for zz in z_peers:
        send("lab", lab_chip, lab.at[z], at(y, zz, c))
    settle("t_mate", t_mate)
    combine(t_own, t_mate, t_send, 0, leads)
    for zz in z_peers:
        send("t", t_send.at[zz], t_recv.at[z], at(y, zz, c))
    t_recv[z] = t_send[z]

    settle("lab", lab.at[pl.ds(0, nz - 1)])
    edge_own[0:1, :] = lab[nz - 1, 0:1, :]
    edge_own[1:2, :] = lab[0, 1:2, :]
    edge[y] = edge_own[...]
    for yy in y_peers:
        send("edge", edge_own, edge.at[y], at(yy, z, c))
    settle("t", t_recv.at[pl.ds(0, nz - 1)])
    line_total(t_recv, t_line, 0, False)
    for yy in y_peers:
        send("t_line", t_line, t_lines.at[y], at(yy, z, c))
    t_lines[y] = t_line[...]
    settle("edge", edge.at[pl.ds(0, ny - 1)])
    settle("t_line", t_lines.at[pl.ds(0, ny - 1)])
    total, before = incoming(t_lines, 0, False)
    chip_before = scan(t_recv, total, before, p_send, 0, False)
    for zz in z_peers:
        send("p", p_send.at[zz], p_recv.at[z], at(y, zz, c))
    p_recv[z] = p_send[z]

    loads[4].wait()
    settle("cot", cot.at[pl.ds(0, nx - 1)])
    for yy in y_peers:
        send("cot_y", cot.at[yy], cot_y.at[y], at(yy, z, c))
    cot_y[y] = cot[y]
    do = nt(cot[0], w[:, 0:width])
    for b in range(1, nx):
        do = do + nt(cot[b], w[:, b * width : (b + 1) * width])

    do_high, do_low, score_two, target_own = [], [], [], []
    for h in range(heads):
        cols = slice(h * DH, (h + 1) * DH)
        kh, vh = k[:, cols], v[:, cols]
        high, low = halves(do[:, cols])
        two = (nt(high, vh) + nt(low, vh)) * same_doc
        two_high, two_low = halves(two)
        do_high.append(high)
        do_low.append(low)
        score_two.append(two)
        target_own.append(nn(two_high, kh) + nn(two_low, kh))
    loads[5].wait()
    loads[6].wait()

    settle("p", p_recv.at[pl.ds(0, nz - 1)])
    label_in = spread(t_own, t_mate, p_recv, p_mate, p_all, 0, chip_before, leads)
    send("p_mate", p_mate, p_all.at[c], mate)
    carried = jnp.where(doc_col == label_in, 1.0, 0.0).astype(F32)
    carried_two = jnp.concatenate([carried, carried], axis=0).astype(BF)
    same_two = jnp.concatenate([same_doc, same_doc], axis=0)
    settle("p_mate", p_mate)

    keys, x, r, p, rr = [], [], [], [], []
    for h in range(heads):
        cols = slice(h * DH, (h + 1) * DH)
        kh = k[:, cols]
        state = get_state(p_all, h)
        value_in = state[DH:]
        target = carried * (nn(do_high[h], value_in) + nn(do_low[h], value_in)) + target_own[h]
        b = jnp.concatenate([q[:, cols].astype(F32), target], axis=0)
        keys.append(jnp.concatenate([kh, state[:DH]], axis=0))
        x.append(jnp.zeros_like(b))
        r.append(b)
        p.append(b)
        rr.append(jnp.sum(b * b, axis=1, keepdims=True))
    for number in range(CG_STEPS):
        for h in range(heads):
            cols = slice(h * DH, (h + 1) * DH)
            kh = k[:, cols]
            p_high, p_low = halves(p[h])
            scores = (nt(p_high, kh) + nt(p_low, kh)) * same_two
            s_high, s_low = halves(scores)
            applied = (
                nn(jnp.concatenate([s_high, p_high * carried_two], axis=1), keys[h])
                + nn(jnp.concatenate([s_low, p_low * carried_two], axis=1), keys[h])
                + ridge[0, h] * p[h]
            )
            step = rr[h] / (jnp.sum(p[h] * applied, axis=1, keepdims=True) + EPS)
            x[h] = x[h] + step * p[h]
            if number < CG_STEPS - 1:
                r[h] = r[h] - step * applied
                fresh = jnp.sum(r[h] * r[h], axis=1, keepdims=True)
                p[h] = r[h] + fresh / (rr[h] + EPS) * p[h]
                rr[h] = fresh

    x_high, x_low, score_x = [], [], []
    for h in range(heads):
        high, low = halves(x[h])
        x_high.append(high)
        x_low.append(low)
        rows_x = (head_rows * x[h][:DH]).astype(BF)
        both = tn(jnp.concatenate([do_high[h], high[DH:]], axis=1), rows_x)
        cross = both[DH:]
        put_state(b_own, h, jnp.concatenate([both[:DH], cross + cross.T], axis=0))
    send("b_mate", b_own.at[other], b_mate, mate)

    for h in range(heads):
        cols = slice(h * DH, (h + 1) * DH)
        kh, vh = k[:, cols], v[:, cols]
        value_in = get_state(p_all, h)[DH:]
        scores = (nt(x_high[h], kh) + nt(x_low[h], kh)) * same_two
        score_x.append(scores)
        s_high, s_low = halves(scores[:DH])
        out = nn(s_high, vh) + nn(s_low, vh) + carried * (nt(x_high[h][:DH], value_in) + nt(x_low[h][:DH], value_in))
        mix[y, :, cols] = out.astype(BF)
    for yy in y_peers:
        send("mix", mix.at[y], mix.at[y], at(yy, z, c))

    settle("b_mate", b_mate)
    combine(b_own, b_mate, b_send, 1, leads_back)
    for zz in z_peers:
        send("b", b_send.at[zz], b_recv.at[z], at(y, zz, c))
    b_recv[z] = b_send[z]

    for h in range(heads):
        gq[:, h * DH : (h + 1) * DH] = x[h][DH:].astype(BF)
    mixed = mix[y]
    for i, hh in enumerate(x_peers):
        part = nn(mixed, w[:, pl.ds(pl.multiple_of(hh * width, width), width)])
        l_send[i] = part.astype(BF)
        send("l", l_send.at[i], l_recv.at[mh], me, hh)
    l_own[...] = nn(mixed, w[:, pl.ds(pl.multiple_of(mh * width, width), width)])
    l_recv[mh] = jnp.zeros((DH, width), BF)

    for h in range(heads):
        cols = slice(h * DH, (h + 1) * DH)
        one = score_x[h][:DH].astype(BF)
        rest = (score_two[h] - score_x[h][DH:]).astype(BF)
        gv[:, cols] = tn(one, do_high[h])
        gk[:, cols] = tn(rest, x_high[h][:DH]) - tn(one, x_high[h][DH:])

    settle("b", b_recv.at[pl.ds(0, nz - 1)])
    line_total(b_recv, b_line, 1, True)
    for yy in y_peers:
        send("b_line", b_line, b_lines.at[y], at(yy, z, c))
    b_lines[y] = b_line[...]

    settle("cot_y", cot_y.at[pl.ds(0, ny - 1)])
    for b in range(ny):
        turned = cot_y[b].T
        for zz in range(nz):
            for cc in range(nc):
                cut = (zz * nc + cc) * strip
                cot_t[cc, zz * strip : (zz + 1) * strip, b * DH : (b + 1) * DH] = turned[cut : cut + strip, :]

    settle("mix", mix.at[pl.ds(0, ny - 1)])
    gathered = mix[...].reshape(ny * DH, width)
    gw_send[...] = nn(cot_t[other], gathered).astype(BF).reshape(nz, strip, width)
    send("gw", gw_send, gw_recv, mate)
    gw_own[...] = nn(cot_t[c], gathered).reshape(nz, strip, width)
    settle("b_line", b_lines.at[pl.ds(0, ny - 1)])
    total, before = incoming(b_lines, 1, True)
    chip_before = scan(b_recv, total, before, r_send, 1, True)
    for zz in z_peers:
        send("r", r_send.at[zz], r_recv.at[z], at(y, zz, c))
    r_recv[z] = r_send[z]

    settle("gw", gw_recv)
    z_send[...] = (gw_own[...] + gw_recv[...].astype(F32)).astype(BF)
    for zz in z_peers:
        send("z", z_send.at[zz], z_recv.at[z], at(y, zz, c))
    z_recv[z] = z_send[z]

    settle("l", l_recv.at[pl.ds(0, nx - 1)])
    total = l_own[...]
    for b in range(nx):
        total = total + l_recv[b].astype(F32)
    lay[...] = total.astype(BF)

    settle("r", r_recv.at[pl.ds(0, nz - 1)])
    label_next = spread(b_own, b_mate, r_recv, r_mate, r_all, 1, chip_before, leads_back)
    send("r_mate", r_mate, r_all.at[c], mate)
    later = jnp.where(doc_col == label_next, 1.0, 0.0).astype(F32)
    settle("r_mate", r_mate)
    for h in range(heads):
        cols = slice(h * DH, (h + 1) * DH)
        kh, vh = k[:, cols], v[:, cols]
        state = get_state(r_all, h)
        grad_state, gram_grad = state[:DH], state[DH:]
        gv_out[:, cols] = (gv[:, cols] + later * nt(kh, grad_state)).astype(BF)
        gk_out[:, cols] = (gk[:, cols] + later * (nn(vh, grad_state) - nn(kh, gram_grad))).astype(BF)

    settle("z", z_recv.at[pl.ds(0, nz - 1)])
    total = z_recv[0].astype(F32)
    for b in range(1, nz):
        total = total + z_recv[b].astype(F32)
    gw[...] = total

    for name, ref in sent:
        pltpu.make_async_copy(ref, ref, send_sem.at[sems[name]]).wait()


def move(*refs):
    count = (len(refs) - 1) // 2
    ins, outs, sem = refs[:count], refs[count : 2 * count], refs[-1]
    writes = [pltpu.make_async_copy(a, b, sem.at[i]) for i, (a, b) in enumerate(zip(ins, outs))]
    for write in writes:
        write.start()
    for write in writes:
        write.wait()


def per_device(dims, nx, query_rows, key_rows, value_rows, ridge_reg, out_weight, out_grad, doc_ids):
    ny, nz, nc = dims
    heads = ridge_reg.shape[0]
    width = heads * DH
    rows = heads * 2 * DH // (nc * nz)
    strip = width // (nz * nc)
    any_space = pl.BlockSpec(memory_space=pl.ANY)
    half = pltpu.VMEM((nz, rows, DH), BF)
    both = pltpu.VMEM((nc, nz, rows, DH), BF)
    line = pltpu.VMEM((rows, DH), BF)
    lines = pltpu.VMEM((ny, rows, DH), BF)
    label = pltpu.VMEM((2, DH), F32)
    wide = pltpu.VMEM((DH, width), BF)
    held = (wide, wide, wide, wide, pltpu.VMEM((strip, width), F32))
    states = [both, half, half, half, line, lines, half, half, half, both]
    made = pl.pallas_call(
        functools.partial(kernel, dims, nx),
        out_shape=held,
        in_specs=[any_space] * 7,
        out_specs=(pl.BlockSpec(memory_space=pltpu.VMEM),) * 5,
        scratch_shapes=[
            pltpu.SMEM((1, heads), F32),
            wide,
            wide,
            wide,
            pltpu.VMEM((width, nx * width), BF),
            pltpu.VMEM((1, DH), jnp.int32),
            label,
            label,
            label,
            pltpu.VMEM((nz, 2, DH), F32),
            label,
            pltpu.VMEM((ny, 2, DH), F32),
            *states,
            *states,
            pltpu.VMEM((nx, DH, width), BF),
            pltpu.VMEM((ny, DH, width), BF),
            pltpu.VMEM((nc, nz * strip, ny * DH), BF),
            pltpu.VMEM((ny, DH, width), BF),
            pltpu.VMEM((nx, DH, width), BF),
            pltpu.VMEM((nx, DH, width), BF),
            pltpu.VMEM((DH, width), F32),
            pltpu.VMEM((nz, strip, width), F32),
            pltpu.VMEM((nz, strip, width), BF),
            pltpu.VMEM((nz, strip, width), BF),
            pltpu.VMEM((nz, strip, width), BF),
            pltpu.VMEM((nz, strip, width), BF),
            pltpu.VMEM((DH, width), F32),
            pltpu.VMEM((DH, width), F32),
            pltpu.SemaphoreType.DMA((7,)),
            pltpu.SemaphoreType.DMA((19,)),
            pltpu.SemaphoreType.DMA((19,)),
        ],
        compiler_params=pltpu.CompilerParams(collective_id=0, has_side_effects=True),
    )(ridge_reg.reshape(1, -1), query_rows, key_rows, value_rows, out_weight, out_grad, doc_ids.reshape(1, -1))
    return pl.pallas_call(
        move,
        out_shape=[jax.ShapeDtypeStruct(a.shape, a.dtype) for a in made],
        in_specs=[pl.BlockSpec(memory_space=pltpu.VMEM)] * 5,
        out_specs=[any_space] * 5,
        scratch_shapes=[pltpu.SemaphoreType.DMA((5,))],
    )(*[pltpu.with_memory_space_constraint(a, pltpu.VMEM) for a in made])


def build(mesh, dims):
    nx = mesh.shape["head"]
    spec = P("seq", "head")
    return jax.shard_map(
        functools.partial(per_device, dims, nx),
        mesh=mesh,
        in_specs=(spec, spec, spec, P("head"), P("head", None), spec, P("seq")),
        out_specs=(spec,) * 5,
        check_vma=False,
    )


def solution(mesh):
    return build(mesh, SEQ_DIMS)
```

```python
import functools

import jax
import jax.numpy as jnp
from jax import lax
from jax.experimental import pallas as pl
from jax.experimental.pallas import tpu as pltpu
from jax.sharding import PartitionSpec as P

CG_STEPS = 4
EPS = 1e-6
DH = 128
F32 = jnp.float32
BF = jnp.bfloat16
MESH = pl.DeviceIdType.MESH

SEQ_DIMS = (4, 8, 2)


def nn(a, b):
    return lax.dot_general(a, b, (((1,), (0,)), ((), ())), preferred_element_type=F32)


def nt(a, b):
    return lax.dot_general(a, b, (((1,), (1,)), ((), ())), preferred_element_type=F32)


def tn(a, b):
    return lax.dot_general(a, b, (((0,), (0,)), ((), ())), preferred_element_type=F32)


def halves(a):
    high = a.astype(BF)
    return high, (a - high.astype(F32)).astype(BF)


def twice(product, high, low, right):
    axis = 1 if product is nt else 0
    return product(jnp.concatenate([high, low], axis=1), jnp.concatenate([right, right], axis=axis))


def kernel(
    dims, nx,
    ridge_in, q_in, k_in, v_in, w_in, og_in, doc_in,
    lay, gq, gk_out, gv_out, gw,
    ridge,
    q, k, v, w, doc, lab_own, lab_mate, lab_chip, lab, edge_own, edge,
    t_own, t_mate, t_send, t_recv, t_line, t_lines, p_send, p_recv, p_mate, p_all,
    b_own, b_mate, b_send, b_recv, b_line, b_lines, r_send, r_recv, r_mate, r_all,
    cot, cot_y, cot_t, do_all, target_own, x_all, mix, l_send, l_recv, l_own,
    gw_own, gw_send, gw_recv, z_send, z_recv,
    gk, gv,
    load_sem, send_sem, recv_sem,
):
    ny, nz, nc = dims
    heads = ridge.shape[1]
    width = heads * DH
    me, mh = lax.axis_index("seq"), lax.axis_index("head")
    c = lax.rem(me, nc)
    z = lax.rem(me // nc, nz)
    y = me // (nc * nz)
    other = nc - 1 - c
    rows = t_line.shape[0]
    strip = gw.shape[0]

    def at(yy, zz, cc):
        return (yy * nz + zz) * nc + cc

    mate = at(y, z, other)
    y_peers = [lax.rem(y + i, ny) for i in sorted(range(1, ny), key=lambda i: -min(i, ny - i))]
    z_peers = [lax.rem(z + i, nz) for i in sorted(range(1, nz), key=lambda i: -min(i, nz - i))]
    x_peers = [lax.rem(mh + i, nx) for i in range(1, nx)]

    names = ("lab_mate", "lab", "edge", "t_mate", "t", "t_line", "p", "p_mate", "b_mate", "b", "b_line",
             "r", "r_mate", "cot", "cot_y", "l", "mix0", "mix1", "gw0", "gw1", "z0", "z1")
    sems = {name: i for i, name in enumerate(names)}
    sent = []

    def send(name, src, dst, seq, head=None):
        copy = pltpu.make_async_remote_copy(
            src_ref=src, dst_ref=dst,
            send_sem=send_sem.at[sems[name]], recv_sem=recv_sem.at[sems[name]],
            device_id=(seq, mh if head is None else head), device_id_type=MESH,
        )
        copy.start()

    def settle(name, ref):
        sent.append((name, ref))
        pltpu.make_async_copy(ref, ref, recv_sem.at[sems[name]]).wait()

    loads = [
        pltpu.make_async_copy(src, dst, load_sem.at[i])
        for i, (src, dst) in enumerate(
            ((doc_in, doc), (k_in, k), (v_in, v), (og_in, cot.at[mh]), (w_in, w), (q_in, q), (ridge_in, ridge))
        )
    ]
    for load in loads:
        load.start()

    barrier = pltpu.get_barrier_semaphore()
    peers = [(at(y, zz, c), mh) for zz in z_peers] + [(at(yy, z, c), mh) for yy in y_peers]
    peers += [(me, hh) for hh in x_peers] + [(mate, mh)]
    for peer in peers:
        pl.semaphore_signal(barrier, inc=1, device_id=peer, device_id_type=MESH)

    loads[0].wait()
    doc_row = jnp.broadcast_to(doc[...].astype(F32), (DH, DH))
    doc_col = doc_row.T
    last, first = doc_col[DH - 1 : DH, :], doc_col[0:1, :]
    lab_own[0:1, :] = last
    lab_own[1:2, :] = first
    below = lax.broadcasted_iota(jnp.int32, (DH, DH), 1) <= lax.broadcasted_iota(jnp.int32, (DH, DH), 0)
    same_doc = jnp.where((doc_row == doc_col) & below, 1.0, 0.0).astype(F32)
    tail = jnp.where(doc_col == last, 1.0, 0.0).astype(BF)
    head_rows = jnp.where(doc_col == first, 1.0, 0.0).astype(F32)

    in_half = heads // nc
    per_head = 2 * DH // rows
    chunk = in_half * DH
    order = [(half, i) for half in range(nc) for i in range(in_half)]

    def put_state(ref, half, i, state):
        ref[half, i * per_head : (i + 1) * per_head] = state.astype(BF).reshape(per_head, rows, DH)

    def get_state(ref, half, i):
        return ref[half, i * per_head : (i + 1) * per_head].reshape(2 * DH, DH)

    def cols_of(half, i):
        start = (half * in_half + i) * DH
        return pl.ds(start if isinstance(start, int) else pl.multiple_of(start, DH), DH)

    loads[1].wait()
    loads[2].wait()
    def gram(half):
        for i in range(in_half):
            cols = cols_of(half, i)
            kh, vh = k[:, cols], v[:, cols]
            put_state(t_own, half, i, tn(jnp.concatenate([kh * tail, vh * tail], axis=1), kh))

    gram(other)
    loads[3].wait()
    pl.semaphore_wait(barrier, len(peers))

    def combine(own, from_mate, chip, row, leads):
        joined = jnp.where(lab_own[row : row + 1, :] == lab_mate[row : row + 1, :], 1.0, 0.0)
        own_part = jnp.where(leads, joined, 1.0)
        mate_part = jnp.where(leads, 1.0, joined)
        for i in range(nz):
            chip[i] = (own[c, i].astype(F32) * own_part + from_mate[i].astype(F32) * mate_part).astype(BF)

    def line_total(parts, line, row, reverse):
        total, before = jnp.zeros((rows, DH), F32), None
        for i in reversed(range(nz)) if reverse else range(nz):
            label = lab[i, row : row + 1, :]
            if before is not None:
                total = jnp.where(label == before, total, 0.0)
            total = total + parts[i].astype(F32)
            before = label
        line[...] = total.astype(BF)

    def incoming(lines, row, reverse):
        total, before = jnp.zeros((rows, DH), F32), jnp.full((1, DH), -1.0, F32)
        for i in reversed(range(ny)) if reverse else range(ny):
            label = edge[i, row : row + 1, :]
            grown = jnp.where(label == before, total, 0.0) + lines[i].astype(F32)
            reached = i > y if reverse else i < y
            total = jnp.where(reached, grown, total)
            before = jnp.where(reached, label, before)
        return total, before

    def scan(parts, total, before, out, row, reverse):
        chip_before = before
        for i in reversed(range(nz)) if reverse else range(nz):
            label = lab[i, row : row + 1, :]
            out[i] = total.astype(BF)
            chip_before = jnp.where(i == z, before, chip_before)
            total = jnp.where(label == before, total, 0.0) + parts[i].astype(F32)
            before = label
        return chip_before

    def spread(own, from_mate, chip, to_mate, whole, row, chip_before, leads):
        lead_label = jnp.where(leads, lab_own[row : row + 1, :], lab_mate[row : row + 1, :])
        joined = jnp.where(lead_label == chip_before, 1.0, 0.0)
        for i in range(nz):
            ahead = chip[i].astype(F32)
            lead_state = jnp.where(leads, own[c, i].astype(F32), from_mate[i].astype(F32))
            trail = lead_state + joined * ahead
            whole[c, i] = jnp.where(leads, ahead, trail).astype(BF)
            to_mate[i] = jnp.where(leads, trail, ahead).astype(BF)
        return jnp.where(leads, chip_before, lead_label)

    leads, leads_back = c == 0, c == nc - 1

    send("lab_mate", lab_own, lab_mate, mate)
    send("t_mate", t_own.at[other], t_mate, mate)
    for hh in x_peers:
        send("cot", cot.at[mh], cot.at[mh], me, hh)
    gram(c)

    settle("lab_mate", lab_mate)
    lab_chip[0:1, :] = jnp.where(leads, lab_mate[0:1, :], lab_own[0:1, :])
    lab_chip[1:2, :] = jnp.where(leads, lab_own[1:2, :], lab_mate[1:2, :])
    lab[z] = lab_chip[...]
    for zz in z_peers:
        send("lab", lab_chip, lab.at[z], at(y, zz, c))
    settle("t_mate", t_mate)
    combine(t_own, t_mate, t_send, 0, leads)
    for zz in z_peers:
        send("t", t_send.at[zz], t_recv.at[z], at(y, zz, c))
    t_recv[z] = t_send[z]

    settle("lab", lab.at[pl.ds(0, nz - 1)])
    edge_own[0:1, :] = lab[nz - 1, 0:1, :]
    edge_own[1:2, :] = lab[0, 1:2, :]
    edge[y] = edge_own[...]
    for yy in y_peers:
        send("edge", edge_own, edge.at[y], at(yy, z, c))
    settle("t", t_recv.at[pl.ds(0, nz - 1)])
    line_total(t_recv, t_line, 0, False)
    for yy in y_peers:
        send("t_line", t_line, t_lines.at[y], at(yy, z, c))
    t_lines[y] = t_line[...]
    settle("edge", edge.at[pl.ds(0, ny - 1)])
    settle("t_line", t_lines.at[pl.ds(0, ny - 1)])
    total, before = incoming(t_lines, 0, False)
    chip_before = scan(t_recv, total, before, p_send, 0, False)
    for zz in z_peers:
        send("p", p_send.at[zz], p_recv.at[z], at(y, zz, c))
    p_recv[z] = p_send[z]

    loads[4].wait()
    settle("cot", cot.at[pl.ds(0, nx - 1)])
    for yy in y_peers:
        send("cot_y", cot.at[yy], cot_y.at[y], at(yy, z, c))
    cot_y[y] = cot[y]
    do = nt(cot[0], w[:, 0:width])
    for b in range(1, nx):
        do = do + nt(cot[b], w[:, b * width : (b + 1) * width])
    do_all[...] = do

    do_high, score_two = [], []
    for h, (half, i) in enumerate(order):
        cols = cols_of(half, i)
        kh, vh = k[:, cols], v[:, cols]
        high, low = halves(do[:, h * DH : (h + 1) * DH])
        two = twice(nt, high, low, vh) * same_doc
        do_high.append(high)
        score_two.append(two)
        target_own[:, cols] = twice(nn, *halves(two), kh)
    loads[5].wait()
    loads[6].wait()

    settle("p", p_recv.at[pl.ds(0, nz - 1)])
    label_in = spread(t_own, t_mate, p_recv, p_mate, p_all, 0, chip_before, leads)
    send("p_mate", p_mate, p_all.at[c], mate)
    carried = jnp.where(doc_col == label_in, 1.0, 0.0).astype(F32)
    carried_two = jnp.concatenate([carried, carried], axis=0).astype(BF)
    same_two = jnp.concatenate([same_doc, same_doc], axis=0)

    def solve(half):
        slots = range(in_half)
        cols = [cols_of(half, i) for i in slots]
        keys, x, r, p, rr = [], [], [], [], []
        for i in slots:
            state = get_state(p_all, half, i)
            value_in = state[DH:]
            target = carried * twice(nn, *halves(do_all[:, cols[i]]), value_in) + target_own[:, cols[i]]
            b = jnp.concatenate([q[:, cols[i]].astype(F32), target], axis=0)
            kh = k[:, cols[i]]
            keys.append(jnp.concatenate([kh, kh, state[:DH], state[:DH]], axis=0))
            x.append(jnp.zeros_like(b))
            r.append(b)
            p.append(b)
            rr.append(jnp.sum(b * b, axis=1, keepdims=True))
        for number in range(CG_STEPS):
            for i in slots:
                kh = k[:, cols[i]]
                p_high, p_low = halves(p[i])
                s_high, s_low = halves(twice(nt, p_high, p_low, kh) * same_two)
                left = jnp.concatenate([s_high, s_low, p_high * carried_two, p_low * carried_two], axis=1)
                applied = nn(left, keys[i]) + ridge[0, half * in_half + i] * p[i]
                step = rr[i] / (jnp.sum(p[i] * applied, axis=1, keepdims=True) + EPS)
                x[i] = x[i] + step * p[i]
                if number < CG_STEPS - 1:
                    r[i] = r[i] - step * applied
                    fresh = jnp.sum(r[i] * r[i], axis=1, keepdims=True)
                    p[i] = r[i] + fresh / (rr[i] + EPS) * p[i]
                    rr[i] = fresh
        for i in slots:
            x_all[half * in_half + i] = x[i]

    solve(c)
    settle("p_mate", p_mate)
    solve(other)

    for h, (half, i) in enumerate(order):
        x_h = x_all[h]
        rows_x = (head_rows * x_h[:DH]).astype(BF)
        both = tn(jnp.concatenate([do_high[h], x_h[DH:].astype(BF)], axis=1), rows_x)
        cross = both[DH:]
        put_state(b_own, half, i, jnp.concatenate([both[:DH], cross + cross.T], axis=0))
    send("b_mate", b_own.at[other], b_mate, mate)

    x_high, score_x = [], []
    for h, (half, i) in enumerate(order):
        cols = cols_of(half, i)
        kh, vh = k[:, cols], v[:, cols]
        value_in = get_state(p_all, half, i)[DH:]
        high, low = halves(x_all[h])
        x_high.append(high)
        scores = twice(nt, high, low, kh) * same_two
        score_x.append(scores)
        out = twice(nn, *halves(scores[:DH]), vh) + carried * twice(nt, high[:DH], low[:DH], value_in)
        group = h // in_half
        mix[group, y, :, i * DH : (i + 1) * DH] = out.astype(BF)
        if i == in_half - 1:
            for yy in y_peers:
                send(f"mix{group}", mix.at[group, y], mix.at[group, y], at(yy, z, c))

    settle("b_mate", b_mate)
    combine(b_own, b_mate, b_send, 1, leads_back)
    for zz in z_peers:
        send("b", b_send.at[zz], b_recv.at[z], at(y, zz, c))
    b_recv[z] = b_send[z]

    for h, (half, i) in enumerate(order):
        gq[:, cols_of(half, i)] = x_high[h][DH:]
    mixed = jnp.concatenate([mix[group, y] for group in range(nc)], axis=1)

    def project(block):
        cols = pl.ds(pl.multiple_of(block * width, width), width)
        return nn(mixed, w[:, cols])

    for i, hh in enumerate(x_peers):
        l_send[i] = project(hh).astype(BF)
        send("l", l_send.at[i], l_recv.at[mh], me, hh)
    l_own[...] = project(mh)
    l_recv[mh] = jnp.zeros((DH, width), BF)

    for h, (half, i) in enumerate(order):
        cols = cols_of(half, i)
        one = score_x[h][:DH].astype(BF)
        rest = (score_two[h] - score_x[h][DH:]).astype(BF)
        gv[:, cols] = tn(one, do_high[h])
        gk[:, cols] = tn(rest, x_high[h][:DH]) - tn(one, x_high[h][DH:])

    settle("cot_y", cot_y.at[pl.ds(0, ny - 1)])
    for b in range(ny):
        turned = cot_y[b].T
        for zz in range(nz):
            for cc in range(nc):
                cut = (zz * nc + cc) * strip
                cot_t[cc, zz * strip : (zz + 1) * strip, b * DH : (b + 1) * DH] = turned[cut : cut + strip, :]

    def product(group):
        settle(f"mix{group}", mix.at[group, pl.ds(0, ny - 1)])
        gathered = mix[group].reshape(ny * DH, chunk)
        gw_send[group] = nn(cot_t[other], gathered).astype(BF).reshape(nz, strip, chunk)
        send(f"gw{group}", gw_send.at[group], gw_recv.at[group], mate)
        gw_own[group] = nn(cot_t[c], gathered).reshape(nz, strip, chunk)

    def along_z(group):
        settle(f"gw{group}", gw_recv.at[group])
        z_send[group] = (gw_own[group] + gw_recv[group].astype(F32)).astype(BF)
        for zz in z_peers:
            send(f"z{group}", z_send.at[group, zz], z_recv.at[group, z], at(y, zz, c))
        z_recv[group, z] = z_send[group, z]

    product(0)
    settle("b", b_recv.at[pl.ds(0, nz - 1)])
    line_total(b_recv, b_line, 1, True)
    for yy in y_peers:
        send("b_line", b_line, b_lines.at[y], at(yy, z, c))
    b_lines[y] = b_line[...]
    along_z(0)
    product(1)
    settle("b_line", b_lines.at[pl.ds(0, ny - 1)])
    total, before = incoming(b_lines, 1, True)
    chip_before = scan(b_recv, total, before, r_send, 1, True)
    for zz in z_peers:
        send("r", r_send.at[zz], r_recv.at[z], at(y, zz, c))
    r_recv[z] = r_send[z]
    along_z(1)

    settle("l", l_recv.at[pl.ds(0, nx - 1)])
    total = l_own[...]
    for b in range(nx):
        total = total + l_recv[b].astype(F32)
    lay[...] = total.astype(BF)

    settle("r", r_recv.at[pl.ds(0, nz - 1)])
    label_next = spread(b_own, b_mate, r_recv, r_mate, r_all, 1, chip_before, leads_back)
    send("r_mate", r_mate, r_all.at[c], mate)
    later = jnp.where(doc_col == label_next, 1.0, 0.0).astype(F32)

    def finish(half):
        for i in range(in_half):
            cols = cols_of(half, i)
            kh, vh = k[:, cols], v[:, cols]
            state = get_state(r_all, half, i)
            grad_state, gram_grad = state[:DH], state[DH:]
            gv_out[:, cols] = (gv[:, cols] + later * nt(kh, grad_state)).astype(BF)
            gk_out[:, cols] = (gk[:, cols] + later * (nn(vh, grad_state) - nn(kh, gram_grad))).astype(BF)

    finish(c)
    settle("r_mate", r_mate)
    finish(other)

    for group in range(nc):
        settle(f"z{group}", z_recv.at[group, pl.ds(0, nz - 1)])
        total = z_recv[group, 0].astype(F32)
        for b in range(1, nz):
            total = total + z_recv[group, b].astype(F32)
        gw[:, group * chunk : (group + 1) * chunk] = total

    for name, ref in sent:
        pltpu.make_async_copy(ref, ref, send_sem.at[sems[name]]).wait()


def move(*refs):
    count = (len(refs) - 1) // 2
    ins, outs, sem = refs[:count], refs[count : 2 * count], refs[-1]
    writes = [pltpu.make_async_copy(a, b, sem.at[i]) for i, (a, b) in enumerate(zip(ins, outs))]
    for write in writes:
        write.start()
    for write in writes:
        write.wait()


def per_device(dims, nx, query_rows, key_rows, value_rows, ridge_reg, out_weight, out_grad, doc_ids):
    ny, nz, nc = dims
    heads = ridge_reg.shape[0]
    width = heads * DH
    rows = heads * 2 * DH // (nc * nz)
    strip = width // (nz * nc)
    any_space = pl.BlockSpec(memory_space=pl.ANY)
    half = pltpu.VMEM((nz, rows, DH), BF)
    both = pltpu.VMEM((nc, nz, rows, DH), BF)
    line = pltpu.VMEM((rows, DH), BF)
    lines = pltpu.VMEM((ny, rows, DH), BF)
    label = pltpu.VMEM((2, DH), F32)
    wide = pltpu.VMEM((DH, width), BF)
    held = (wide, wide, wide, wide, pltpu.VMEM((strip, width), F32))
    states = [both, half, half, half, line, lines, half, half, half, both]
    made = pl.pallas_call(
        functools.partial(kernel, dims, nx),
        out_shape=held,
        in_specs=[any_space] * 7,
        out_specs=(pl.BlockSpec(memory_space=pltpu.VMEM),) * 5,
        scratch_shapes=[
            pltpu.SMEM((1, heads), F32),
            wide,
            wide,
            wide,
            pltpu.VMEM((width, nx * width), BF),
            pltpu.VMEM((1, DH), jnp.int32),
            label,
            label,
            label,
            pltpu.VMEM((nz, 2, DH), F32),
            label,
            pltpu.VMEM((ny, 2, DH), F32),
            *states,
            *states,
            pltpu.VMEM((nx, DH, width), BF),
            pltpu.VMEM((ny, DH, width), BF),
            pltpu.VMEM((nc, nz * strip, ny * DH), BF),
            pltpu.VMEM((DH, width), F32),
            pltpu.VMEM((DH, width), F32),
            pltpu.VMEM((heads, 2 * DH, DH), F32),
            pltpu.VMEM((nc, ny, DH, width // nc), BF),
            pltpu.VMEM((nx, DH, width), BF),
            pltpu.VMEM((nx, DH, width), BF),
            pltpu.VMEM((DH, width), F32),
            pltpu.VMEM((nc, nz, strip, width // nc), F32),
            *[pltpu.VMEM((nc, nz, strip, width // nc), BF)] * 4,
            pltpu.VMEM((DH, width), F32),
            pltpu.VMEM((DH, width), F32),
            pltpu.SemaphoreType.DMA((7,)),
            pltpu.SemaphoreType.DMA((22,)),
            pltpu.SemaphoreType.DMA((22,)),
        ],
        compiler_params=pltpu.CompilerParams(collective_id=0, has_side_effects=True),
    )(ridge_reg.reshape(1, -1), query_rows, key_rows, value_rows, out_weight, out_grad, doc_ids.reshape(1, -1))
    return pl.pallas_call(
        move,
        out_shape=[jax.ShapeDtypeStruct(a.shape, a.dtype) for a in made],
        in_specs=[pl.BlockSpec(memory_space=pltpu.VMEM)] * 5,
        out_specs=[any_space] * 5,
        scratch_shapes=[pltpu.SemaphoreType.DMA((5,))],
    )(*[pltpu.with_memory_space_constraint(a, pltpu.VMEM) for a in made])


def build(mesh, dims):
    nx = mesh.shape["head"]
    spec = P("seq", "head")
    return jax.shard_map(
        functools.partial(per_device, dims, nx),
        mesh=mesh,
        in_specs=(spec, spec, spec, P("head"), P("head", None), spec, P("seq")),
        out_specs=(spec,) * 5,
        check_vma=False,
    )


def solution(mesh):
    return build(mesh, SEQ_DIMS)
```

```python
import functools

import jax
import jax.numpy as jnp
from jax import lax
from jax.experimental import pallas as pl
from jax.experimental.pallas import tpu as pltpu
from jax.sharding import PartitionSpec as P

CG_STEPS = 4
EPS = 1e-6
DH = 128
F32 = jnp.float32
BF = jnp.bfloat16
MESH = pl.DeviceIdType.MESH

SEQ_DIMS = (4, 8, 2)


def nn(a, b):
    return lax.dot_general(a, b, (((1,), (0,)), ((), ())), preferred_element_type=F32)


def nt(a, b):
    return lax.dot_general(a, b, (((1,), (1,)), ((), ())), preferred_element_type=F32)


def tn(a, b):
    return lax.dot_general(a, b, (((0,), (0,)), ((), ())), preferred_element_type=F32)


def halves(a):
    high = a.astype(BF)
    return high, (a - high.astype(F32)).astype(BF)


def twice(product, high, low, right):
    axis = 1 if product is nt else 0
    return product(jnp.concatenate([high, low], axis=1), jnp.concatenate([right, right], axis=axis))


def kernel(
    dims, nx,
    ridge_in, q_in, k_in, v_in, w_in, og_in, doc_in,
    lay, gq, gk_out, gv_out, gw,
    ridge,
    q, k, v, w, doc, lab_own, lab_mate, lab_chip, lab, edge_own, edge, note_chip, note, rim_own, rim,
    t_own, t_mate, t_send, t_recv, t_line, t_lines, p_send, p_recv, p_mate, p_all,
    b_own, b_mate, b_send, b_recv, b_line, b_lines, r_send, r_recv, r_mate, r_all,
    cot, cot_y, cot_t, do_all, target_own, x_all, mix, l_send, l_recv, l_own,
    gw_own, gw_send, gw_recv, z_send, z_far, z_add, z_recv,
    gk, gv,
    load_sem, send_sem, recv_sem,
):
    ny, nz, nc = dims
    heads = ridge.shape[1]
    width = heads * DH
    me, mh = lax.axis_index("seq"), lax.axis_index("head")
    c = lax.rem(me, nc)
    z = lax.rem(me // nc, nz)
    y = me // (nc * nz)
    other = nc - 1 - c
    rows = t_line.shape[0]
    strip = gw.shape[0]

    def at(yy, zz, cc):
        return (yy * nz + zz) * nc + cc

    mate = at(y, z, other)
    y_peers = [lax.rem(y + i, ny) for i in sorted(range(1, ny), key=lambda i: -min(i, ny - i))]
    z_peers = [lax.rem(z + i, nz) for i in sorted(range(1, nz), key=lambda i: -min(i, nz - i))]
    x_peers = [lax.rem(mh + i, nx) for i in range(1, nx)]

    names = ("lab_mate", "lab", "edge", "t_mate", "t", "t_line", "p", "p_mate", "b_mate", "b", "b_line", "note", "rim",
             "r", "r_mate", "cot", "cot_y", "l", "mix0", "mix1", "gw0", "gw1", "far0", "far1", "z0", "z1")
    sems = {name: i for i, name in enumerate(names)}
    sent = []

    def send(name, src, dst, seq, head=None):
        copy = pltpu.make_async_remote_copy(
            src_ref=src, dst_ref=dst,
            send_sem=send_sem.at[sems[name]], recv_sem=recv_sem.at[sems[name]],
            device_id=(seq, mh if head is None else head), device_id_type=MESH,
        )
        copy.start()

    def settle(name, ref, count=None):
        if count == 0:
            return
        ref = ref if count is None else ref.at[pl.ds(0, count)]
        sent.append((name, ref))
        pltpu.make_async_copy(ref, ref, recv_sem.at[sems[name]]).wait()

    loads = [
        pltpu.make_async_copy(src, dst, load_sem.at[i])
        for i, (src, dst) in enumerate(
            ((doc_in, doc), (k_in, k), (v_in, v), (og_in, cot.at[mh]), (w_in, w), (q_in, q), (ridge_in, ridge))
        )
    ]
    for load in loads:
        load.start()

    barrier = pltpu.get_barrier_semaphore()
    peers = [(at(y, zz, c), mh) for zz in z_peers] + [(at(yy, z, c), mh) for yy in y_peers]
    peers += [(me, hh) for hh in x_peers] + [(mate, mh)]
    for peer in peers:
        pl.semaphore_signal(barrier, inc=1, device_id=peer, device_id_type=MESH)

    loads[0].wait()
    doc_row = jnp.broadcast_to(doc[...].astype(F32), (DH, DH))
    doc_col = doc_row.T
    last, first = doc_col[DH - 1 : DH, :], doc_col[0:1, :]
    for small in (lab_own, lab_chip, edge_own, note_chip, rim_own):
        small[...] = jnp.zeros_like(small)
    lab_own[0:1, :] = last
    lab_own[1:2, :] = first
    same_doc = jnp.where(
        (doc_row == doc_col)
        & (lax.broadcasted_iota(jnp.int32, (DH, DH), 1) <= lax.broadcasted_iota(jnp.int32, (DH, DH), 0)),
        1.0,
        0.0,
    ).astype(F32)
    tail = jnp.where(doc_col == last, 1.0, 0.0).astype(BF)
    head_rows = jnp.where(doc_col == first, 1.0, 0.0).astype(F32)

    in_half = heads // nc
    chunk = in_half * DH
    order = [(half, i) for half in range(nc) for i in range(in_half)]
    row_idx = lax.broadcasted_iota(jnp.int32, (DH, DH), 0)
    col_idx = lax.broadcasted_iota(jnp.int32, (DH, DH), 1)

    def cols_of(half, i):
        start = (half * in_half + i) * DH
        return pl.ds(start if isinstance(start, int) else pl.multiple_of(start, DH), DH)

    loads[1].wait()
    loads[2].wait()
    def gram(half):
        for i in range(in_half):
            cols = cols_of(half, i)
            kh, vh = k[:, cols], v[:, cols]
            t_own[half, i] = tn(jnp.concatenate([kh * tail, vh * tail], axis=1), kh).astype(BF)

    gram(other)
    loads[3].wait()
    pl.semaphore_wait(barrier, len(peers))

    def combine(own, from_mate, packed, row, leads):
        joined = jnp.where(lab_own[row : row + 1, :] == lab_mate[row : row + 1, :], 1.0, 0.0)
        own_part = jnp.where(leads, joined, 1.0)
        mate_part = jnp.where(leads, 1.0, joined)
        one, two = [own[c, i].astype(F32) * own_part + from_mate[i].astype(F32) * mate_part for i in range(in_half)]
        mixed = jnp.where(col_idx >= row_idx, one[:DH], two[:DH])
        packed[...] = jnp.concatenate([mixed, one[DH:], two[DH:]], axis=0).astype(BF).reshape(nz, rows, DH)
        return jnp.sum(jnp.where(col_idx == row_idx, two[:DH], 0.0), axis=0, keepdims=True)

    def unpack(packed, diagonal):
        whole = packed[...].reshape(3 * DH, DH).astype(F32)
        mixed = whole[:DH]
        turned = mixed.T
        one = jnp.where(col_idx >= row_idx, mixed, turned)
        two = jnp.where(col_idx < row_idx, mixed, jnp.where(col_idx == row_idx, diagonal, turned))
        return jnp.concatenate([one, whole[DH : 2 * DH]], axis=0), jnp.concatenate([two, whole[2 * DH :]], axis=0)

    def line_total(parts, diagonals, line, row, reverse):
        total, diagonal, before = jnp.zeros((rows, DH), F32), jnp.zeros((1, DH), F32), None
        for i in reversed(range(nz)) if reverse else range(nz):
            label = lab[i, row : row + 1, :]
            if before is not None:
                total = jnp.where(label == before, total, 0.0)
                diagonal = jnp.where(label == before, diagonal, 0.0)
            total = total + parts[i].astype(F32)
            diagonal = diagonal + diagonals[i, 2:3, :]
            before = label
        line[...] = total.astype(BF)
        return diagonal

    def incoming(lines, diagonals, row, reverse):
        total, diagonal = jnp.zeros((rows, DH), F32), jnp.zeros((1, DH), F32)
        before = jnp.full((1, DH), -1.0, F32)
        for i in reversed(range(ny)) if reverse else range(ny):
            label = edge[i, row : row + 1, :]
            grown = jnp.where(label == before, total, 0.0) + lines[i].astype(F32)
            grown_diagonal = jnp.where(label == before, diagonal, 0.0) + diagonals[i, 2:3, :]
            reached = i > y if reverse else i < y
            total = jnp.where(reached, grown, total)
            diagonal = jnp.where(reached, grown_diagonal, diagonal)
            before = jnp.where(reached, label, before)
        return total, diagonal, before

    def scan(parts, diagonals, start, out, row, reverse):
        total, diagonal, before = start
        chip_diagonal, chip_before = diagonal, before
        for i in reversed(range(nz)) if reverse else range(nz):
            label = lab[i, row : row + 1, :]
            out[i] = total.astype(BF)
            chip_before = jnp.where(i == z, before, chip_before)
            chip_diagonal = jnp.where(i == z, diagonal, chip_diagonal)
            total = jnp.where(label == before, total, 0.0) + parts[i].astype(F32)
            diagonal = jnp.where(label == before, diagonal, 0.0) + diagonals[i, 2:3, :]
            before = label
        return chip_diagonal, chip_before

    def spread(own, from_mate, packed, chip_diagonal, to_mate, whole, row, chip_before, leads):
        lead_label = jnp.where(leads, lab_own[row : row + 1, :], lab_mate[row : row + 1, :])
        joined = jnp.where(lead_label == chip_before, 1.0, 0.0)
        for i, ahead in enumerate(unpack(packed, chip_diagonal)):
            lead_state = jnp.where(leads, own[c, i].astype(F32), from_mate[i].astype(F32))
            trail = lead_state + joined * ahead
            whole[c, i] = jnp.where(leads, ahead, trail).astype(BF)
            to_mate[i] = jnp.where(leads, trail, ahead).astype(BF)
        return jnp.where(leads, chip_before, lead_label)

    leads, leads_back = c == 0, c == nc - 1

    send("lab_mate", lab_own, lab_mate, mate)
    send("t_mate", t_own.at[other], t_mate, mate)
    for hh in x_peers:
        send("cot", cot.at[mh], cot.at[mh], me, hh)
    gram(c)

    settle("lab_mate", lab_mate)
    lab_chip[0:1, :] = jnp.where(leads, lab_mate[0:1, :], lab_own[0:1, :])
    lab_chip[1:2, :] = jnp.where(leads, lab_own[1:2, :], lab_mate[1:2, :])
    settle("t_mate", t_mate)
    lab_chip[2:3, :] = combine(t_own, t_mate, t_send, 0, leads)
    lab[z] = lab_chip[...]
    for zz in z_peers:
        send("lab", lab_chip, lab.at[z], at(y, zz, c))
        send("t", t_send.at[zz], t_recv.at[z], at(y, zz, c))
    t_recv[z] = t_send[z]

    settle("lab", lab, nz - 1)
    settle("t", t_recv, nz - 1)
    edge_own[0:1, :] = lab[nz - 1, 0:1, :]
    edge_own[1:2, :] = lab[0, 1:2, :]
    edge_own[2:3, :] = line_total(t_recv, lab, t_line, 0, False)
    edge[y] = edge_own[...]
    for yy in y_peers:
        send("edge", edge_own, edge.at[y], at(yy, z, c))
        send("t_line", t_line, t_lines.at[y], at(yy, z, c))
    t_lines[y] = t_line[...]
    settle("edge", edge, ny - 1)
    settle("t_line", t_lines, ny - 1)
    chip_diagonal, chip_before = scan(t_recv, lab, incoming(t_lines, edge, 0, False), p_send, 0, False)
    for zz in z_peers:
        send("p", p_send.at[zz], p_recv.at[z], at(y, zz, c))
    p_recv[z] = p_send[z]

    loads[4].wait()
    settle("cot", cot, nx - 1)
    for yy in y_peers:
        send("cot_y", cot.at[yy], cot_y.at[y], at(yy, z, c))
    cot_y[y] = cot[y]
    do = nt(cot[0], w[:, 0:width])
    for b in range(1, nx):
        do = do + nt(cot[b], w[:, b * width : (b + 1) * width])
    do_all[...] = do

    do_high, score_two = [], []
    for h, (half, i) in enumerate(order):
        cols = cols_of(half, i)
        kh, vh = k[:, cols], v[:, cols]
        high, low = halves(do[:, h * DH : (h + 1) * DH])
        two = twice(nt, high, low, vh) * same_doc
        do_high.append(high)
        score_two.append(two)
        target_own[:, cols] = twice(nn, *halves(two), kh)
    loads[5].wait()
    loads[6].wait()

    settle("p", p_recv, nz - 1)
    label_in = spread(t_own, t_mate, p_recv, chip_diagonal, p_mate, p_all, 0, chip_before, leads)
    send("p_mate", p_mate, p_all.at[c], mate)
    carried = jnp.where(doc_col == label_in, 1.0, 0.0).astype(F32)
    carried_two = jnp.concatenate([carried, carried], axis=0).astype(BF)
    same_two = jnp.concatenate([same_doc, same_doc], axis=0)

    def solve(half):
        slots = range(in_half)
        cols = [cols_of(half, i) for i in slots]
        keys, x, r, p, rr = [], [], [], [], []
        for i in slots:
            state = p_all[half, i]
            value_in = state[DH:]
            target = carried * twice(nn, *halves(do_all[:, cols[i]]), value_in) + target_own[:, cols[i]]
            b = jnp.concatenate([q[:, cols[i]].astype(F32), target], axis=0)
            kh = k[:, cols[i]]
            keys.append(jnp.concatenate([kh, kh, state[:DH], state[:DH]], axis=0))
            x.append(jnp.zeros_like(b))
            r.append(b)
            p.append(b)
            rr.append(jnp.sum(b * b, axis=1, keepdims=True))
        for number in range(CG_STEPS):
            for i in slots:
                kh = k[:, cols[i]]
                p_high, p_low = halves(p[i])
                s_high, s_low = halves(twice(nt, p_high, p_low, kh) * same_two)
                left = jnp.concatenate([s_high, s_low, p_high * carried_two, p_low * carried_two], axis=1)
                applied = nn(left, keys[i]) + ridge[0, half * in_half + i] * p[i]
                step = rr[i] / (jnp.sum(p[i] * applied, axis=1, keepdims=True) + EPS)
                x[i] = x[i] + step * p[i]
                if number < CG_STEPS - 1:
                    r[i] = r[i] - step * applied
                    fresh = jnp.sum(r[i] * r[i], axis=1, keepdims=True)
                    p[i] = r[i] + fresh / (rr[i] + EPS) * p[i]
                    rr[i] = fresh
        for i in slots:
            x_all[half * in_half + i] = x[i]

    solve(c)
    settle("p_mate", p_mate)
    solve(other)

    for h, (half, i) in enumerate(order):
        x_h = x_all[h]
        rows_x = (head_rows * x_h[:DH]).astype(BF)
        both = tn(jnp.concatenate([do_high[h], x_h[DH:].astype(BF)], axis=1), rows_x)
        cross = both[DH:]
        b_own[half, i] = jnp.concatenate([cross + cross.T, both[:DH]], axis=0).astype(BF)
    send("b_mate", b_own.at[other], b_mate, mate)

    x_high, score_x = [], []
    for h, (half, i) in enumerate(order):
        cols = cols_of(half, i)
        kh, vh = k[:, cols], v[:, cols]
        value_in = p_all[half, i, DH:, :]
        high, low = halves(x_all[h])
        x_high.append(high)
        scores = twice(nt, high, low, kh) * same_two
        score_x.append(scores)
        out = twice(nn, *halves(scores[:DH]), vh) + carried * twice(nt, high[:DH], low[:DH], value_in)
        group = h // in_half
        mix[group, y, :, i * DH : (i + 1) * DH] = out.astype(BF)
        if i == in_half - 1:
            for yy in y_peers:
                send(f"mix{group}", mix.at[group, y], mix.at[group, y], at(yy, z, c))

    settle("b_mate", b_mate)
    note_chip[2:3, :] = combine(b_own, b_mate, b_send, 1, leads_back)
    note[z] = note_chip[...]
    for zz in z_peers:
        send("note", note_chip, note.at[z], at(y, zz, c))
        send("b", b_send.at[zz], b_recv.at[z], at(y, zz, c))
    b_recv[z] = b_send[z]

    for h, (half, i) in enumerate(order):
        gq[:, cols_of(half, i)] = x_high[h][DH:]
    mixed = jnp.concatenate([mix[group, y] for group in range(nc)], axis=1)

    def project(block):
        cols = pl.ds(pl.multiple_of(block * width, width), width)
        return nn(mixed, w[:, cols])

    for i, hh in enumerate(x_peers):
        l_send[i] = project(hh).astype(BF)
        send("l", l_send.at[i], l_recv.at[mh], me, hh)
    l_own[...] = project(mh)
    l_recv[mh] = jnp.zeros((DH, width), BF)

    for h, (half, i) in enumerate(order):
        cols = cols_of(half, i)
        one = score_x[h][:DH].astype(BF)
        rest = (score_two[h] - score_x[h][DH:]).astype(BF)
        gv[:, cols] = tn(one, do_high[h])
        gk[:, cols] = tn(rest, x_high[h][:DH]) - tn(one, x_high[h][DH:])

    settle("cot_y", cot_y, ny - 1)
    for b in range(ny):
        turned = cot_y[b].T
        for zz in range(nz):
            for cc in range(nc):
                cut = (zz * nc + cc) * strip
                cot_t[cc, zz * strip : (zz + 1) * strip, b * DH : (b + 1) * DH] = turned[cut : cut + strip, :]

    def product(group):
        settle(f"mix{group}", mix.at[group], ny - 1)
        gathered = mix[group].reshape(ny * DH, chunk)
        gw_send[group] = nn(cot_t[other], gathered).astype(BF).reshape(nz, strip, chunk)
        send(f"gw{group}", gw_send.at[group], gw_recv.at[group], mate)
        gw_own[group] = nn(cot_t[c], gathered).reshape(nz, strip, chunk)

    distances = [i if i <= nz // 2 else i - nz for i in range(1, nz)]
    near = [d for d in (1, -1, 2, -2) if d in distances]
    far = [d for d in distances if abs(d) > 2]
    side = jnp.where(leads, 2, -2)
    two_away = [d for d in near if abs(d) == 2]

    def chip(distance):
        return lax.rem(z + distance + nz, nz)

    def along_z(group):
        settle(f"gw{group}", gw_recv.at[group])
        z_send[group] = (gw_own[group] + gw_recv[group].astype(F32)).astype(BF)
        for slot, d in enumerate(far):
            via = side if abs(d) == 4 else d // 3
            send(f"far{group}", z_send.at[group, chip(d)], z_far.at[group, slot], at(y, chip(via), c))
        for slot, d in enumerate(near):
            if d not in two_away:
                send(f"z{group}", z_send.at[group, chip(d)], z_recv.at[group, slot], at(y, chip(d), c))

    def along_z_again(group):
        if not two_away:
            return
        settle(f"far{group}", z_far.at[group])
        for d in two_away:
            total = z_send[group, chip(d)].astype(F32)
            for slot, e in enumerate(far):
                if abs(e) == 4:
                    total = total + jnp.where(side == d, z_far[group, slot].astype(F32), 0.0)
                elif e * d > 0:
                    total = total + z_far[group, slot].astype(F32)
            z_add[group, two_away.index(d)] = total.astype(BF)
            slot = near.index(d)
            send(f"z{group}", z_add.at[group, two_away.index(d)], z_recv.at[group, slot], at(y, chip(d), c))

    product(0)
    settle("note", note, nz - 1)
    settle("b", b_recv, nz - 1)
    rim_own[2:3, :] = line_total(b_recv, note, b_line, 1, True)
    rim[y] = rim_own[...]
    for yy in y_peers:
        send("rim", rim_own, rim.at[y], at(yy, z, c))
        send("b_line", b_line, b_lines.at[y], at(yy, z, c))
    b_lines[y] = b_line[...]
    along_z(0)
    product(1)
    along_z(1)
    settle("rim", rim, ny - 1)
    settle("b_line", b_lines, ny - 1)
    chip_diagonal, chip_before = scan(b_recv, note, incoming(b_lines, rim, 1, True), r_send, 1, True)
    for zz in z_peers:
        send("r", r_send.at[zz], r_recv.at[z], at(y, zz, c))
    r_recv[z] = r_send[z]

    along_z_again(0)
    settle("l", l_recv, nx - 1)
    total = l_own[...]
    for b in range(nx):
        total = total + l_recv[b].astype(F32)
    lay[...] = total.astype(BF)
    along_z_again(1)

    settle("r", r_recv, nz - 1)
    label_next = spread(b_own, b_mate, r_recv, chip_diagonal, r_mate, r_all, 1, chip_before, leads_back)
    send("r_mate", r_mate, r_all.at[c], mate)
    later = jnp.where(doc_col == label_next, 1.0, 0.0).astype(F32)

    def finish(half):
        for i in range(in_half):
            cols = cols_of(half, i)
            kh, vh = k[:, cols], v[:, cols]
            state = r_all[half, i]
            gram_grad, grad_state = state[:DH], state[DH:]
            gv_out[:, cols] = (gv[:, cols] + later * nt(kh, grad_state)).astype(BF)
            gk_out[:, cols] = (gk[:, cols] + later * (nn(vh, grad_state) - nn(kh, gram_grad))).astype(BF)

    finish(c)
    settle("r_mate", r_mate)
    finish(other)

    for group in range(nc):
        settle(f"z{group}", z_recv.at[group])
        total = z_send[group, z].astype(F32)
        for slot in range(len(near)):
            total = total + z_recv[group, slot].astype(F32)
        gw[:, group * chunk : (group + 1) * chunk] = total

    for name, ref in sent:
        pltpu.make_async_copy(ref, ref, send_sem.at[sems[name]]).wait()


def move(*refs):
    count = (len(refs) - 1) // 2
    ins, outs, sem = refs[:count], refs[count : 2 * count], refs[-1]
    writes = [pltpu.make_async_copy(a, b, sem.at[i]) for i, (a, b) in enumerate(zip(ins, outs))]
    for write in writes:
        write.start()
    for write in writes:
        write.wait()


def per_device(dims, nx, query_rows, key_rows, value_rows, ridge_reg, out_weight, out_grad, doc_ids):
    ny, nz, nc = dims
    heads = ridge_reg.shape[0]
    width = heads * DH
    rows = 3 * DH // nz
    strip = width // (nz * nc)
    any_space = pl.BlockSpec(memory_space=pl.ANY)
    packed = pltpu.VMEM((nz, rows, DH), BF)
    half = pltpu.VMEM((heads // nc, 2 * DH, DH), BF)
    both = pltpu.VMEM((nc, heads // nc, 2 * DH, DH), BF)
    line = pltpu.VMEM((rows, DH), BF)
    lines = pltpu.VMEM((ny, rows, DH), BF)
    label = pltpu.VMEM((4, DH), F32)
    wide = pltpu.VMEM((DH, width), BF)
    held = (wide, wide, wide, wide, pltpu.VMEM((strip, width), F32))
    states = [both, half, packed, packed, line, lines, packed, packed, half, both]
    made = pl.pallas_call(
        functools.partial(kernel, dims, nx),
        out_shape=held,
        in_specs=[any_space] * 7,
        out_specs=(pl.BlockSpec(memory_space=pltpu.VMEM),) * 5,
        scratch_shapes=[
            pltpu.SMEM((1, heads), F32),
            wide,
            wide,
            wide,
            pltpu.VMEM((width, nx * width), BF),
            pltpu.VMEM((1, DH), jnp.int32),
            label,
            label,
            label,
            pltpu.VMEM((nz, 4, DH), F32),
            label,
            pltpu.VMEM((ny, 4, DH), F32),
            label,
            pltpu.VMEM((nz, 4, DH), F32),
            label,
            pltpu.VMEM((ny, 4, DH), F32),
            *states,
            *states,
            pltpu.VMEM((nx, DH, width), BF),
            pltpu.VMEM((ny, DH, width), BF),
            pltpu.VMEM((nc, nz * strip, ny * DH), BF),
            pltpu.VMEM((DH, width), F32),
            pltpu.VMEM((DH, width), F32),
            pltpu.VMEM((heads, 2 * DH, DH), F32),
            pltpu.VMEM((nc, ny, DH, width // nc), BF),
            pltpu.VMEM((nx, DH, width), BF),
            pltpu.VMEM((nx, DH, width), BF),
            pltpu.VMEM((DH, width), F32),
            pltpu.VMEM((nc, nz, strip, width // nc), F32),
            *[pltpu.VMEM((nc, nz, strip, width // nc), BF)] * 3,
            pltpu.VMEM((nc, 3, strip, width // nc), BF),
            pltpu.VMEM((nc, 2, strip, width // nc), BF),
            pltpu.VMEM((nc, min(4, nz - 1), strip, width // nc), BF),
            pltpu.VMEM((DH, width), F32),
            pltpu.VMEM((DH, width), F32),
            pltpu.SemaphoreType.DMA((7,)),
            pltpu.SemaphoreType.DMA((26,)),
            pltpu.SemaphoreType.DMA((26,)),
        ],
        compiler_params=pltpu.CompilerParams(collective_id=0, has_side_effects=True),
    )(ridge_reg.reshape(1, -1), query_rows, key_rows, value_rows, out_weight, out_grad, doc_ids.reshape(1, -1))
    return pl.pallas_call(
        move,
        out_shape=[jax.ShapeDtypeStruct(a.shape, a.dtype) for a in made],
        in_specs=[pl.BlockSpec(memory_space=pltpu.VMEM)] * 5,
        out_specs=[any_space] * 5,
        scratch_shapes=[pltpu.SemaphoreType.DMA((5,))],
    )(*[pltpu.with_memory_space_constraint(a, pltpu.VMEM) for a in made])


def build(mesh, dims):
    nx = mesh.shape["head"]
    spec = P("seq", "head")
    return jax.shard_map(
        functools.partial(per_device, dims, nx),
        mesh=mesh,
        in_specs=(spec, spec, spec, P("head"), P("head", None), spec, P("seq")),
        out_specs=(spec,) * 5,
        check_vma=False,
    )


def solution(mesh):
    return build(mesh, SEQ_DIMS)
```

```python
import functools

import jax
import jax.numpy as jnp
from jax import lax
from jax.experimental import pallas as pl
from jax.experimental.pallas import tpu as pltpu
from jax.sharding import PartitionSpec as P

CG_STEPS = 4
EPS = 1e-6
DH = 128
F32 = jnp.float32
BF = jnp.bfloat16
MESH = pl.DeviceIdType.MESH

SEQ_DIMS = (4, 8, 2)


def nn(a, b):
    return lax.dot_general(a, b, (((1,), (0,)), ((), ())), preferred_element_type=F32)


def nt(a, b):
    return lax.dot_general(a, b, (((1,), (1,)), ((), ())), preferred_element_type=F32)


def tn(a, b):
    return lax.dot_general(a, b, (((0,), (0,)), ((), ())), preferred_element_type=F32)


def halves(a):
    high = a.astype(BF)
    return high, (a - high.astype(F32)).astype(BF)


def twice(product, high, low, right):
    axis = 1 if product is nt else 0
    return product(jnp.concatenate([high, low], axis=1), jnp.concatenate([right, right], axis=axis))


def kernel(
    dims, nx,
    ridge_in, q_in, k_in, v_in, w_in, og_in, doc_in,
    lay, gq, gk_out, gv_out, gw,
    ridge,
    q, k, v, w, doc, lab_own, lab_mate, lab_chip, lab, edge_own, edge, note_chip, note, rim_own, rim,
    t_own, t_mate, t_send, t_recv, t_line, t_lines, p_send, p_recv, p_mate, p_all,
    b_own, b_mate, b_send, b_recv, b_line, b_lines, r_send, r_recv, r_mate, r_all,
    cot, cot_y, cot_t, do_all, target_own, x_all, mix, l_send, l_recv, l_own,
    gw_own, gw_send, gw_recv, z_send, z_far, z_add, z_recv,
    gk, gv,
    load_sem, send_sem, recv_sem,
):
    ny, nz, nc = dims
    heads = ridge.shape[1]
    width = heads * DH
    me, mh = lax.axis_index("seq"), lax.axis_index("head")
    c = lax.rem(me, nc)
    z = lax.rem(me // nc, nz)
    y = me // (nc * nz)
    other = nc - 1 - c
    rows = t_line.shape[0]
    strip = gw.shape[0]

    def at(yy, zz, cc):
        return (yy * nz + zz) * nc + cc

    mate = at(y, z, other)
    y_peers = [lax.rem(y + i, ny) for i in sorted(range(1, ny), key=lambda i: -min(i, ny - i))]
    z_peers = [lax.rem(z + i, nz) for i in sorted(range(1, nz), key=lambda i: -min(i, nz - i))]
    x_peers = [lax.rem(mh + i, nx) for i in range(1, nx)]

    names = ("lab_mate", "lab", "edge", "t_mate", "t", "t_line", "p", "p_mate", "b_mate", "b", "b_line", "note", "rim",
             "r", "r_mate", "cot", "cot_y", "l", "mix0", "mix1", "gw0", "gw1", "far0", "far1", "z0", "z1")
    sems = {name: i for i, name in enumerate(names)}
    sent = []

    def send(name, src, dst, seq, head=None):
        copy = pltpu.make_async_remote_copy(
            src_ref=src, dst_ref=dst,
            send_sem=send_sem.at[sems[name]], recv_sem=recv_sem.at[sems[name]],
            device_id=(seq, mh if head is None else head), device_id_type=MESH,
        )
        copy.start()

    def settle(name, ref, count=None):
        if count == 0:
            return
        ref = ref if count is None else ref.at[pl.ds(0, count)]
        sent.append((name, ref))
        pltpu.make_async_copy(ref, ref, recv_sem.at[sems[name]]).wait()

    loads = [
        pltpu.make_async_copy(src, dst, load_sem.at[i])
        for i, (src, dst) in enumerate(
            ((doc_in, doc), (k_in, k), (v_in, v), (og_in, cot.at[mh]), (w_in, w), (q_in, q), (ridge_in, ridge))
        )
    ]
    for load in loads:
        load.start()

    barrier = pltpu.get_barrier_semaphore()
    peers = [(at(y, zz, c), mh) for zz in z_peers] + [(at(yy, z, c), mh) for yy in y_peers]
    peers += [(me, hh) for hh in x_peers] + [(mate, mh)]
    for peer in peers:
        pl.semaphore_signal(barrier, inc=1, device_id=peer, device_id_type=MESH)

    loads[0].wait()
    doc_row = jnp.broadcast_to(doc[...].astype(F32), (DH, DH))
    doc_col = doc_row.T
    last, first = doc_col[DH - 1 : DH, :], doc_col[0:1, :]
    for small in (lab_own, lab_chip, edge_own, note_chip, rim_own):
        small[...] = jnp.zeros_like(small)
    lab_own[0:1, :] = last
    lab_own[1:2, :] = first
    same_doc = jnp.where(
        (doc_row == doc_col)
        & (lax.broadcasted_iota(jnp.int32, (DH, DH), 1) <= lax.broadcasted_iota(jnp.int32, (DH, DH), 0)),
        1.0,
        0.0,
    ).astype(F32)
    tail = jnp.where(doc_col == last, 1.0, 0.0).astype(BF)
    head_rows = jnp.where(doc_col == first, 1.0, 0.0).astype(F32)

    in_half = heads // nc
    chunk = in_half * DH
    order = [(half, i) for half in range(nc) for i in range(in_half)]
    row_idx = lax.broadcasted_iota(jnp.int32, (DH, DH), 0)
    col_idx = lax.broadcasted_iota(jnp.int32, (DH, DH), 1)

    def cols_of(half, i):
        start = (half * in_half + i) * DH
        return pl.ds(start if isinstance(start, int) else pl.multiple_of(start, DH), DH)

    loads[1].wait()
    loads[2].wait()
    def gram(half):
        for i in range(in_half):
            cols = cols_of(half, i)
            kh, vh = k[:, cols], v[:, cols]
            t_own[half, i] = tn(jnp.concatenate([kh * tail, vh * tail], axis=1), kh).astype(BF)

    gram(other)
    loads[3].wait()
    pl.semaphore_wait(barrier, len(peers))

    def combine(own, from_mate, packed, row, leads):
        joined = jnp.where(lab_own[row : row + 1, :] == lab_mate[row : row + 1, :], 1.0, 0.0)
        own_part = jnp.where(leads, joined, 1.0)
        mate_part = jnp.where(leads, 1.0, joined)
        one, two = [own[c, i].astype(F32) * own_part + from_mate[i].astype(F32) * mate_part for i in range(in_half)]
        mixed = jnp.where(col_idx >= row_idx, one[:DH], two[:DH])
        packed[...] = jnp.concatenate([mixed, one[DH:], two[DH:]], axis=0).astype(BF).reshape(nz, rows, DH)
        return jnp.sum(jnp.where(col_idx == row_idx, two[:DH], 0.0), axis=0, keepdims=True)

    def unpack(packed, diagonal):
        whole = packed[...].reshape(3 * DH, DH).astype(F32)
        mixed = whole[:DH]
        turned = mixed.T
        one = jnp.where(col_idx >= row_idx, mixed, turned)
        two = jnp.where(col_idx < row_idx, mixed, jnp.where(col_idx == row_idx, diagonal, turned))
        return jnp.concatenate([one, whole[DH : 2 * DH]], axis=0), jnp.concatenate([two, whole[2 * DH :]], axis=0)

    def line_total(parts, diagonals, line, row, reverse):
        total, diagonal, before = jnp.zeros((rows, DH), F32), jnp.zeros((1, DH), F32), None
        for i in reversed(range(nz)) if reverse else range(nz):
            label = lab[i, row : row + 1, :]
            if before is not None:
                total = jnp.where(label == before, total, 0.0)
                diagonal = jnp.where(label == before, diagonal, 0.0)
            total = total + parts[i].astype(F32)
            diagonal = diagonal + diagonals[i, 2:3, :]
            before = label
        line[...] = total.astype(BF)
        return diagonal

    def incoming(lines, diagonals, row, reverse):
        total, diagonal = jnp.zeros((rows, DH), F32), jnp.zeros((1, DH), F32)
        before = jnp.full((1, DH), -1.0, F32)
        for i in reversed(range(ny)) if reverse else range(ny):
            label = edge[i, row : row + 1, :]
            grown = jnp.where(label == before, total, 0.0) + lines[i].astype(F32)
            grown_diagonal = jnp.where(label == before, diagonal, 0.0) + diagonals[i, 2:3, :]
            reached = i > y if reverse else i < y
            total = jnp.where(reached, grown, total)
            diagonal = jnp.where(reached, grown_diagonal, diagonal)
            before = jnp.where(reached, label, before)
        return total, diagonal, before

    def scan(parts, diagonals, start, out, row, reverse):
        total, diagonal, before = start
        chip_diagonal, chip_before = diagonal, before
        for i in reversed(range(nz)) if reverse else range(nz):
            label = lab[i, row : row + 1, :]
            out[i] = total.astype(BF)
            chip_before = jnp.where(i == z, before, chip_before)
            chip_diagonal = jnp.where(i == z, diagonal, chip_diagonal)
            total = jnp.where(label == before, total, 0.0) + parts[i].astype(F32)
            diagonal = jnp.where(label == before, diagonal, 0.0) + diagonals[i, 2:3, :]
            before = label
        return chip_diagonal, chip_before

    def spread(own, from_mate, packed, chip_diagonal, to_mate, whole, row, chip_before, leads):
        lead_label = jnp.where(leads, lab_own[row : row + 1, :], lab_mate[row : row + 1, :])
        joined = jnp.where(lead_label == chip_before, 1.0, 0.0)
        for i, ahead in enumerate(unpack(packed, chip_diagonal)):
            lead_state = jnp.where(leads, own[c, i].astype(F32), from_mate[i].astype(F32))
            trail = lead_state + joined * ahead
            whole[c, i] = jnp.where(leads, ahead, trail).astype(BF)
            to_mate[i] = jnp.where(leads, trail, ahead).astype(BF)
        return jnp.where(leads, chip_before, lead_label)

    leads, leads_back = c == 0, c == nc - 1

    send("lab_mate", lab_own, lab_mate, mate)
    send("t_mate", t_own.at[other], t_mate, mate)
    for hh in x_peers:
        send("cot", cot.at[mh], cot.at[mh], me, hh)
    gram(c)

    settle("lab_mate", lab_mate)
    lab_chip[0:1, :] = jnp.where(leads, lab_mate[0:1, :], lab_own[0:1, :])
    lab_chip[1:2, :] = jnp.where(leads, lab_own[1:2, :], lab_mate[1:2, :])
    settle("t_mate", t_mate)
    lab_chip[2:3, :] = combine(t_own, t_mate, t_send, 0, leads)
    lab[z] = lab_chip[...]
    for zz in z_peers:
        send("lab", lab_chip, lab.at[z], at(y, zz, c))
        send("t", t_send.at[zz], t_recv.at[z], at(y, zz, c))
    t_recv[z] = t_send[z]

    settle("lab", lab, nz - 1)
    settle("t", t_recv, nz - 1)
    edge_own[0:1, :] = lab[nz - 1, 0:1, :]
    edge_own[1:2, :] = lab[0, 1:2, :]
    edge_own[2:3, :] = line_total(t_recv, lab, t_line, 0, False)
    edge[y] = edge_own[...]
    for yy in y_peers:
        send("edge", edge_own, edge.at[y], at(yy, z, c))
        send("t_line", t_line, t_lines.at[y], at(yy, z, c))
    t_lines[y] = t_line[...]
    settle("edge", edge, ny - 1)
    settle("t_line", t_lines, ny - 1)
    chip_diagonal, chip_before = scan(t_recv, lab, incoming(t_lines, edge, 0, False), p_send, 0, False)
    for zz in z_peers:
        send("p", p_send.at[zz], p_recv.at[z], at(y, zz, c))
    p_recv[z] = p_send[z]

    loads[4].wait()
    settle("cot", cot, nx - 1)
    for yy in y_peers:
        send("cot_y", cot.at[yy], cot_y.at[y], at(yy, z, c))
    cot_y[y] = cot[y]
    do = nt(cot[0], w[:, 0:width])
    for b in range(1, nx):
        do = do + nt(cot[b], w[:, b * width : (b + 1) * width])
    do_all[...] = do

    do_high, score_two = [], []
    for h, (half, i) in enumerate(order):
        cols = cols_of(half, i)
        kh, vh = k[:, cols], v[:, cols]
        high, low = halves(do[:, h * DH : (h + 1) * DH])
        two = twice(nt, high, low, vh) * same_doc
        do_high.append(high)
        score_two.append(two)
        target_own[:, cols] = twice(nn, *halves(two), kh)
    loads[5].wait()
    loads[6].wait()

    settle("p", p_recv, nz - 1)
    label_in = spread(t_own, t_mate, p_recv, chip_diagonal, p_mate, p_all, 0, chip_before, leads)
    send("p_mate", p_mate, p_all.at[c], mate)
    carried = jnp.where(doc_col == label_in, 1.0, 0.0).astype(F32)
    carried_two = jnp.concatenate([carried, carried], axis=0).astype(BF)
    same_two = jnp.concatenate([same_doc, same_doc], axis=0)

    def solve():
        slots = range(heads)
        cols = [cols_of(*order[i]) for i in slots]
        keys, x, r, p, rr = [], [], [], [], []
        for i in slots:
            state = p_all[order[i]]
            value_in = state[DH:]
            target = carried * twice(nn, *halves(do_all[:, cols[i]]), value_in) + target_own[:, cols[i]]
            b = jnp.concatenate([q[:, cols[i]].astype(F32), target], axis=0)
            kh = k[:, cols[i]]
            keys.append(jnp.concatenate([kh, state[:DH]], axis=0))
            x.append(jnp.zeros_like(b))
            r.append(b)
            p.append(b)
            rr.append(jnp.sum(b * b, axis=1, keepdims=True))
        for number in range(CG_STEPS):
            high = [p[i].astype(BF) for i in slots]
            scores = [nt(high[i], k[:, cols[i]]) * same_two for i in slots]
            applied = [
                nn(jnp.concatenate([scores[i].astype(BF), high[i] * carried_two], axis=1), keys[i])
                + ridge[0, i] * p[i]
                for i in slots
            ]
            step = [rr[i] / (jnp.sum(p[i] * applied[i], axis=1, keepdims=True) + EPS) for i in slots]
            for i in slots:
                x[i] = x[i] + step[i] * p[i]
            if number < CG_STEPS - 1:
                for i in slots:
                    r[i] = r[i] - step[i] * applied[i]
                fresh = [jnp.sum(r[i] * r[i], axis=1, keepdims=True) for i in slots]
                for i in slots:
                    p[i] = r[i] + fresh[i] / (rr[i] + EPS) * p[i]
                rr = fresh
        for i in slots:
            x_all[i] = x[i]

    settle("p_mate", p_mate)
    solve()

    for h, (half, i) in enumerate(order):
        x_h = x_all[h]
        rows_x = (head_rows * x_h[:DH]).astype(BF)
        both = tn(jnp.concatenate([do_high[h], x_h[DH:].astype(BF)], axis=1), rows_x)
        cross = both[DH:]
        b_own[half, i] = jnp.concatenate([cross + cross.T, both[:DH]], axis=0).astype(BF)
    send("b_mate", b_own.at[other], b_mate, mate)

    x_high, score_x = [], []
    for h, (half, i) in enumerate(order):
        cols = cols_of(half, i)
        kh, vh = k[:, cols], v[:, cols]
        value_in = p_all[half, i, DH:, :]
        high, low = halves(x_all[h])
        x_high.append(high)
        scores = twice(nt, high, low, kh) * same_two
        score_x.append(scores)
        out = twice(nn, *halves(scores[:DH]), vh) + carried * twice(nt, high[:DH], low[:DH], value_in)
        group = h // in_half
        mix[group, y, :, i * DH : (i + 1) * DH] = out.astype(BF)
        if i == in_half - 1:
            for yy in y_peers:
                send(f"mix{group}", mix.at[group, y], mix.at[group, y], at(yy, z, c))

    settle("b_mate", b_mate)
    note_chip[2:3, :] = combine(b_own, b_mate, b_send, 1, leads_back)
    note[z] = note_chip[...]
    for zz in z_peers:
        send("note", note_chip, note.at[z], at(y, zz, c))
        send("b", b_send.at[zz], b_recv.at[z], at(y, zz, c))
    b_recv[z] = b_send[z]

    for h, (half, i) in enumerate(order):
        gq[:, cols_of(half, i)] = x_high[h][DH:]
    mixed = jnp.concatenate([mix[group, y] for group in range(nc)], axis=1)

    def project(block):
        cols = pl.ds(pl.multiple_of(block * width, width), width)
        return nn(mixed, w[:, cols])

    for i, hh in enumerate(x_peers):
        l_send[i] = project(hh).astype(BF)
        send("l", l_send.at[i], l_recv.at[mh], me, hh)
    l_own[...] = project(mh)
    l_recv[mh] = jnp.zeros((DH, width), BF)

    for h, (half, i) in enumerate(order):
        cols = cols_of(half, i)
        one = score_x[h][:DH].astype(BF)
        rest = (score_two[h] - score_x[h][DH:]).astype(BF)
        gv[:, cols] = tn(one, do_high[h])
        gk[:, cols] = tn(rest, x_high[h][:DH]) - tn(one, x_high[h][DH:])

    settle("cot_y", cot_y, ny - 1)
    for b in range(ny):
        turned = cot_y[b].T
        for zz in range(nz):
            for cc in range(nc):
                cut = (zz * nc + cc) * strip
                cot_t[cc, zz * strip : (zz + 1) * strip, b * DH : (b + 1) * DH] = turned[cut : cut + strip, :]

    def product(group):
        settle(f"mix{group}", mix.at[group], ny - 1)
        gathered = mix[group].reshape(ny * DH, chunk)
        gw_send[group] = nn(cot_t[other], gathered).astype(BF).reshape(nz, strip, chunk)
        send(f"gw{group}", gw_send.at[group], gw_recv.at[group], mate)
        gw_own[group] = nn(cot_t[c], gathered).reshape(nz, strip, chunk)

    distances = [i if i <= nz // 2 else i - nz for i in range(1, nz)]
    near = [d for d in (1, -1, 2, -2) if d in distances]
    far = [d for d in distances if abs(d) > 2]
    side = jnp.where(leads, 2, -2)
    two_away = [d for d in near if abs(d) == 2]

    def chip(distance):
        return lax.rem(z + distance + nz, nz)

    def along_z(group):
        settle(f"gw{group}", gw_recv.at[group])
        z_send[group] = (gw_own[group] + gw_recv[group].astype(F32)).astype(BF)
        for slot, d in enumerate(far):
            via = side if abs(d) == 4 else d // 3
            send(f"far{group}", z_send.at[group, chip(d)], z_far.at[group, slot], at(y, chip(via), c))
        for slot, d in enumerate(near):
            if d not in two_away:
                send(f"z{group}", z_send.at[group, chip(d)], z_recv.at[group, slot], at(y, chip(d), c))

    def along_z_again(group):
        if not two_away:
            return
        settle(f"far{group}", z_far.at[group])
        for d in two_away:
            total = z_send[group, chip(d)].astype(F32)
            for slot, e in enumerate(far):
                if abs(e) == 4:
                    total = total + jnp.where(side == d, z_far[group, slot].astype(F32), 0.0)
                elif e * d > 0:
                    total = total + z_far[group, slot].astype(F32)
            z_add[group, two_away.index(d)] = total.astype(BF)
            slot = near.index(d)
            send(f"z{group}", z_add.at[group, two_away.index(d)], z_recv.at[group, slot], at(y, chip(d), c))

    product(0)
    settle("note", note, nz - 1)
    settle("b", b_recv, nz - 1)
    rim_own[2:3, :] = line_total(b_recv, note, b_line, 1, True)
    rim[y] = rim_own[...]
    for yy in y_peers:
        send("rim", rim_own, rim.at[y], at(yy, z, c))
        send("b_line", b_line, b_lines.at[y], at(yy, z, c))
    b_lines[y] = b_line[...]
    along_z(0)
    product(1)
    along_z(1)
    settle("rim", rim, ny - 1)
    settle("b_line", b_lines, ny - 1)
    chip_diagonal, chip_before = scan(b_recv, note, incoming(b_lines, rim, 1, True), r_send, 1, True)
    for zz in z_peers:
        send("r", r_send.at[zz], r_recv.at[z], at(y, zz, c))
    r_recv[z] = r_send[z]

    along_z_again(0)
    settle("l", l_recv, nx - 1)
    total = l_own[...]
    for b in range(nx):
        total = total + l_recv[b].astype(F32)
    lay[...] = total.astype(BF)
    along_z_again(1)

    settle("r", r_recv, nz - 1)
    label_next = spread(b_own, b_mate, r_recv, chip_diagonal, r_mate, r_all, 1, chip_before, leads_back)
    send("r_mate", r_mate, r_all.at[c], mate)
    later = jnp.where(doc_col == label_next, 1.0, 0.0).astype(F32)

    def finish(half):
        for i in range(in_half):
            cols = cols_of(half, i)
            kh, vh = k[:, cols], v[:, cols]
            state = r_all[half, i]
            gram_grad, grad_state = state[:DH], state[DH:]
            gv_out[:, cols] = (gv[:, cols] + later * nt(kh, grad_state)).astype(BF)
            gk_out[:, cols] = (gk[:, cols] + later * (nn(vh, grad_state) - nn(kh, gram_grad))).astype(BF)

    finish(c)
    settle("r_mate", r_mate)
    finish(other)

    for group in range(nc):
        settle(f"z{group}", z_recv.at[group])
        total = z_send[group, z].astype(F32)
        for slot in range(len(near)):
            total = total + z_recv[group, slot].astype(F32)
        gw[:, group * chunk : (group + 1) * chunk] = total

    for name, ref in sent:
        pltpu.make_async_copy(ref, ref, send_sem.at[sems[name]]).wait()


def move(*refs):
    count = (len(refs) - 1) // 2
    ins, outs, sem = refs[:count], refs[count : 2 * count], refs[-1]
    writes = [pltpu.make_async_copy(a, b, sem.at[i]) for i, (a, b) in enumerate(zip(ins, outs))]
    for write in writes:
        write.start()
    for write in writes:
        write.wait()


def per_device(dims, nx, query_rows, key_rows, value_rows, ridge_reg, out_weight, out_grad, doc_ids):
    ny, nz, nc = dims
    heads = ridge_reg.shape[0]
    width = heads * DH
    rows = 3 * DH // nz
    strip = width // (nz * nc)
    any_space = pl.BlockSpec(memory_space=pl.ANY)
    packed = pltpu.VMEM((nz, rows, DH), BF)
    half = pltpu.VMEM((heads // nc, 2 * DH, DH), BF)
    both = pltpu.VMEM((nc, heads // nc, 2 * DH, DH), BF)
    line = pltpu.VMEM((rows, DH), BF)
    lines = pltpu.VMEM((ny, rows, DH), BF)
    label = pltpu.VMEM((4, DH), F32)
    wide = pltpu.VMEM((DH, width), BF)
    held = (wide, wide, wide, wide, pltpu.VMEM((strip, width), F32))
    states = [both, half, packed, packed, line, lines, packed, packed, half, both]
    made = pl.pallas_call(
        functools.partial(kernel, dims, nx),
        out_shape=held,
        in_specs=[any_space] * 7,
        out_specs=(pl.BlockSpec(memory_space=pltpu.VMEM),) * 5,
        scratch_shapes=[
            pltpu.SMEM((1, heads), F32),
            wide,
            wide,
            wide,
            pltpu.VMEM((width, nx * width), BF),
            pltpu.VMEM((1, DH), jnp.int32),
            label,
            label,
            label,
            pltpu.VMEM((nz, 4, DH), F32),
            label,
            pltpu.VMEM((ny, 4, DH), F32),
            label,
            pltpu.VMEM((nz, 4, DH), F32),
            label,
            pltpu.VMEM((ny, 4, DH), F32),
            *states,
            *states,
            pltpu.VMEM((nx, DH, width), BF),
            pltpu.VMEM((ny, DH, width), BF),
            pltpu.VMEM((nc, nz * strip, ny * DH), BF),
            pltpu.VMEM((DH, width), F32),
            pltpu.VMEM((DH, width), F32),
            pltpu.VMEM((heads, 2 * DH, DH), F32),
            pltpu.VMEM((nc, ny, DH, width // nc), BF),
            pltpu.VMEM((nx, DH, width), BF),
            pltpu.VMEM((nx, DH, width), BF),
            pltpu.VMEM((DH, width), F32),
            pltpu.VMEM((nc, nz, strip, width // nc), F32),
            *[pltpu.VMEM((nc, nz, strip, width // nc), BF)] * 3,
            pltpu.VMEM((nc, 3, strip, width // nc), BF),
            pltpu.VMEM((nc, 2, strip, width // nc), BF),
            pltpu.VMEM((nc, min(4, nz - 1), strip, width // nc), BF),
            pltpu.VMEM((DH, width), F32),
            pltpu.VMEM((DH, width), F32),
            pltpu.SemaphoreType.DMA((7,)),
            pltpu.SemaphoreType.DMA((26,)),
            pltpu.SemaphoreType.DMA((26,)),
        ],
        compiler_params=pltpu.CompilerParams(collective_id=0, has_side_effects=True),
    )(ridge_reg.reshape(1, -1), query_rows, key_rows, value_rows, out_weight, out_grad, doc_ids.reshape(1, -1))
    return pl.pallas_call(
        move,
        out_shape=[jax.ShapeDtypeStruct(a.shape, a.dtype) for a in made],
        in_specs=[pl.BlockSpec(memory_space=pltpu.VMEM)] * 5,
        out_specs=[any_space] * 5,
        scratch_shapes=[pltpu.SemaphoreType.DMA((5,))],
    )(*[pltpu.with_memory_space_constraint(a, pltpu.VMEM) for a in made])


def build(mesh, dims):
    nx = mesh.shape["head"]
    spec = P("seq", "head")
    return jax.shard_map(
        functools.partial(per_device, dims, nx),
        mesh=mesh,
        in_specs=(spec, spec, spec, P("head"), P("head", None), spec, P("seq")),
        out_specs=(spec,) * 5,
        check_vma=False,
    )


def solution(mesh):
    return build(mesh, SEQ_DIMS)
```

```python
import functools

import jax
import jax.numpy as jnp
from jax import lax
from jax.experimental import pallas as pl
from jax.experimental.pallas import tpu as pltpu
from jax.sharding import PartitionSpec as P

CG_STEPS = 4
EPS = 1e-6
DH = 128
F32 = jnp.float32
BF = jnp.bfloat16
MESH = pl.DeviceIdType.MESH

SEQ_DIMS = (4, 8, 2)


def nn(a, b):
    return lax.dot_general(a, b, (((1,), (0,)), ((), ())), preferred_element_type=F32)


def nt(a, b):
    return lax.dot_general(a, b, (((1,), (1,)), ((), ())), preferred_element_type=F32)


def tn(a, b):
    return lax.dot_general(a, b, (((0,), (0,)), ((), ())), preferred_element_type=F32)


def halves(a):
    high = a.astype(BF)
    return high, (a - high.astype(F32)).astype(BF)


def twice(product, high, low, right):
    axis = 1 if product is nt else 0
    return product(jnp.concatenate([high, low], axis=1), jnp.concatenate([right, right], axis=axis))


def kernel(
    dims, nx,
    ridge_in, q_in, k_in, v_in, w_in, og_in, doc_in,
    lay, gq, gk_out, gv_out, gw,
    ridge,
    q, k, v, w, doc, lab_own, lab_mate, lab_chip, lab, edge_own, edge, note_chip, note, rim_own, rim,
    t_own, t_mate, t_send, t_recv, t_line, t_lines, p_send, p_recv, p_mate, p_all,
    b_own, b_mate, b_send, b_recv, b_line, b_lines, r_send, r_recv, r_mate, r_all,
    cot, cot_y, cot_t, do_all, target_own, x_all, mix, l_send, l_recv, l_own,
    gw_own, gw_send, gw_recv, z_send, z_far, z_add, z_recv,
    gk, gv,
    load_sem, send_sem, recv_sem,
):
    ny, nz, nc = dims
    heads = ridge.shape[1]
    width = heads * DH
    me, mh = lax.axis_index("seq"), lax.axis_index("head")
    c = lax.rem(me, nc)
    z = lax.rem(me // nc, nz)
    y = me // (nc * nz)
    other = nc - 1 - c
    rows = t_line.shape[0]
    strip = gw.shape[0]

    def at(yy, zz, cc):
        return (yy * nz + zz) * nc + cc

    mate = at(y, z, other)
    y_peers = [lax.rem(y + i, ny) for i in sorted(range(1, ny), key=lambda i: -min(i, ny - i))]
    z_peers = [lax.rem(z + i, nz) for i in sorted(range(1, nz), key=lambda i: -min(i, nz - i))]
    x_peers = [lax.rem(mh + i, nx) for i in range(1, nx)]

    names = ("lab_mate", "lab", "edge", "t_mate", "t", "t_line", "p", "p_mate", "b_mate", "b", "b_line", "note", "rim",
             "r", "r_mate", "cot", "cot_y", "l", "mix0", "mix1", "gw0", "gw1", "far0", "far1", "z0", "z1")
    sems = {name: i for i, name in enumerate(names)}
    sent = []

    def send(name, src, dst, seq, head=None):
        copy = pltpu.make_async_remote_copy(
            src_ref=src, dst_ref=dst,
            send_sem=send_sem.at[sems[name]], recv_sem=recv_sem.at[sems[name]],
            device_id=(seq, mh if head is None else head), device_id_type=MESH,
        )
        copy.start()

    def settle(name, ref, count=None):
        if count == 0:
            return
        ref = ref if count is None else ref.at[pl.ds(0, count)]
        sent.append((name, ref))
        pltpu.make_async_copy(ref, ref, recv_sem.at[sems[name]]).wait()

    loads = [
        pltpu.make_async_copy(src, dst, load_sem.at[i])
        for i, (src, dst) in enumerate(
            ((doc_in, doc), (k_in, k), (v_in, v), (og_in, cot.at[mh]), (w_in, w), (q_in, q), (ridge_in, ridge))
        )
    ]
    for load in loads:
        load.start()

    barrier = pltpu.get_barrier_semaphore()
    peers = [(at(y, zz, c), mh) for zz in z_peers] + [(at(yy, z, c), mh) for yy in y_peers]
    peers += [(me, hh) for hh in x_peers] + [(mate, mh)]
    for peer in peers:
        pl.semaphore_signal(barrier, inc=1, device_id=peer, device_id_type=MESH)

    loads[0].wait()
    doc_row = jnp.broadcast_to(doc[...].astype(F32), (DH, DH))
    doc_col = doc_row.T
    last, first = doc_col[DH - 1 : DH, :], doc_col[0:1, :]
    for small in (lab_own, lab_chip, edge_own, note_chip, rim_own):
        small[...] = jnp.zeros_like(small)
    lab_own[0:1, :] = last
    lab_own[1:2, :] = first
    same_doc = jnp.where(
        (doc_row == doc_col)
        & (lax.broadcasted_iota(jnp.int32, (DH, DH), 1) <= lax.broadcasted_iota(jnp.int32, (DH, DH), 0)),
        1.0,
        0.0,
    ).astype(F32)
    tail = jnp.where(doc_col == last, 1.0, 0.0).astype(BF)
    head_rows = jnp.where(doc_col == first, 1.0, 0.0).astype(F32)

    in_half = heads // nc
    chunk = in_half * DH
    order = [(half, i) for half in range(nc) for i in range(in_half)]
    row_idx = lax.broadcasted_iota(jnp.int32, (DH, DH), 0)
    col_idx = lax.broadcasted_iota(jnp.int32, (DH, DH), 1)

    def cols_of(half, i):
        start = (half * in_half + i) * DH
        return pl.ds(start if isinstance(start, int) else pl.multiple_of(start, DH), DH)

    loads[1].wait()
    loads[2].wait()
    def gram(half):
        for i in range(in_half):
            cols = cols_of(half, i)
            kh, vh = k[:, cols], v[:, cols]
            t_own[half, i] = tn(jnp.concatenate([kh * tail, vh * tail], axis=1), kh).astype(BF)

    gram(other)
    loads[3].wait()
    pl.semaphore_wait(barrier, len(peers))

    def combine(own, from_mate, packed, row, leads):
        joined = jnp.where(lab_own[row : row + 1, :] == lab_mate[row : row + 1, :], 1.0, 0.0)
        own_part = jnp.where(leads, joined, 1.0)
        mate_part = jnp.where(leads, 1.0, joined)
        one, two = [own[c, i].astype(F32) * own_part + from_mate[i].astype(F32) * mate_part for i in range(in_half)]
        mixed = jnp.where(col_idx >= row_idx, one[:DH], two[:DH])
        packed[...] = jnp.concatenate([mixed, one[DH:], two[DH:]], axis=0).astype(BF).reshape(nz, rows, DH)
        return jnp.sum(jnp.where(col_idx == row_idx, two[:DH], 0.0), axis=0, keepdims=True)

    def unpack(packed, diagonal):
        whole = packed[...].reshape(3 * DH, DH).astype(F32)
        mixed = whole[:DH]
        turned = mixed.T
        one = jnp.where(col_idx >= row_idx, mixed, turned)
        two = jnp.where(col_idx < row_idx, mixed, jnp.where(col_idx == row_idx, diagonal, turned))
        return jnp.concatenate([one, whole[DH : 2 * DH]], axis=0), jnp.concatenate([two, whole[2 * DH :]], axis=0)

    def line_total(parts, diagonals, line, row, reverse):
        total, diagonal, before = jnp.zeros((rows, DH), F32), jnp.zeros((1, DH), F32), None
        for i in reversed(range(nz)) if reverse else range(nz):
            label = lab[i, row : row + 1, :]
            if before is not None:
                total = jnp.where(label == before, total, 0.0)
                diagonal = jnp.where(label == before, diagonal, 0.0)
            total = total + parts[i].astype(F32)
            diagonal = diagonal + diagonals[i, 2:3, :]
            before = label
        line[...] = total.astype(BF)
        return diagonal

    def incoming(lines, diagonals, row, reverse):
        total, diagonal = jnp.zeros((rows, DH), F32), jnp.zeros((1, DH), F32)
        before = jnp.full((1, DH), -1.0, F32)
        for i in reversed(range(ny)) if reverse else range(ny):
            label = edge[i, row : row + 1, :]
            grown = jnp.where(label == before, total, 0.0) + lines[i].astype(F32)
            grown_diagonal = jnp.where(label == before, diagonal, 0.0) + diagonals[i, 2:3, :]
            reached = i > y if reverse else i < y
            total = jnp.where(reached, grown, total)
            diagonal = jnp.where(reached, grown_diagonal, diagonal)
            before = jnp.where(reached, label, before)
        return total, diagonal, before

    def scan(parts, diagonals, start, out, row, reverse):
        total, diagonal, before = start
        chip_diagonal, chip_before = diagonal, before
        for i in reversed(range(nz)) if reverse else range(nz):
            label = lab[i, row : row + 1, :]
            out[i] = total.astype(BF)
            chip_before = jnp.where(i == z, before, chip_before)
            chip_diagonal = jnp.where(i == z, diagonal, chip_diagonal)
            total = jnp.where(label == before, total, 0.0) + parts[i].astype(F32)
            diagonal = jnp.where(label == before, diagonal, 0.0) + diagonals[i, 2:3, :]
            before = label
        return chip_diagonal, chip_before

    def spread(own, from_mate, packed, chip_diagonal, to_mate, whole, row, chip_before, leads):
        lead_label = jnp.where(leads, lab_own[row : row + 1, :], lab_mate[row : row + 1, :])
        joined = jnp.where(lead_label == chip_before, 1.0, 0.0)
        for i, ahead in enumerate(unpack(packed, chip_diagonal)):
            lead_state = jnp.where(leads, own[c, i].astype(F32), from_mate[i].astype(F32))
            trail = lead_state + joined * ahead
            whole[c, i] = jnp.where(leads, ahead, trail).astype(BF)
            to_mate[i] = jnp.where(leads, trail, ahead).astype(BF)
        return jnp.where(leads, chip_before, lead_label)

    leads, leads_back = c == 0, c == nc - 1

    send("lab_mate", lab_own, lab_mate, mate)
    send("t_mate", t_own.at[other], t_mate, mate)
    for hh in x_peers:
        send("cot", cot.at[mh], cot.at[mh], me, hh)
    gram(c)

    settle("lab_mate", lab_mate)
    lab_chip[0:1, :] = jnp.where(leads, lab_mate[0:1, :], lab_own[0:1, :])
    lab_chip[1:2, :] = jnp.where(leads, lab_own[1:2, :], lab_mate[1:2, :])
    settle("t_mate", t_mate)
    lab_chip[2:3, :] = combine(t_own, t_mate, t_send, 0, leads)
    lab[z] = lab_chip[...]
    for zz in z_peers:
        send("lab", lab_chip, lab.at[z], at(y, zz, c))
        send("t", t_send.at[zz], t_recv.at[z], at(y, zz, c))
    t_recv[z] = t_send[z]

    settle("lab", lab, nz - 1)
    settle("t", t_recv, nz - 1)
    edge_own[0:1, :] = lab[nz - 1, 0:1, :]
    edge_own[1:2, :] = lab[0, 1:2, :]
    edge_own[2:3, :] = line_total(t_recv, lab, t_line, 0, False)
    edge[y] = edge_own[...]
    for yy in y_peers:
        send("edge", edge_own, edge.at[y], at(yy, z, c))
        send("t_line", t_line, t_lines.at[y], at(yy, z, c))
    t_lines[y] = t_line[...]
    settle("edge", edge, ny - 1)
    settle("t_line", t_lines, ny - 1)
    chip_diagonal, chip_before = scan(t_recv, lab, incoming(t_lines, edge, 0, False), p_send, 0, False)
    for zz in z_peers:
        send("p", p_send.at[zz], p_recv.at[z], at(y, zz, c))
    p_recv[z] = p_send[z]

    loads[4].wait()
    settle("cot", cot, nx - 1)
    for yy in y_peers:
        send("cot_y", cot.at[yy], cot_y.at[y], at(yy, z, c))
    cot_y[y] = cot[y]
    do = nt(cot[0], w[:, 0:width])
    for b in range(1, nx):
        do = do + nt(cot[b], w[:, b * width : (b + 1) * width])
    do_all[...] = do

    do_high, score_two = [], []
    for h, (half, i) in enumerate(order):
        cols = cols_of(half, i)
        kh, vh = k[:, cols], v[:, cols]
        high, low = halves(do[:, h * DH : (h + 1) * DH])
        two = twice(nt, high, low, vh) * same_doc
        do_high.append(high)
        score_two.append(two)
        target_own[:, cols] = twice(nn, *halves(two), kh)
    loads[5].wait()
    loads[6].wait()

    settle("p", p_recv, nz - 1)
    label_in = spread(t_own, t_mate, p_recv, chip_diagonal, p_mate, p_all, 0, chip_before, leads)
    send("p_mate", p_mate, p_all.at[c], mate)
    carried = jnp.where(doc_col == label_in, 1.0, 0.0).astype(F32)
    carried_two = jnp.concatenate([carried, carried], axis=0).astype(BF)
    same_two = jnp.concatenate([same_doc, same_doc], axis=0)

    def solve():
        slots = range(heads)
        cols = [cols_of(*order[i]) for i in slots]
        keys, x, r, p, rr = [], [], [], [], []
        for i in slots:
            state = p_all[order[i]]
            value_in = state[DH:]
            target = carried * twice(nn, *halves(do_all[:, cols[i]]), value_in) + target_own[:, cols[i]]
            b = jnp.concatenate([q[:, cols[i]].astype(F32), target], axis=0)
            kh = k[:, cols[i]]
            keys.append(jnp.concatenate([kh, state[:DH]], axis=0))
            x.append(jnp.zeros_like(b))
            r.append(b)
            p.append(b)
            rr.append(jnp.sum(b * b, axis=1, keepdims=True))
        for number in range(CG_STEPS):
            high = [p[i].astype(BF) for i in slots]
            scores = [nt(high[i], k[:, cols[i]]) * same_two for i in slots]
            applied = [
                nn(jnp.concatenate([scores[i].astype(BF), high[i] * carried_two], axis=1), keys[i])
                + ridge[0, i] * p[i]
                for i in slots
            ]
            step = [rr[i] / (jnp.sum(p[i] * applied[i], axis=1, keepdims=True) + EPS) for i in slots]
            for i in slots:
                x[i] = x[i] + step[i] * p[i]
            if number < CG_STEPS - 1:
                for i in slots:
                    r[i] = r[i] - step[i] * applied[i]
                fresh = [jnp.sum(r[i] * r[i], axis=1, keepdims=True) for i in slots]
                for i in slots:
                    p[i] = r[i] + fresh[i] / (rr[i] + EPS) * p[i]
                rr = fresh
        for i in slots:
            x_all[i] = x[i]

    settle("p_mate", p_mate)
    solve()

    for h, (half, i) in enumerate(order):
        x_h = x_all[h]
        rows_x = (head_rows * x_h[:DH]).astype(BF)
        both = tn(jnp.concatenate([do_high[h], x_h[DH:].astype(BF)], axis=1), rows_x)
        cross = both[DH:]
        b_own[half, i] = jnp.concatenate([cross + cross.T, both[:DH]], axis=0).astype(BF)
    send("b_mate", b_own.at[other], b_mate, mate)

    x_high, score_x = [], []

    def read_out(group):
        for i in range(in_half):
            h = group * in_half + i
            cols = slice(h * DH, (h + 1) * DH)
            kh, vh = k[:, cols], v[:, cols]
            value_in = p_all[group, i, DH:, :]
            high, low = halves(x_all[h])
            x_high.append(high)
            scores = twice(nt, high, low, kh) * same_two
            score_x.append(scores)
            out = twice(nn, *halves(scores[:DH]), vh) + carried * twice(nt, high[:DH], low[:DH], value_in)
            mix[group, y, :, i * DH : (i + 1) * DH] = out.astype(BF)
        for yy in y_peers:
            send(f"mix{group}", mix.at[group, y], mix.at[group, y], at(yy, z, c))

    read_out(0)
    settle("b_mate", b_mate)
    note_chip[2:3, :] = combine(b_own, b_mate, b_send, 1, leads_back)
    note[z] = note_chip[...]
    for zz in z_peers:
        send("note", note_chip, note.at[z], at(y, zz, c))
        send("b", b_send.at[zz], b_recv.at[z], at(y, zz, c))
    b_recv[z] = b_send[z]

    read_out(1)

    for h, (half, i) in enumerate(order):
        gq[:, cols_of(half, i)] = x_high[h][DH:]
    mixed = jnp.concatenate([mix[group, y] for group in range(nc)], axis=1)

    def project(block):
        cols = pl.ds(pl.multiple_of(block * width, width), width)
        return nn(mixed, w[:, cols])

    for i, hh in enumerate(x_peers):
        l_send[i] = project(hh).astype(BF)
        send("l", l_send.at[i], l_recv.at[mh], me, hh)
    l_own[...] = project(mh)
    l_recv[mh] = jnp.zeros((DH, width), BF)

    for h, (half, i) in enumerate(order):
        cols = cols_of(half, i)
        one = score_x[h][:DH].astype(BF)
        rest = (score_two[h] - score_x[h][DH:]).astype(BF)
        gv[:, cols] = tn(one, do_high[h])
        gk[:, cols] = tn(rest, x_high[h][:DH]) - tn(one, x_high[h][DH:])

    settle("cot_y", cot_y, ny - 1)
    for b in range(ny):
        turned = cot_y[b].T
        for zz in range(nz):
            for cc in range(nc):
                cut = (zz * nc + cc) * strip
                cot_t[cc, zz * strip : (zz + 1) * strip, b * DH : (b + 1) * DH] = turned[cut : cut + strip, :]

    def product(group):
        settle(f"mix{group}", mix.at[group], ny - 1)
        gathered = mix[group].reshape(ny * DH, chunk)
        gw_send[group] = nn(cot_t[other], gathered).astype(BF).reshape(nz, strip, chunk)
        send(f"gw{group}", gw_send.at[group], gw_recv.at[group], mate)
        gw_own[group] = nn(cot_t[c], gathered).reshape(nz, strip, chunk)

    distances = [i if i <= nz // 2 else i - nz for i in range(1, nz)]
    near = [d for d in (1, -1, 2, -2) if d in distances]
    far = [d for d in distances if abs(d) > 2]
    two_away = [d for d in near if abs(d) == 2]

    def chip(distance):
        return lax.rem(z + distance + nz, nz)

    def along_z(group):
        settle(f"gw{group}", gw_recv.at[group])
        z_send[group] = (gw_own[group] + gw_recv[group].astype(F32)).astype(BF)
        for slot, d in enumerate(far):
            via = -2 if abs(d) == 4 else d // 3
            send(f"far{group}", z_send.at[group, chip(d)], z_far.at[group, slot], at(y, chip(via), c))
        for slot, d in enumerate(near):
            if d not in two_away:
                send(f"z{group}", z_send.at[group, chip(d)], z_recv.at[group, slot], at(y, chip(d), c))

    def along_z_again(group):
        if not two_away:
            return
        settle(f"far{group}", z_far.at[group])
        for d in two_away:
            total = z_send[group, chip(d)].astype(F32)
            for slot, e in enumerate(far):
                if (d == -2) if abs(e) == 4 else (e * d > 0):
                    total = total + z_far[group, slot].astype(F32)
            z_add[group, two_away.index(d)] = total.astype(BF)
            slot = near.index(d)
            send(f"z{group}", z_add.at[group, two_away.index(d)], z_recv.at[group, slot], at(y, chip(d), c))

    product(0)
    settle("note", note, nz - 1)
    settle("b", b_recv, nz - 1)
    rim_own[2:3, :] = line_total(b_recv, note, b_line, 1, True)
    rim[y] = rim_own[...]
    for yy in y_peers:
        send("rim", rim_own, rim.at[y], at(yy, z, c))
        send("b_line", b_line, b_lines.at[y], at(yy, z, c))
    b_lines[y] = b_line[...]
    along_z(0)
    product(1)
    along_z(1)
    settle("rim", rim, ny - 1)
    settle("b_line", b_lines, ny - 1)
    chip_diagonal, chip_before = scan(b_recv, note, incoming(b_lines, rim, 1, True), r_send, 1, True)
    for zz in z_peers:
        send("r", r_send.at[zz], r_recv.at[z], at(y, zz, c))
    r_recv[z] = r_send[z]

    along_z_again(0)
    settle("l", l_recv, nx - 1)
    total = l_own[...]
    for b in range(nx):
        total = total + l_recv[b].astype(F32)
    lay[...] = total.astype(BF)
    along_z_again(1)

    settle("r", r_recv, nz - 1)
    label_next = spread(b_own, b_mate, r_recv, chip_diagonal, r_mate, r_all, 1, chip_before, leads_back)
    send("r_mate", r_mate, r_all.at[c], mate)
    later = jnp.where(doc_col == label_next, 1.0, 0.0).astype(F32)

    def finish(half):
        for i in range(in_half):
            cols = cols_of(half, i)
            kh, vh = k[:, cols], v[:, cols]
            state = r_all[half, i]
            gram_grad, grad_state = state[:DH], state[DH:]
            gv_out[:, cols] = (gv[:, cols] + later * nt(kh, grad_state)).astype(BF)
            gk_out[:, cols] = (gk[:, cols] + later * (nn(vh, grad_state) - nn(kh, gram_grad))).astype(BF)

    finish(c)
    settle("r_mate", r_mate)
    finish(other)

    for group in range(nc):
        settle(f"z{group}", z_recv.at[group])
        total = z_send[group, z].astype(F32)
        for slot in range(len(near)):
            total = total + z_recv[group, slot].astype(F32)
        gw[:, group * chunk : (group + 1) * chunk] = total

    for name, ref in sent:
        pltpu.make_async_copy(ref, ref, send_sem.at[sems[name]]).wait()


def move(*refs):
    count = (len(refs) - 1) // 2
    ins, outs, sem = refs[:count], refs[count : 2 * count], refs[-1]
    writes = [pltpu.make_async_copy(a, b, sem.at[i]) for i, (a, b) in enumerate(zip(ins, outs))]
    for write in writes:
        write.start()
    for write in writes:
        write.wait()


def per_device(dims, nx, query_rows, key_rows, value_rows, ridge_reg, out_weight, out_grad, doc_ids):
    ny, nz, nc = dims
    heads = ridge_reg.shape[0]
    width = heads * DH
    rows = 3 * DH // nz
    strip = width // (nz * nc)
    any_space = pl.BlockSpec(memory_space=pl.ANY)
    packed = pltpu.VMEM((nz, rows, DH), BF)
    half = pltpu.VMEM((heads // nc, 2 * DH, DH), BF)
    both = pltpu.VMEM((nc, heads // nc, 2 * DH, DH), BF)
    line = pltpu.VMEM((rows, DH), BF)
    lines = pltpu.VMEM((ny, rows, DH), BF)
    label = pltpu.VMEM((4, DH), F32)
    wide = pltpu.VMEM((DH, width), BF)
    held = (wide, wide, wide, wide, pltpu.VMEM((strip, width), F32))
    states = [both, half, packed, packed, line, lines, packed, packed, half, both]
    made = pl.pallas_call(
        functools.partial(kernel, dims, nx),
        out_shape=held,
        in_specs=[any_space] * 7,
        out_specs=(pl.BlockSpec(memory_space=pltpu.VMEM),) * 5,
        scratch_shapes=[
            pltpu.SMEM((1, heads), F32),
            wide,
            wide,
            wide,
            pltpu.VMEM((width, nx * width), BF),
            pltpu.VMEM((1, DH), jnp.int32),
            label,
            label,
            label,
            pltpu.VMEM((nz, 4, DH), F32),
            label,
            pltpu.VMEM((ny, 4, DH), F32),
            label,
            pltpu.VMEM((nz, 4, DH), F32),
            label,
            pltpu.VMEM((ny, 4, DH), F32),
            *states,
            *states,
            pltpu.VMEM((nx, DH, width), BF),
            pltpu.VMEM((ny, DH, width), BF),
            pltpu.VMEM((nc, nz * strip, ny * DH), BF),
            pltpu.VMEM((DH, width), F32),
            pltpu.VMEM((DH, width), F32),
            pltpu.VMEM((heads, 2 * DH, DH), F32),
            pltpu.VMEM((nc, ny, DH, width // nc), BF),
            pltpu.VMEM((nx, DH, width), BF),
            pltpu.VMEM((nx, DH, width), BF),
            pltpu.VMEM((DH, width), F32),
            pltpu.VMEM((nc, nz, strip, width // nc), F32),
            *[pltpu.VMEM((nc, nz, strip, width // nc), BF)] * 3,
            pltpu.VMEM((nc, 3, strip, width // nc), BF),
            pltpu.VMEM((nc, 2, strip, width // nc), BF),
            pltpu.VMEM((nc, min(4, nz - 1), strip, width // nc), BF),
            pltpu.VMEM((DH, width), F32),
            pltpu.VMEM((DH, width), F32),
            pltpu.SemaphoreType.DMA((7,)),
            pltpu.SemaphoreType.DMA((26,)),
            pltpu.SemaphoreType.DMA((26,)),
        ],
        compiler_params=pltpu.CompilerParams(collective_id=0, has_side_effects=True),
    )(ridge_reg.reshape(1, -1), query_rows, key_rows, value_rows, out_weight, out_grad, doc_ids.reshape(1, -1))
    return pl.pallas_call(
        move,
        out_shape=[jax.ShapeDtypeStruct(a.shape, a.dtype) for a in made],
        in_specs=[pl.BlockSpec(memory_space=pltpu.VMEM)] * 5,
        out_specs=[any_space] * 5,
        scratch_shapes=[pltpu.SemaphoreType.DMA((5,))],
    )(*[pltpu.with_memory_space_constraint(a, pltpu.VMEM) for a in made])


def build(mesh, dims):
    nx = mesh.shape["head"]
    spec = P("seq", "head")
    return jax.shard_map(
        functools.partial(per_device, dims, nx),
        mesh=mesh,
        in_specs=(spec, spec, spec, P("head"), P("head", None), spec, P("seq")),
        out_specs=(spec,) * 5,
        check_vma=False,
    )


def solution(mesh):
    return build(mesh, SEQ_DIMS)
```

```python
import functools

import jax
import jax.numpy as jnp
from jax import lax
from jax.experimental import pallas as pl
from jax.experimental.pallas import tpu as pltpu
from jax.sharding import PartitionSpec as P

CG_STEPS = 4
EPS = 1e-6
DH = 128
F32 = jnp.float32
BF = jnp.bfloat16
MESH = pl.DeviceIdType.MESH

SEQ_DIMS = (4, 8, 2)


def nn(a, b):
    return lax.dot_general(a, b, (((1,), (0,)), ((), ())), preferred_element_type=F32)


def nt(a, b):
    return lax.dot_general(a, b, (((1,), (1,)), ((), ())), preferred_element_type=F32)


def tn(a, b):
    return lax.dot_general(a, b, (((0,), (0,)), ((), ())), preferred_element_type=F32)


def halves(a):
    high = a.astype(BF)
    return high, (a - high.astype(F32)).astype(BF)


def twice(product, high, low, right):
    axis = 1 if product is nt else 0
    return product(jnp.concatenate([high, low], axis=1), jnp.concatenate([right, right], axis=axis))


def kernel(
    dims, nx,
    ridge_in, q_in, k_in, v_in, w_in, og_in, doc_in,
    lay, gq, gk_out, gv_out, gw,
    ridge,
    q, k, v, w, doc, lab_own, lab_mate, lab_chip, lab, edge_own, edge, note_chip, note, rim_own, rim,
    t_own, t_mate, t_send, t_recv, t_line, t_lines, p_send, p_recv, p_mate, p_all,
    b_own, b_mate, b_send, b_recv, b_line, b_lines, r_send, r_recv, r_mate, r_all,
    cot, cot_y, cot_t, do_all, target_own, x_all, mix, l_send, l_recv, l_own,
    gw_own, gw_send, gw_recv, z_send, z_far, z_add, z_recv,
    gk, gv,
    load_sem, send_sem, recv_sem,
):
    ny, nz, nc = dims
    heads = ridge.shape[1]
    width = heads * DH
    me, mh = lax.axis_index("seq"), lax.axis_index("head")
    c = lax.rem(me, nc)
    z = lax.rem(me // nc, nz)
    y = me // (nc * nz)
    other = nc - 1 - c
    rows = t_line.shape[0]
    strip = gw.shape[0]

    def at(yy, zz, cc):
        return (yy * nz + zz) * nc + cc

    mate = at(y, z, other)
    y_peers = [lax.rem(y + i, ny) for i in sorted(range(1, ny), key=lambda i: -min(i, ny - i))]
    z_peers = [lax.rem(z + i, nz) for i in sorted(range(1, nz), key=lambda i: -min(i, nz - i))]
    x_peers = [lax.rem(mh + i, nx) for i in range(1, nx)]

    names = ("lab_mate", "lab", "edge", "t_mate", "t", "t_line", "p", "p_mate", "b_mate", "b", "b_line", "note", "rim",
             "r", "r_mate", "cot", "cot_y", "l", "mix0", "mix1", "gw0", "gw1", "far0", "far1", "z0", "z1")
    sems = {name: i for i, name in enumerate(names)}
    sent = []

    def send(name, src, dst, seq, head=None):
        copy = pltpu.make_async_remote_copy(
            src_ref=src, dst_ref=dst,
            send_sem=send_sem.at[sems[name]], recv_sem=recv_sem.at[sems[name]],
            device_id=(seq, mh if head is None else head), device_id_type=MESH,
        )
        copy.start()

    def settle(name, ref, count=None):
        if count == 0:
            return
        ref = ref if count is None else ref.at[pl.ds(0, count)]
        sent.append((name, ref))
        pltpu.make_async_copy(ref, ref, recv_sem.at[sems[name]]).wait()

    loads = [
        pltpu.make_async_copy(src, dst, load_sem.at[i])
        for i, (src, dst) in enumerate(
            ((doc_in, doc), (k_in, k), (v_in, v), (og_in, cot.at[mh]), (w_in, w), (q_in, q), (ridge_in, ridge))
        )
    ]
    for load in loads:
        load.start()

    barrier = pltpu.get_barrier_semaphore()
    peers = [(at(y, zz, c), mh) for zz in z_peers] + [(at(yy, z, c), mh) for yy in y_peers]
    peers += [(me, hh) for hh in x_peers] + [(mate, mh)]
    for peer in peers:
        pl.semaphore_signal(barrier, inc=1, device_id=peer, device_id_type=MESH)

    loads[0].wait()
    doc_row = jnp.broadcast_to(doc[...].astype(F32), (DH, DH))
    doc_col = doc_row.T
    last, first = doc_col[DH - 1 : DH, :], doc_col[0:1, :]
    for small in (lab_own, lab_chip, edge_own, note_chip, rim_own):
        small[...] = jnp.zeros_like(small)
    lab_own[0:1, :] = last
    lab_own[1:2, :] = first
    same_doc = jnp.where(
        (doc_row == doc_col)
        & (lax.broadcasted_iota(jnp.int32, (DH, DH), 1) <= lax.broadcasted_iota(jnp.int32, (DH, DH), 0)),
        1.0,
        0.0,
    ).astype(F32)
    tail = jnp.where(doc_col == last, 1.0, 0.0).astype(BF)
    head_rows = jnp.where(doc_col == first, 1.0, 0.0).astype(F32)

    in_half = heads // nc
    chunk = in_half * DH
    order = [(half, i) for half in range(nc) for i in range(in_half)]
    row_idx = lax.broadcasted_iota(jnp.int32, (DH, DH), 0)
    col_idx = lax.broadcasted_iota(jnp.int32, (DH, DH), 1)

    def cols_of(half, i):
        start = (half * in_half + i) * DH
        return pl.ds(start if isinstance(start, int) else pl.multiple_of(start, DH), DH)

    loads[1].wait()
    loads[2].wait()
    def gram(half):
        for i in range(in_half):
            cols = cols_of(half, i)
            kh, vh = k[:, cols], v[:, cols]
            t_own[half, i] = tn(jnp.concatenate([kh * tail, vh * tail], axis=1), kh).astype(BF)

    gram(other)
    loads[3].wait()
    pl.semaphore_wait(barrier, len(peers))

    def combine(own, from_mate, packed, row, leads):
        joined = jnp.where(lab_own[row : row + 1, :] == lab_mate[row : row + 1, :], 1.0, 0.0)
        own_part = jnp.where(leads, joined, 1.0)
        mate_part = jnp.where(leads, 1.0, joined)
        one, two = [own[c, i].astype(F32) * own_part + from_mate[i].astype(F32) * mate_part for i in range(in_half)]
        mixed = jnp.where(col_idx >= row_idx, one[:DH], two[:DH])
        packed[...] = jnp.concatenate([mixed, one[DH:], two[DH:]], axis=0).astype(BF).reshape(nz, rows, DH)
        return jnp.sum(jnp.where(col_idx == row_idx, two[:DH], 0.0), axis=0, keepdims=True)

    def unpack(packed, diagonal):
        whole = packed[...].reshape(3 * DH, DH).astype(F32)
        mixed = whole[:DH]
        turned = mixed.T
        one = jnp.where(col_idx >= row_idx, mixed, turned)
        two = jnp.where(col_idx < row_idx, mixed, jnp.where(col_idx == row_idx, diagonal, turned))
        return jnp.concatenate([one, whole[DH : 2 * DH]], axis=0), jnp.concatenate([two, whole[2 * DH :]], axis=0)

    def line_total(parts, diagonals, line, row, reverse):
        total, diagonal, before = jnp.zeros((rows, DH), F32), jnp.zeros((1, DH), F32), None
        for i in reversed(range(nz)) if reverse else range(nz):
            label = lab[i, row : row + 1, :]
            if before is not None:
                total = jnp.where(label == before, total, 0.0)
                diagonal = jnp.where(label == before, diagonal, 0.0)
            total = total + parts[i].astype(F32)
            diagonal = diagonal + diagonals[i, 2:3, :]
            before = label
        line[...] = total.astype(BF)
        return diagonal

    def incoming(lines, diagonals, row, reverse):
        total, diagonal = jnp.zeros((rows, DH), F32), jnp.zeros((1, DH), F32)
        before = jnp.full((1, DH), -1.0, F32)
        for i in reversed(range(ny)) if reverse else range(ny):
            label = edge[i, row : row + 1, :]
            grown = jnp.where(label == before, total, 0.0) + lines[i].astype(F32)
            grown_diagonal = jnp.where(label == before, diagonal, 0.0) + diagonals[i, 2:3, :]
            reached = i > y if reverse else i < y
            total = jnp.where(reached, grown, total)
            diagonal = jnp.where(reached, grown_diagonal, diagonal)
            before = jnp.where(reached, label, before)
        return total, diagonal, before

    def scan(parts, diagonals, start, out, row, reverse):
        total, diagonal, before = start
        chip_diagonal, chip_before = diagonal, before
        for i in reversed(range(nz)) if reverse else range(nz):
            label = lab[i, row : row + 1, :]
            out[i] = total.astype(BF)
            chip_before = jnp.where(i == z, before, chip_before)
            chip_diagonal = jnp.where(i == z, diagonal, chip_diagonal)
            total = jnp.where(label == before, total, 0.0) + parts[i].astype(F32)
            diagonal = jnp.where(label == before, diagonal, 0.0) + diagonals[i, 2:3, :]
            before = label
        return chip_diagonal, chip_before

    def spread(own, from_mate, packed, chip_diagonal, to_mate, whole, row, chip_before, leads):
        lead_label = jnp.where(leads, lab_own[row : row + 1, :], lab_mate[row : row + 1, :])
        joined = jnp.where(lead_label == chip_before, 1.0, 0.0)
        for i, ahead in enumerate(unpack(packed, chip_diagonal)):
            lead_state = jnp.where(leads, own[c, i].astype(F32), from_mate[i].astype(F32))
            trail = lead_state + joined * ahead
            whole[c, i] = jnp.where(leads, ahead, trail).astype(BF)
            to_mate[i] = jnp.where(leads, trail, ahead).astype(BF)
        return jnp.where(leads, chip_before, lead_label)

    leads, leads_back = c == 0, c == nc - 1

    send("lab_mate", lab_own, lab_mate, mate)
    send("t_mate", t_own.at[other], t_mate, mate)
    for hh in x_peers:
        send("cot", cot.at[mh], cot.at[mh], me, hh)
    gram(c)

    settle("lab_mate", lab_mate)
    lab_chip[0:1, :] = jnp.where(leads, lab_mate[0:1, :], lab_own[0:1, :])
    lab_chip[1:2, :] = jnp.where(leads, lab_own[1:2, :], lab_mate[1:2, :])
    settle("t_mate", t_mate)
    lab_chip[2:3, :] = combine(t_own, t_mate, t_send, 0, leads)
    lab[z] = lab_chip[...]
    for zz in z_peers:
        send("lab", lab_chip, lab.at[z], at(y, zz, c))
        send("t", t_send.at[zz], t_recv.at[z], at(y, zz, c))
    t_recv[z] = t_send[z]

    settle("lab", lab, nz - 1)
    settle("t", t_recv, nz - 1)
    edge_own[0:1, :] = lab[nz - 1, 0:1, :]
    edge_own[1:2, :] = lab[0, 1:2, :]
    edge_own[2:3, :] = line_total(t_recv, lab, t_line, 0, False)
    edge[y] = edge_own[...]
    for yy in y_peers:
        send("edge", edge_own, edge.at[y], at(yy, z, c))
        send("t_line", t_line, t_lines.at[y], at(yy, z, c))
    t_lines[y] = t_line[...]
    settle("edge", edge, ny - 1)
    settle("t_line", t_lines, ny - 1)
    chip_diagonal, chip_before = scan(t_recv, lab, incoming(t_lines, edge, 0, False), p_send, 0, False)
    for zz in z_peers:
        send("p", p_send.at[zz], p_recv.at[z], at(y, zz, c))
    p_recv[z] = p_send[z]

    loads[4].wait()
    settle("cot", cot, nx - 1)
    for yy in y_peers:
        send("cot_y", cot.at[yy], cot_y.at[y], at(yy, z, c))
    cot_y[y] = cot[y]
    do = nt(cot[0], w[:, 0:width])
    for b in range(1, nx):
        do = do + nt(cot[b], w[:, b * width : (b + 1) * width])
    do_all[...] = do

    do_high, score_two = [], []
    for h, (half, i) in enumerate(order):
        cols = cols_of(half, i)
        kh, vh = k[:, cols], v[:, cols]
        high, low = halves(do[:, h * DH : (h + 1) * DH])
        two = twice(nt, high, low, vh) * same_doc
        do_high.append(high)
        score_two.append(two)
        target_own[:, cols] = twice(nn, *halves(two), kh)
    loads[5].wait()
    loads[6].wait()

    settle("p", p_recv, nz - 1)
    label_in = spread(t_own, t_mate, p_recv, chip_diagonal, p_mate, p_all, 0, chip_before, leads)
    send("p_mate", p_mate, p_all.at[c], mate)
    carried = jnp.where(doc_col == label_in, 1.0, 0.0).astype(F32)
    carried_two = jnp.concatenate([carried, carried], axis=0).astype(BF)
    same_two = jnp.concatenate([same_doc, same_doc], axis=0)

    def solve():
        slots = range(heads)
        cols = [cols_of(*order[i]) for i in slots]
        keys, x, r, p, rr = [], [], [], [], []
        for i in slots:
            state = p_all[order[i]]
            value_in = state[DH:]
            target = carried * twice(nn, *halves(do_all[:, cols[i]]), value_in) + target_own[:, cols[i]]
            b = jnp.concatenate([q[:, cols[i]].astype(F32), target], axis=0)
            kh = k[:, cols[i]]
            keys.append(jnp.concatenate([kh, state[:DH]], axis=0))
            x.append(jnp.zeros_like(b))
            r.append(b)
            p.append(b)
            rr.append(jnp.sum(b * b, axis=1, keepdims=True))
        for number in range(CG_STEPS):
            high = [p[i].astype(BF) for i in slots]
            scores = [nt(high[i], k[:, cols[i]]) * same_two for i in slots]
            applied = [
                nn(jnp.concatenate([scores[i].astype(BF), high[i] * carried_two], axis=1), keys[i])
                + ridge[0, i] * p[i]
                for i in slots
            ]
            step = [rr[i] / (jnp.sum(p[i] * applied[i], axis=1, keepdims=True) + EPS) for i in slots]
            for i in slots:
                x[i] = x[i] + step[i] * p[i]
            if number < CG_STEPS - 1:
                for i in slots:
                    r[i] = r[i] - step[i] * applied[i]
                fresh = [jnp.sum(r[i] * r[i], axis=1, keepdims=True) for i in slots]
                for i in slots:
                    p[i] = r[i] + fresh[i] / (rr[i] + EPS) * p[i]
                rr = fresh
        for i in slots:
            x_all[i] = x[i]

    settle("p_mate", p_mate)
    solve()

    for h, (half, i) in enumerate(order):
        x_h = x_all[h]
        rows_x = (head_rows * x_h[:DH]).astype(BF)
        both = tn(jnp.concatenate([do_high[h], x_h[DH:].astype(BF)], axis=1), rows_x)
        cross = both[DH:]
        b_own[half, i] = jnp.concatenate([cross + cross.T, both[:DH]], axis=0).astype(BF)
    send("b_mate", b_own.at[other], b_mate, mate)

    x_high, score_x = [], []

    def read_out(group):
        for i in range(in_half):
            h = group * in_half + i
            cols = slice(h * DH, (h + 1) * DH)
            kh, vh = k[:, cols], v[:, cols]
            value_in = p_all[group, i, DH:, :]
            high, low = halves(x_all[h])
            x_high.append(high)
            scores = twice(nt, high, low, kh) * same_two
            score_x.append(scores)
            out = twice(nn, *halves(scores[:DH]), vh) + carried * twice(nt, high[:DH], low[:DH], value_in)
            mix[group, y, :, i * DH : (i + 1) * DH] = out.astype(BF)
        for yy in y_peers:
            send(f"mix{group}", mix.at[group, y], mix.at[group, y], at(yy, z, c))

    read_out(0)
    settle("b_mate", b_mate)
    note_chip[2:3, :] = combine(b_own, b_mate, b_send, 1, leads_back)
    note[z] = note_chip[...]
    for zz in z_peers:
        send("note", note_chip, note.at[z], at(y, zz, c))
        send("b", b_send.at[zz], b_recv.at[z], at(y, zz, c))
    b_recv[z] = b_send[z]

    read_out(1)

    for h, (half, i) in enumerate(order):
        gq[:, cols_of(half, i)] = x_high[h][DH:]
    mixed = jnp.concatenate([mix[group, y] for group in range(nc)], axis=1)

    def project(block):
        cols = pl.ds(pl.multiple_of(block * width, width), width)
        return nn(mixed, w[:, cols])

    for i, hh in enumerate(x_peers):
        l_send[i] = project(hh).astype(BF)
        send("l", l_send.at[i], l_recv.at[mh], me, hh)
    l_own[...] = project(mh)
    l_recv[mh] = jnp.zeros((DH, width), BF)

    for h, (half, i) in enumerate(order):
        cols = cols_of(half, i)
        one = score_x[h][:DH].astype(BF)
        rest = (score_two[h] - score_x[h][DH:]).astype(BF)
        gv[:, cols] = tn(one, do_high[h])
        gk[:, cols] = tn(rest, x_high[h][:DH]) - tn(one, x_high[h][DH:])

    settle("cot_y", cot_y, ny - 1)
    for b in range(ny):
        turned = cot_y[b].T
        for zz in range(nz):
            for cc in range(nc):
                cut = (zz * nc + cc) * strip
                cot_t[cc, zz * strip : (zz + 1) * strip, b * DH : (b + 1) * DH] = turned[cut : cut + strip, :]

    def product(group):
        settle(f"mix{group}", mix.at[group], ny - 1)
        gathered = mix[group].reshape(ny * DH, chunk)
        gw_send[group] = nn(cot_t[other], gathered).astype(BF).reshape(nz, strip, chunk)
        send(f"gw{group}", gw_send.at[group], gw_recv.at[group], mate)
        gw_own[group] = nn(cot_t[c], gathered).reshape(nz, strip, chunk)

    distances = [i if i <= nz // 2 else i - nz for i in range(1, nz)]
    near = [d for d in (1, -1, 2, -2) if d in distances]
    far = [d for d in distances if abs(d) > 2]
    two_away = [d for d in near if abs(d) == 2]

    def chip(distance):
        return lax.rem(z + distance + nz, nz)

    def along_z(group):
        settle(f"gw{group}", gw_recv.at[group])
        z_send[group] = (gw_own[group] + gw_recv[group].astype(F32)).astype(BF)
        for slot, d in enumerate(far):
            via = -2 if abs(d) == 4 else d // 3
            send(f"far{group}", z_send.at[group, chip(d)], z_far.at[group, slot], at(y, chip(via), c))

    def along_z_again(group):
        for slot, d in enumerate(near):
            if d not in two_away:
                send(f"z{group}", z_send.at[group, chip(d)], z_recv.at[group, slot], at(y, chip(d), c))
        if not two_away:
            return
        settle(f"far{group}", z_far.at[group])
        for d in two_away:
            total = z_send[group, chip(d)].astype(F32)
            for slot, e in enumerate(far):
                if (d == -2) if abs(e) == 4 else (e * d > 0):
                    total = total + z_far[group, slot].astype(F32)
            z_add[group, two_away.index(d)] = total.astype(BF)
            slot = near.index(d)
            send(f"z{group}", z_add.at[group, two_away.index(d)], z_recv.at[group, slot], at(y, chip(d), c))

    product(0)
    settle("note", note, nz - 1)
    settle("b", b_recv, nz - 1)
    rim_own[2:3, :] = line_total(b_recv, note, b_line, 1, True)
    rim[y] = rim_own[...]
    for yy in y_peers:
        send("rim", rim_own, rim.at[y], at(yy, z, c))
        send("b_line", b_line, b_lines.at[y], at(yy, z, c))
    b_lines[y] = b_line[...]
    along_z(0)
    product(1)
    along_z(1)
    settle("rim", rim, ny - 1)
    settle("b_line", b_lines, ny - 1)
    chip_diagonal, chip_before = scan(b_recv, note, incoming(b_lines, rim, 1, True), r_send, 1, True)
    for zz in z_peers:
        send("r", r_send.at[zz], r_recv.at[z], at(y, zz, c))
    r_recv[z] = r_send[z]

    along_z_again(0)
    settle("l", l_recv, nx - 1)
    total = l_own[...]
    for b in range(nx):
        total = total + l_recv[b].astype(F32)
    lay[...] = total.astype(BF)
    along_z_again(1)

    settle("r", r_recv, nz - 1)
    label_next = spread(b_own, b_mate, r_recv, chip_diagonal, r_mate, r_all, 1, chip_before, leads_back)
    send("r_mate", r_mate, r_all.at[c], mate)
    later = jnp.where(doc_col == label_next, 1.0, 0.0).astype(F32)

    def finish(half):
        for i in range(in_half):
            cols = cols_of(half, i)
            kh, vh = k[:, cols], v[:, cols]
            state = r_all[half, i]
            gram_grad, grad_state = state[:DH], state[DH:]
            gv_out[:, cols] = (gv[:, cols] + later * nt(kh, grad_state)).astype(BF)
            gk_out[:, cols] = (gk[:, cols] + later * (nn(vh, grad_state) - nn(kh, gram_grad))).astype(BF)

    finish(c)
    settle("r_mate", r_mate)
    finish(other)

    for group in range(nc):
        settle(f"z{group}", z_recv.at[group])
        total = z_send[group, z].astype(F32)
        for slot in range(len(near)):
            total = total + z_recv[group, slot].astype(F32)
        gw[:, group * chunk : (group + 1) * chunk] = total

    for name, ref in sent:
        pltpu.make_async_copy(ref, ref, send_sem.at[sems[name]]).wait()


def move(*refs):
    count = (len(refs) - 1) // 2
    ins, outs, sem = refs[:count], refs[count : 2 * count], refs[-1]
    writes = [pltpu.make_async_copy(a, b, sem.at[i]) for i, (a, b) in enumerate(zip(ins, outs))]
    for write in writes:
        write.start()
    for write in writes:
        write.wait()


def per_device(dims, nx, query_rows, key_rows, value_rows, ridge_reg, out_weight, out_grad, doc_ids):
    ny, nz, nc = dims
    heads = ridge_reg.shape[0]
    width = heads * DH
    rows = 3 * DH // nz
    strip = width // (nz * nc)
    any_space = pl.BlockSpec(memory_space=pl.ANY)
    packed = pltpu.VMEM((nz, rows, DH), BF)
    half = pltpu.VMEM((heads // nc, 2 * DH, DH), BF)
    both = pltpu.VMEM((nc, heads // nc, 2 * DH, DH), BF)
    line = pltpu.VMEM((rows, DH), BF)
    lines = pltpu.VMEM((ny, rows, DH), BF)
    label = pltpu.VMEM((4, DH), F32)
    wide = pltpu.VMEM((DH, width), BF)
    held = (wide, wide, wide, wide, pltpu.VMEM((strip, width), F32))
    states = [both, half, packed, packed, line, lines, packed, packed, half, both]
    made = pl.pallas_call(
        functools.partial(kernel, dims, nx),
        out_shape=held,
        in_specs=[any_space] * 7,
        out_specs=(pl.BlockSpec(memory_space=pltpu.VMEM),) * 5,
        scratch_shapes=[
            pltpu.SMEM((1, heads), F32),
            wide,
            wide,
            wide,
            pltpu.VMEM((width, nx * width), BF),
            pltpu.VMEM((1, DH), jnp.int32),
            label,
            label,
            label,
            pltpu.VMEM((nz, 4, DH), F32),
            label,
            pltpu.VMEM((ny, 4, DH), F32),
            label,
            pltpu.VMEM((nz, 4, DH), F32),
            label,
            pltpu.VMEM((ny, 4, DH), F32),
            *states,
            *states,
            pltpu.VMEM((nx, DH, width), BF),
            pltpu.VMEM((ny, DH, width), BF),
            pltpu.VMEM((nc, nz * strip, ny * DH), BF),
            pltpu.VMEM((DH, width), F32),
            pltpu.VMEM((DH, width), F32),
            pltpu.VMEM((heads, 2 * DH, DH), F32),
            pltpu.VMEM((nc, ny, DH, width // nc), BF),
            pltpu.VMEM((nx, DH, width), BF),
            pltpu.VMEM((nx, DH, width), BF),
            pltpu.VMEM((DH, width), F32),
            pltpu.VMEM((nc, nz, strip, width // nc), F32),
            *[pltpu.VMEM((nc, nz, strip, width // nc), BF)] * 3,
            pltpu.VMEM((nc, 3, strip, width // nc), BF),
            pltpu.VMEM((nc, 2, strip, width // nc), BF),
            pltpu.VMEM((nc, min(4, nz - 1), strip, width // nc), BF),
            pltpu.VMEM((DH, width), F32),
            pltpu.VMEM((DH, width), F32),
            pltpu.SemaphoreType.DMA((7,)),
            pltpu.SemaphoreType.DMA((26,)),
            pltpu.SemaphoreType.DMA((26,)),
        ],
        compiler_params=pltpu.CompilerParams(collective_id=0, has_side_effects=True),
    )(ridge_reg.reshape(1, -1), query_rows, key_rows, value_rows, out_weight, out_grad, doc_ids.reshape(1, -1))
    return pl.pallas_call(
        move,
        out_shape=[jax.ShapeDtypeStruct(a.shape, a.dtype) for a in made],
        in_specs=[pl.BlockSpec(memory_space=pltpu.VMEM)] * 5,
        out_specs=[any_space] * 5,
        scratch_shapes=[pltpu.SemaphoreType.DMA((5,))],
    )(*[pltpu.with_memory_space_constraint(a, pltpu.VMEM) for a in made])


def build(mesh, dims):
    nx = mesh.shape["head"]
    spec = P("seq", "head")
    return jax.shard_map(
        functools.partial(per_device, dims, nx),
        mesh=mesh,
        in_specs=(spec, spec, spec, P("head"), P("head", None), spec, P("seq")),
        out_specs=(spec,) * 5,
        check_vma=False,
    )


def solution(mesh):
    return build(mesh, SEQ_DIMS)
```

```python
import functools

import jax
import jax.numpy as jnp
from jax import lax
from jax.experimental import pallas as pl
from jax.experimental.pallas import tpu as pltpu
from jax.sharding import PartitionSpec as P

CG_STEPS = 4
EPS = 1e-6
DH = 128
F32 = jnp.float32
BF = jnp.bfloat16
MESH = pl.DeviceIdType.MESH

SEQ_DIMS = (4, 8, 2)


def nn(a, b):
    return lax.dot_general(a, b, (((1,), (0,)), ((), ())), preferred_element_type=F32)


def nt(a, b):
    return lax.dot_general(a, b, (((1,), (1,)), ((), ())), preferred_element_type=F32)


def tn(a, b):
    return lax.dot_general(a, b, (((0,), (0,)), ((), ())), preferred_element_type=F32)


def halves(a):
    high = a.astype(BF)
    return high, (a - high.astype(F32)).astype(BF)


def twice(product, high, low, right):
    axis = 1 if product is nt else 0
    return product(jnp.concatenate([high, low], axis=1), jnp.concatenate([right, right], axis=axis))


def kernel(
    dims, nx,
    ridge_in, q_in, k_in, v_in, w_in, og_in, doc_in,
    lay, gq, gk_out, gv_out, gw,
    ridge,
    q, k, v, w, doc, lab_own, lab_mate, lab_chip, lab, edge_own, edge, note_chip, note, rim_own, rim,
    t_own, t_mate, t_send, t_recv, t_line, t_lines, p_send, p_recv, p_mate, p_all,
    b_own, b_mate, b_send, b_recv, b_line, b_lines, r_send, r_recv, r_mate, r_all,
    cot, cot_y, cot_t, do_all, target_own, x_all, mix, l_send, l_recv, l_own,
    gw_own, gw_send, gw_recv, z_send, z_far, z_add, z_recv,
    gk, gv,
    load_sem, send_sem, recv_sem,
):
    ny, nz, nc = dims
    heads = ridge.shape[1]
    width = heads * DH
    me, mh = lax.axis_index("seq"), lax.axis_index("head")
    c = lax.rem(me, nc)
    z = lax.rem(me // nc, nz)
    y = me // (nc * nz)
    other = nc - 1 - c
    rows = t_line.shape[0]
    strip = gw.shape[0]

    def at(yy, zz, cc):
        return (yy * nz + zz) * nc + cc

    mate = at(y, z, other)
    y_peers = [lax.rem(y + i, ny) for i in sorted(range(1, ny), key=lambda i: -min(i, ny - i))]
    z_peers = [lax.rem(z + i, nz) for i in sorted(range(1, nz), key=lambda i: -min(i, nz - i))]
    x_peers = [lax.rem(mh + i, nx) for i in range(1, nx)]

    names = ("lab_mate", "lab", "edge", "t_mate", "t", "t_line", "p", "p_mate", "b_mate", "b", "b_line", "note", "rim",
             "r", "r_mate", "cot", "cot_y", "l", "mix0", "mix1", "gw0", "gw1", "far0", "far1", "z0", "z1")
    sems = {name: i for i, name in enumerate(names)}
    sent = []

    def send(name, src, dst, seq, head=None):
        copy = pltpu.make_async_remote_copy(
            src_ref=src, dst_ref=dst,
            send_sem=send_sem.at[sems[name]], recv_sem=recv_sem.at[sems[name]],
            device_id=(seq, mh if head is None else head), device_id_type=MESH,
        )
        copy.start()

    def settle(name, ref, count=None):
        if count == 0:
            return
        ref = ref if count is None else ref.at[pl.ds(0, count)]
        sent.append((name, ref))
        pltpu.make_async_copy(ref, ref, recv_sem.at[sems[name]]).wait()

    loads = [
        pltpu.make_async_copy(src, dst, load_sem.at[i])
        for i, (src, dst) in enumerate(
            ((doc_in, doc), (k_in, k), (v_in, v), (og_in, cot.at[mh]), (w_in, w), (q_in, q), (ridge_in, ridge))
        )
    ]
    for load in loads:
        load.start()

    barrier = pltpu.get_barrier_semaphore()
    peers = [(at(y, zz, c), mh) for zz in z_peers] + [(at(yy, z, c), mh) for yy in y_peers]
    peers += [(me, hh) for hh in x_peers] + [(mate, mh)]
    for peer in peers:
        pl.semaphore_signal(barrier, inc=1, device_id=peer, device_id_type=MESH)

    loads[0].wait()
    doc_row = jnp.broadcast_to(doc[...].astype(F32), (DH, DH))
    doc_col = doc_row.T
    last, first = doc_col[DH - 1 : DH, :], doc_col[0:1, :]
    for small in (lab_own, lab_chip, edge_own, note_chip, rim_own):
        small[...] = jnp.zeros_like(small)
    lab_own[0:1, :] = last
    lab_own[1:2, :] = first
    same_doc = jnp.where(
        (doc_row == doc_col)
        & (lax.broadcasted_iota(jnp.int32, (DH, DH), 1) <= lax.broadcasted_iota(jnp.int32, (DH, DH), 0)),
        1.0,
        0.0,
    ).astype(F32)
    tail = jnp.where(doc_col == last, 1.0, 0.0).astype(BF)
    head_rows = jnp.where(doc_col == first, 1.0, 0.0).astype(F32)

    in_half = heads // nc
    chunk = in_half * DH
    order = [(half, i) for half in range(nc) for i in range(in_half)]
    row_idx = lax.broadcasted_iota(jnp.int32, (DH, DH), 0)
    col_idx = lax.broadcasted_iota(jnp.int32, (DH, DH), 1)

    def cols_of(half, i):
        start = (half * in_half + i) * DH
        return pl.ds(start if isinstance(start, int) else pl.multiple_of(start, DH), DH)

    loads[1].wait()
    loads[2].wait()
    def gram(half):
        for i in range(in_half):
            cols = cols_of(half, i)
            kh, vh = k[:, cols], v[:, cols]
            t_own[half, i] = tn(jnp.concatenate([kh * tail, vh * tail], axis=1), kh).astype(BF)

    gram(other)
    loads[3].wait()
    pl.semaphore_wait(barrier, len(peers))

    def combine(own, from_mate, packed, row, leads):
        joined = jnp.where(lab_own[row : row + 1, :] == lab_mate[row : row + 1, :], 1.0, 0.0)
        own_part = jnp.where(leads, joined, 1.0)
        mate_part = jnp.where(leads, 1.0, joined)
        one, two = [own[c, i].astype(F32) * own_part + from_mate[i].astype(F32) * mate_part for i in range(in_half)]
        mixed = jnp.where(col_idx >= row_idx, one[:DH], two[:DH])
        packed[...] = jnp.concatenate([mixed, one[DH:], two[DH:]], axis=0).astype(BF).reshape(nz, rows, DH)
        return jnp.sum(jnp.where(col_idx == row_idx, two[:DH], 0.0), axis=0, keepdims=True)

    def unpack(packed, diagonal):
        whole = packed[...].reshape(3 * DH, DH).astype(F32)
        mixed = whole[:DH]
        turned = mixed.T
        one = jnp.where(col_idx >= row_idx, mixed, turned)
        two = jnp.where(col_idx < row_idx, mixed, jnp.where(col_idx == row_idx, diagonal, turned))
        return jnp.concatenate([one, whole[DH : 2 * DH]], axis=0), jnp.concatenate([two, whole[2 * DH :]], axis=0)

    def line_total(parts, diagonals, line, row, reverse):
        total, diagonal, before = jnp.zeros((rows, DH), F32), jnp.zeros((1, DH), F32), None
        for i in reversed(range(nz)) if reverse else range(nz):
            label = lab[i, row : row + 1, :]
            if before is not None:
                total = jnp.where(label == before, total, 0.0)
                diagonal = jnp.where(label == before, diagonal, 0.0)
            total = total + parts[i].astype(F32)
            diagonal = diagonal + diagonals[i, 2:3, :]
            before = label
        line[...] = total.astype(BF)
        return diagonal

    def incoming(lines, diagonals, row, reverse):
        total, diagonal = jnp.zeros((rows, DH), F32), jnp.zeros((1, DH), F32)
        before = jnp.full((1, DH), -1.0, F32)
        for i in reversed(range(ny)) if reverse else range(ny):
            label = edge[i, row : row + 1, :]
            grown = jnp.where(label == before, total, 0.0) + lines[i].astype(F32)
            grown_diagonal = jnp.where(label == before, diagonal, 0.0) + diagonals[i, 2:3, :]
            reached = i > y if reverse else i < y
            total = jnp.where(reached, grown, total)
            diagonal = jnp.where(reached, grown_diagonal, diagonal)
            before = jnp.where(reached, label, before)
        return total, diagonal, before

    def scan(parts, diagonals, start, out, row, reverse):
        total, diagonal, before = start
        chip_diagonal, chip_before = diagonal, before
        for i in reversed(range(nz)) if reverse else range(nz):
            label = lab[i, row : row + 1, :]
            out[i] = total.astype(BF)
            chip_before = jnp.where(i == z, before, chip_before)
            chip_diagonal = jnp.where(i == z, diagonal, chip_diagonal)
            total = jnp.where(label == before, total, 0.0) + parts[i].astype(F32)
            diagonal = jnp.where(label == before, diagonal, 0.0) + diagonals[i, 2:3, :]
            before = label
        return chip_diagonal, chip_before

    def spread(own, from_mate, packed, chip_diagonal, to_mate, whole, row, chip_before, leads):
        lead_label = jnp.where(leads, lab_own[row : row + 1, :], lab_mate[row : row + 1, :])
        joined = jnp.where(lead_label == chip_before, 1.0, 0.0)
        for i, ahead in enumerate(unpack(packed, chip_diagonal)):
            lead_state = jnp.where(leads, own[c, i].astype(F32), from_mate[i].astype(F32))
            trail = lead_state + joined * ahead
            whole[c, i] = jnp.where(leads, ahead, trail).astype(BF)
            to_mate[i] = jnp.where(leads, trail, ahead).astype(BF)
        return jnp.where(leads, chip_before, lead_label)

    leads, leads_back = c == 0, c == nc - 1

    send("lab_mate", lab_own, lab_mate, mate)
    send("t_mate", t_own.at[other], t_mate, mate)
    for hh in x_peers:
        send("cot", cot.at[mh], cot.at[mh], me, hh)
    gram(c)

    settle("lab_mate", lab_mate)
    lab_chip[0:1, :] = jnp.where(leads, lab_mate[0:1, :], lab_own[0:1, :])
    lab_chip[1:2, :] = jnp.where(leads, lab_own[1:2, :], lab_mate[1:2, :])
    settle("t_mate", t_mate)
    lab_chip[2:3, :] = combine(t_own, t_mate, t_send, 0, leads)
    lab[z] = lab_chip[...]
    for zz in z_peers:
        send("lab", lab_chip, lab.at[z], at(y, zz, c))
        send("t", t_send.at[zz], t_recv.at[z], at(y, zz, c))
    t_recv[z] = t_send[z]

    settle("lab", lab, nz - 1)
    settle("t", t_recv, nz - 1)
    edge_own[0:1, :] = lab[nz - 1, 0:1, :]
    edge_own[1:2, :] = lab[0, 1:2, :]
    edge_own[2:3, :] = line_total(t_recv, lab, t_line, 0, False)
    edge[y] = edge_own[...]
    for yy in y_peers:
        send("edge", edge_own, edge.at[y], at(yy, z, c))
        send("t_line", t_line, t_lines.at[y], at(yy, z, c))
    t_lines[y] = t_line[...]
    settle("edge", edge, ny - 1)
    settle("t_line", t_lines, ny - 1)
    chip_diagonal, chip_before = scan(t_recv, lab, incoming(t_lines, edge, 0, False), p_send, 0, False)
    for zz in z_peers:
        send("p", p_send.at[zz], p_recv.at[z], at(y, zz, c))
    p_recv[z] = p_send[z]

    loads[4].wait()
    settle("cot", cot, nx - 1)
    for yy in y_peers:
        send("cot_y", cot.at[yy], cot_y.at[y], at(yy, z, c))
    cot_y[y] = cot[y]
    do = nt(cot[0], w[:, 0:width])
    for b in range(1, nx):
        do = do + nt(cot[b], w[:, b * width : (b + 1) * width])
    do_all[...] = do

    do_high, score_two = [], []
    for h, (half, i) in enumerate(order):
        cols = cols_of(half, i)
        kh, vh = k[:, cols], v[:, cols]
        high, low = halves(do[:, h * DH : (h + 1) * DH])
        two = twice(nt, high, low, vh) * same_doc
        do_high.append(high)
        score_two.append(two)
        target_own[:, cols] = twice(nn, *halves(two), kh)
    loads[5].wait()
    loads[6].wait()

    settle("p", p_recv, nz - 1)
    label_in = spread(t_own, t_mate, p_recv, chip_diagonal, p_mate, p_all, 0, chip_before, leads)
    send("p_mate", p_mate, p_all.at[c], mate)
    carried = jnp.where(doc_col == label_in, 1.0, 0.0).astype(F32)
    carried_two = jnp.concatenate([carried, carried], axis=0).astype(BF)
    same_two = jnp.concatenate([same_doc, same_doc], axis=0)

    def solve():
        slots = range(heads)
        cols = [cols_of(*order[i]) for i in slots]
        keys, x, r, p, rr = [], [], [], [], []
        for i in slots:
            state = p_all[order[i]]
            value_in = state[DH:]
            target = carried * twice(nn, *halves(do_all[:, cols[i]]), value_in) + target_own[:, cols[i]]
            b = jnp.concatenate([q[:, cols[i]].astype(F32), target], axis=0)
            kh = k[:, cols[i]]
            keys.append(jnp.concatenate([kh, state[:DH]], axis=0))
            x.append(jnp.zeros_like(b))
            r.append(b)
            p.append(b)
            rr.append(jnp.sum(b * b, axis=1, keepdims=True))
        for number in range(CG_STEPS):
            high = [p[i].astype(BF) for i in slots]
            scores = [nt(high[i], k[:, cols[i]]) * same_two for i in slots]
            applied = [
                nn(jnp.concatenate([scores[i].astype(BF), high[i] * carried_two], axis=1), keys[i])
                + ridge[0, i] * p[i]
                for i in slots
            ]
            step = [rr[i] / (jnp.sum(p[i] * applied[i], axis=1, keepdims=True) + EPS) for i in slots]
            for i in slots:
                x[i] = x[i] + step[i] * p[i]
            if number < CG_STEPS - 1:
                for i in slots:
                    r[i] = r[i] - step[i] * applied[i]
                fresh = [jnp.sum(r[i] * r[i], axis=1, keepdims=True) for i in slots]
                for i in slots:
                    p[i] = r[i] + fresh[i] / (rr[i] + EPS) * p[i]
                rr = fresh
        for i in slots:
            x_all[i] = x[i]

    settle("p_mate", p_mate)
    solve()

    for h, (half, i) in enumerate(order):
        x_h = x_all[h]
        rows_x = (head_rows * x_h[:DH]).astype(BF)
        both = tn(jnp.concatenate([do_high[h], x_h[DH:].astype(BF)], axis=1), rows_x)
        cross = both[DH:]
        b_own[half, i] = jnp.concatenate([cross + cross.T, both[:DH]], axis=0).astype(BF)
    send("b_mate", b_own.at[other], b_mate, mate)

    x_high, score_x = [], []

    def read_out(group):
        for i in range(in_half):
            h = group * in_half + i
            cols = slice(h * DH, (h + 1) * DH)
            kh, vh = k[:, cols], v[:, cols]
            value_in = p_all[group, i, DH:, :]
            high, low = halves(x_all[h])
            x_high.append(high)
            scores = twice(nt, high, low, kh) * same_two
            score_x.append(scores)
            out = twice(nn, *halves(scores[:DH]), vh) + carried * twice(nt, high[:DH], low[:DH], value_in)
            mix[group, y, :, i * DH : (i + 1) * DH] = out.astype(BF)
        for yy in y_peers:
            send(f"mix{group}", mix.at[group, y], mix.at[group, y], at(yy, z, c))

    read_out(0)
    settle("b_mate", b_mate)
    note_chip[2:3, :] = combine(b_own, b_mate, b_send, 1, leads_back)
    note[z] = note_chip[...]
    for zz in z_peers:
        send("note", note_chip, note.at[z], at(y, zz, c))
        send("b", b_send.at[zz], b_recv.at[z], at(y, zz, c))
    b_recv[z] = b_send[z]

    read_out(1)

    for h, (half, i) in enumerate(order):
        gq[:, cols_of(half, i)] = x_high[h][DH:]
    mixed = jnp.concatenate([mix[group, y] for group in range(nc)], axis=1)

    def project(block):
        cols = pl.ds(pl.multiple_of(block * width, width), width)
        return nn(mixed, w[:, cols])

    for i, hh in enumerate(x_peers):
        l_send[i] = project(hh).astype(BF)
        send("l", l_send.at[i], l_recv.at[mh], me, hh)
    l_own[...] = project(mh)
    l_recv[mh] = jnp.zeros((DH, width), BF)

    for h, (half, i) in enumerate(order):
        cols = cols_of(half, i)
        one = score_x[h][:DH].astype(BF)
        rest = (score_two[h] - score_x[h][DH:]).astype(BF)
        gv[:, cols] = tn(one, do_high[h])
        gk[:, cols] = tn(rest, x_high[h][:DH]) - tn(one, x_high[h][DH:])

    settle("cot_y", cot_y, ny - 1)
    for b in range(ny):
        turned = cot_y[b].T
        for zz in range(nz):
            for cc in range(nc):
                cut = (zz * nc + cc) * strip
                cot_t[cc, zz * strip : (zz + 1) * strip, b * DH : (b + 1) * DH] = turned[cut : cut + strip, :]

    def product(group):
        settle(f"mix{group}", mix.at[group], ny - 1)
        gathered = mix[group].reshape(ny * DH, chunk)
        gw_send[group] = nn(cot_t[other], gathered).astype(BF).reshape(nz, strip, chunk)
        send(f"gw{group}", gw_send.at[group], gw_recv.at[group], mate)
        gw_own[group] = nn(cot_t[c], gathered).reshape(nz, strip, chunk)

    distances = [i if i <= nz // 2 else i - nz for i in range(1, nz)]
    near = [d for d in (1, -1, 2, -2) if d in distances]
    far = [d for d in distances if abs(d) > 2]
    two_away = [d for d in near if abs(d) == 2]

    def chip(distance):
        return lax.rem(z + distance + nz, nz)

    def send_near(group):
        for slot, d in enumerate(near):
            if d not in two_away:
                send(f"z{group}", z_send.at[group, chip(d)], z_recv.at[group, slot], at(y, chip(d), c))

    def along_z(group):
        settle(f"gw{group}", gw_recv.at[group])
        z_send[group] = (gw_own[group] + gw_recv[group].astype(F32)).astype(BF)
        for slot, d in enumerate(far):
            via = -2 if abs(d) == 4 else d // 3
            send(f"far{group}", z_send.at[group, chip(d)], z_far.at[group, slot], at(y, chip(via), c))
        if group == 0:
            send_near(group)

    def along_z_again(group):
        if group > 0:
            send_near(group)
        if not two_away:
            return
        settle(f"far{group}", z_far.at[group])
        for d in two_away:
            total = z_send[group, chip(d)].astype(F32)
            for slot, e in enumerate(far):
                if (d == -2) if abs(e) == 4 else (e * d > 0):
                    total = total + z_far[group, slot].astype(F32)
            z_add[group, two_away.index(d)] = total.astype(BF)
            slot = near.index(d)
            send(f"z{group}", z_add.at[group, two_away.index(d)], z_recv.at[group, slot], at(y, chip(d), c))

    product(0)
    settle("note", note, nz - 1)
    settle("b", b_recv, nz - 1)
    rim_own[2:3, :] = line_total(b_recv, note, b_line, 1, True)
    rim[y] = rim_own[...]
    for yy in y_peers:
        send("rim", rim_own, rim.at[y], at(yy, z, c))
        send("b_line", b_line, b_lines.at[y], at(yy, z, c))
    b_lines[y] = b_line[...]
    along_z(0)
    product(1)
    along_z(1)
    settle("rim", rim, ny - 1)
    settle("b_line", b_lines, ny - 1)
    chip_diagonal, chip_before = scan(b_recv, note, incoming(b_lines, rim, 1, True), r_send, 1, True)
    for zz in z_peers:
        send("r", r_send.at[zz], r_recv.at[z], at(y, zz, c))
    r_recv[z] = r_send[z]

    along_z_again(0)
    settle("l", l_recv, nx - 1)
    total = l_own[...]
    for b in range(nx):
        total = total + l_recv[b].astype(F32)
    lay[...] = total.astype(BF)
    along_z_again(1)

    settle("r", r_recv, nz - 1)
    label_next = spread(b_own, b_mate, r_recv, chip_diagonal, r_mate, r_all, 1, chip_before, leads_back)
    send("r_mate", r_mate, r_all.at[c], mate)
    later = jnp.where(doc_col == label_next, 1.0, 0.0).astype(F32)

    def finish(half):
        for i in range(in_half):
            cols = cols_of(half, i)
            kh, vh = k[:, cols], v[:, cols]
            state = r_all[half, i]
            gram_grad, grad_state = state[:DH], state[DH:]
            gv_out[:, cols] = (gv[:, cols] + later * nt(kh, grad_state)).astype(BF)
            gk_out[:, cols] = (gk[:, cols] + later * (nn(vh, grad_state) - nn(kh, gram_grad))).astype(BF)

    finish(c)
    settle("r_mate", r_mate)
    finish(other)

    for group in range(nc):
        settle(f"z{group}", z_recv.at[group])
        total = z_send[group, z].astype(F32)
        for slot in range(len(near)):
            total = total + z_recv[group, slot].astype(F32)
        gw[:, group * chunk : (group + 1) * chunk] = total

    for name, ref in sent:
        pltpu.make_async_copy(ref, ref, send_sem.at[sems[name]]).wait()


def move(*refs):
    count = (len(refs) - 1) // 2
    ins, outs, sem = refs[:count], refs[count : 2 * count], refs[-1]
    writes = [pltpu.make_async_copy(a, b, sem.at[i]) for i, (a, b) in enumerate(zip(ins, outs))]
    for write in writes:
        write.start()
    for write in writes:
        write.wait()


def per_device(dims, nx, query_rows, key_rows, value_rows, ridge_reg, out_weight, out_grad, doc_ids):
    ny, nz, nc = dims
    heads = ridge_reg.shape[0]
    width = heads * DH
    rows = 3 * DH // nz
    strip = width // (nz * nc)
    any_space = pl.BlockSpec(memory_space=pl.ANY)
    packed = pltpu.VMEM((nz, rows, DH), BF)
    half = pltpu.VMEM((heads // nc, 2 * DH, DH), BF)
    both = pltpu.VMEM((nc, heads // nc, 2 * DH, DH), BF)
    line = pltpu.VMEM((rows, DH), BF)
    lines = pltpu.VMEM((ny, rows, DH), BF)
    label = pltpu.VMEM((4, DH), F32)
    wide = pltpu.VMEM((DH, width), BF)
    held = (wide, wide, wide, wide, pltpu.VMEM((strip, width), F32))
    states = [both, half, packed, packed, line, lines, packed, packed, half, both]
    made = pl.pallas_call(
        functools.partial(kernel, dims, nx),
        out_shape=held,
        in_specs=[any_space] * 7,
        out_specs=(pl.BlockSpec(memory_space=pltpu.VMEM),) * 5,
        scratch_shapes=[
            pltpu.SMEM((1, heads), F32),
            wide,
            wide,
            wide,
            pltpu.VMEM((width, nx * width), BF),
            pltpu.VMEM((1, DH), jnp.int32),
            label,
            label,
            label,
            pltpu.VMEM((nz, 4, DH), F32),
            label,
            pltpu.VMEM((ny, 4, DH), F32),
            label,
            pltpu.VMEM((nz, 4, DH), F32),
            label,
            pltpu.VMEM((ny, 4, DH), F32),
            *states,
            *states,
            pltpu.VMEM((nx, DH, width), BF),
            pltpu.VMEM((ny, DH, width), BF),
            pltpu.VMEM((nc, nz * strip, ny * DH), BF),
            pltpu.VMEM((DH, width), F32),
            pltpu.VMEM((DH, width), F32),
            pltpu.VMEM((heads, 2 * DH, DH), F32),
            pltpu.VMEM((nc, ny, DH, width // nc), BF),
            pltpu.VMEM((nx, DH, width), BF),
            pltpu.VMEM((nx, DH, width), BF),
            pltpu.VMEM((DH, width), F32),
            pltpu.VMEM((nc, nz, strip, width // nc), F32),
            *[pltpu.VMEM((nc, nz, strip, width // nc), BF)] * 3,
            pltpu.VMEM((nc, 3, strip, width // nc), BF),
            pltpu.VMEM((nc, 2, strip, width // nc), BF),
            pltpu.VMEM((nc, min(4, nz - 1), strip, width // nc), BF),
            pltpu.VMEM((DH, width), F32),
            pltpu.VMEM((DH, width), F32),
            pltpu.SemaphoreType.DMA((7,)),
            pltpu.SemaphoreType.DMA((26,)),
            pltpu.SemaphoreType.DMA((26,)),
        ],
        compiler_params=pltpu.CompilerParams(collective_id=0, has_side_effects=True),
    )(ridge_reg.reshape(1, -1), query_rows, key_rows, value_rows, out_weight, out_grad, doc_ids.reshape(1, -1))
    return pl.pallas_call(
        move,
        out_shape=[jax.ShapeDtypeStruct(a.shape, a.dtype) for a in made],
        in_specs=[pl.BlockSpec(memory_space=pltpu.VMEM)] * 5,
        out_specs=[any_space] * 5,
        scratch_shapes=[pltpu.SemaphoreType.DMA((5,))],
    )(*[pltpu.with_memory_space_constraint(a, pltpu.VMEM) for a in made])


def build(mesh, dims):
    nx = mesh.shape["head"]
    spec = P("seq", "head")
    return jax.shard_map(
        functools.partial(per_device, dims, nx),
        mesh=mesh,
        in_specs=(spec, spec, spec, P("head"), P("head", None), spec, P("seq")),
        out_specs=(spec,) * 5,
        check_vma=False,
    )


def solution(mesh):
    return build(mesh, SEQ_DIMS)
```
